32 devices in a mesh: bead: 2 (over x), space: 16 (over z, y, core).
Axes of the slice: x: 2, y: 2, z: 4, core: 2. Of those that a mesh axis runs over, the one named last changes fastest.
Arguments:
- positions: float32 [32, 3, 6144], P('bead', None, 'space'), as said below
- charges: float32 [6144], P('space'), may hold values from -3 to 3
- polar: float32 [6144], P('space'), may hold values from 0.4 to 1.6
- molecule: int32 [6144], P('space'), may hold values from 0 to 2047, as said below
Outputs:
- total_field: float32 [32, 3, 6144], P('bead', None, 'space')
- dipoles: float32 [4, 3, 6144], P(None, None, 'space')
The draws below stay inside these ranges and needn't reach their ends.
Inputs may be any that keep to these rules, and one draw needn't show every extreme that they name: Each molecule has three atoms, all in one slab block of 384 atoms; no id appears in two blocks. `positions`: in slab block d every atom's first coordinate lies between 15.2 d and 15.2 (d + 1).
All inputs are finite; a program needn't handle non-finite values.
Results may differ from the reference program's by a relative error of at most 0.0003.
Values sent between devices are 32-bit elements; how exact they have to be, the bound alone decides.
No kernel may reach another device: no remote copies, remote signals or barrier semaphores. Data moves between devices by JAX's collectives and lax.ppermute only.
A program may use at most 64 MiB of HBM per device.

```python
import math
import jax
import jax.numpy as jnp
from jax import lax

BEADS = 32
CONTR = 4
ITERS = 2
ROWS_Y = 4
ATOMS_DEV = 384
ATOMS = 6144


def atom_roles(key):
    domains = ATOMS // ATOMS_DEV
    keys = jax.random.split(jax.random.fold_in(key, 11), domains)
    return jax.vmap(lambda k: jax.random.permutation(k, ATOMS_DEV))(keys).astype(jnp.int32)


def draw_molecule(key, part):
    roles = atom_roles(key)
    domains = roles.shape[0]
    base = jnp.arange(domains, dtype=jnp.int32)[:, None] * (ATOMS_DEV // 3)
    return (base + roles // 3).reshape(-1)


def draw_positions(key, part):
    roles = atom_roles(key)
    domains = roles.shape[0]
    mols = ATOMS_DEV // 3
    spacing = 3.8
    mol = roles // 3
    kind = roles % 3
    first, second, third = jax.random.split(jax.random.fold_in(key, 23), 3)
    jitter = jax.random.uniform(first, (domains, mols, 3), jnp.float32, -0.3, 0.3)
    arms = jax.random.normal(second, (domains, mols * 2, 3), jnp.float32)
    arms = arms / jnp.sqrt(jnp.sum(arms * arms, axis=-1, keepdims=True) + 1e-12)
    xrow = (mol % 4).astype(jnp.float32)
    yrow = (mol // 4 % ROWS_Y).astype(jnp.float32)
    zrow = (mol // (4 * ROWS_Y)).astype(jnp.float32)
    slab = jnp.arange(domains, dtype=jnp.float32)[:, None] * 4.0 * spacing
    centre = jnp.stack([slab + (xrow + 0.5) * spacing, (yrow + 0.5) * spacing, (zrow + 0.5) * spacing], -1)
    centre = centre + jnp.take_along_axis(jitter, jnp.broadcast_to(mol[:, :, None], (domains, ATOMS_DEV, 3)), axis=1)
    which = mol * 2 + jnp.maximum(kind - 1, 0)
    chosen = jnp.take_along_axis(arms, jnp.broadcast_to(which[:, :, None], (domains, ATOMS_DEV, 3)), axis=1)
    atom = centre + jnp.where((kind > 0)[:, :, None], 0.96 * chosen, 0.0)
    atom = atom.reshape(domains * ATOMS_DEV, 3).T
    offsets = jnp.clip(0.1 * jax.random.normal(third, (BEADS, 3, ATOMS), jnp.float32), -0.3, 0.3)
    return atom[None] + offsets


def steps_of(own_key, dims, pieces, low, largest):
    def one(position, shards_of):
        draws = jax.random.uniform(jax.random.fold_in(jax.random.fold_in(own_key, 6), position), (shards_of,), jnp.float32, low / len(pieces), largest / len(pieces))
        return jnp.repeat(jnp.exp(draws), dims[position] // shards_of).reshape((-1,) + (1,) * (len(dims) - position - 1))

    level = one(*pieces[0])
    for cut in pieces[1:]:
        level = level * one(*cut)
    return level


def gaussian(key, shape, deviation, limit, cuts=(), kind=jnp.bfloat16):
    values = jax.random.normal(key, shape, jnp.float32) * deviation
    if len(cuts) > 0:
        values = steps_of(key, shape, cuts, -0.22, 0.18) * values
    return jnp.clip(values, min=-limit, max=limit).astype(kind)


def setup_inputs(seed: int = 0) -> dict:
    arg_keys = jax.random.split(jax.random.key(seed), 5)
    return {
        "positions": draw_positions(jax.random.fold_in(arg_keys[4], 71), 0),
        "charges": gaussian(arg_keys[1], (ATOMS,), 0.5, 3.0, ((0, 16),), jnp.float32),
        "polar": jnp.clip(jnp.exp(math.log(1.6) - 1.3862944 * jax.random.uniform(arg_keys[2], (ATOMS,), jnp.float32) ** steps_of(arg_keys[2], (ATOMS,), ((0, 16),), -0.2, 0.2)), 0.4, 1.6),
        "molecule": draw_molecule(jax.random.fold_in(arg_keys[4], 71), 0),
    }


THOLE = 0.39
CUTOFF = 9.0

def pair_field(target, target_alpha, target_mol, source, source_charge, source_alpha, source_dip, source_mol, dipolar):
    width = source.shape[1] // 18
    count = source.shape[1] // width
    blocks = (source.reshape(3, count, width).transpose(1, 0, 2), source_charge.reshape(count, width), source_alpha.reshape(count, width), source_dip.reshape(3, count, width).transpose(1, 0, 2), source_mol.reshape(count, width))

    def step(total, block):
        spot, charge, alpha, dip, mol = block
        diff = target[:, :, None] - spot[:, None, :]
        dist2 = lax.optimization_barrier(jnp.sum(diff * diff, axis=0))
        keep = (alpha[None, :] > 0.0) & (target_mol[:, None] != mol[None, :]) & (dist2 < CUTOFF * CUTOFF)
        safe2 = jnp.where(keep, dist2, 1.0)
        inverse = lax.rsqrt(safe2)
        inv3 = inverse * inverse * inverse
        both = jnp.where(keep, target_alpha[:, None] * alpha[None, :], 1.0)
        cube = 0.39 * safe2 * jnp.sqrt(safe2) * lax.rsqrt(both)
        decay = jnp.exp(-cube)
        damp3 = 1.0 - decay
        damp5 = 1.0 - (1.0 + cube) * decay
        ratio = 1.0 - dist2 / (CUTOFF * CUTOFF)
        taper = jnp.where(keep, ratio * ratio, 0.0)
        if dipolar:
            along = lax.optimization_barrier(jnp.sum(diff * dip[:, None, :], axis=0))
            term = (3.0 * taper * damp5 * inv3 * inverse * inverse * along)[None] * diff - (taper * damp3 * inv3)[None] * dip[:, None, :]
        else:
            term = (taper * damp3 * inv3 * charge[None, :])[None] * diff
        return (total + lax.optimization_barrier(jnp.sum(term, axis=2)), None)
    start = jnp.zeros((3, target.shape[1]), jnp.float32)
    total, unused = lax.scan(step, start, blocks)
    return total

def reference(positions, charges, polar, molecule):
    atoms_dom = ATOMS_DEV
    domains = ATOMS // atoms_dom

    def widen(values, fill):
        edge = jnp.full(values.shape[:-1] + (atoms_dom,), fill, values.dtype)
        return jnp.concatenate([edge, values, edge], -1)
    wide_charge = widen(charges, 0.0)
    wide_alpha = widen(polar, 0.0)
    wide_mol = widen(molecule, -1)

    def field_all(spots, dips, dipolar):
        wide_spots = widen(spots, 0.0)
        wide_dips = widen(dips, 0.0)

        def one(index):
            start = (index * atoms_dom).astype(jnp.int32)
            target = lax.dynamic_slice_in_dim(spots, start, atoms_dom, 1)
            talpha = lax.dynamic_slice_in_dim(polar, start, atoms_dom, 0)
            tmol = lax.dynamic_slice_in_dim(molecule, start, atoms_dom, 0)
            return pair_field(target, talpha, tmol, lax.dynamic_slice_in_dim(wide_spots, start, 3 * atoms_dom, 1), lax.dynamic_slice_in_dim(wide_charge, start, 3 * atoms_dom, 0), lax.dynamic_slice_in_dim(wide_alpha, start, 3 * atoms_dom, 0), lax.dynamic_slice_in_dim(wide_dips, start, 3 * atoms_dom, 1), lax.dynamic_slice_in_dim(wide_mol, start, 3 * atoms_dom, 0), dipolar)
        result = lax.map(one, jnp.arange(domains, dtype=jnp.int32))
        return result.transpose(1, 0, 2).reshape(3, domains * atoms_dom)
    nothing = jnp.zeros((3, ATOMS), jnp.float32)
    perm = lax.map(lambda spots: field_all(spots, nothing, False), positions)
    kidx = jnp.arange(CONTR, dtype=jnp.float32)[:, None] / CONTR
    bidx = jnp.arange(BEADS, dtype=jnp.float32)[None, :] / BEADS
    theta = 2.0 * jnp.pi * (kidx - bidx)
    series = 1.0 + 2.0 * jnp.cos(theta) + jnp.cos(2.0 * theta)
    contract = series / BEADS
    spread = series.T / CONTR
    high = lax.Precision.HIGHEST
    cpos = jnp.einsum('kb,bxa->kxa', contract, positions, precision=high)
    cfield = jnp.einsum('kb,bxa->kxa', contract, perm, precision=high)

    def induce(mu):
        return lax.map(lambda pair: field_all(pair[0], pair[1], True), (cpos, mu))
    mu = polar[None, None, :] * cfield
    for step in range(ITERS):
        mu = polar[None, None, :] * (cfield + induce(mu))
    induced = induce(mu)
    total = perm + jnp.einsum('bk,kxa->bxa', spread, induced, precision=high)
    return (total, mu)
```

```python
import functools
import math

import jax
import jax.numpy as jnp
import numpy as np
from jax import lax
from jax.experimental import pallas as pl
from jax.experimental.pallas import tpu as pltpu
from jax.sharding import PartitionSpec as P

BEADS = 32
CONTR = 4
ITERS = 2
CUTOFF = 9.0
CUT2 = CUTOFF * CUTOFF
THOLE = 0.39
LOG2E = 1.4426950408889634
LN2 = 0.6931471805599453
L = 128
KP = 8
F32 = jnp.float32
BF16 = jnp.bfloat16
VMEM_LIMIT = 40 * 1024 * 1024


def split3(x):
    h = x.astype(BF16).astype(F32)
    r = x - h
    m = r.astype(BF16).astype(F32)
    return h, m, r - m


def dot(a, b, ca=1, cb=0):
    return lax.dot_general(a, b, (((ca,), (cb,)), ((), ())), preferred_element_type=F32)


def dot3(x, mat, cb):
    rows = x.shape[0]
    out = dot(jnp.concatenate(split3(x), 0).astype(BF16), mat, 1, cb)
    return (out[:rows] + out[rows : 2 * rows]) + out[2 * rows :]


T_SLOTS, S_SLOTS = [], []
for _a in range(3):
    T_SLOTS += [(_a, 1)] * 3 + [(3 + _a, 1)] * 2 + [(6 + _a, 1)]
    S_SLOTS += [(_a, -2), (3 + _a, -2), (6 + _a, -2), (_a, -2), (3 + _a, -2), (_a, -2)]
T_SLOTS += [(9, 1), (10, 1), (11, 1), (12, 1), (12, 1), (12, 1)]
S_SLOTS += [(12, 1), (12, 1), (12, 1), (9, 1), (10, 1), (11, 1)]
TYPES = 13


def sel_pair(rows, count):
    groups = (count + 3) // 4
    sel_t = np.zeros((count * L, TYPES * rows), np.float32)
    sel_s = np.zeros((TYPES * rows, groups * L), np.float32)
    for b in range(count):
        for f in range(len(T_SLOTS)):
            kind, coef = T_SLOTS[f]
            sel_t[b * L + (b % 4) * 32 + f, kind * rows + b] = coef
            kind, coef = S_SLOTS[f]
            sel_s[kind * rows + b, (b // 4) * L + (b % 4) * 32 + f] = coef
    return jnp.asarray(sel_t, BF16), jnp.asarray(sel_s, BF16)


def sel_sum(rows, count):
    sel = np.zeros((count * 32, 12 * rows), np.float32)
    for b in range(count):
        for p in range(3):
            for f in range(4):
                sel[b * 32 + p * 8 + f, (p * 4 + f) * rows + b] = 1
    return jnp.asarray(sel, BF16)


def sel_induce():
    sel = np.zeros((CONTR * L, 48 * KP), np.float32)
    for k in range(CONTR):
        for p in range(3):
            for f in range(16):
                sel[k * L + p * 16 + f, (p * 16 + f) * KP + k] = 1
            for f in range(3):
                sel[k * L + 64 + p * 8 + f, (p * 16 + f) * KP + k] = 1
    return jnp.asarray(sel, BF16)


def perm_matrix(rank_row, w):
    rows = lax.broadcasted_iota(jnp.int32, (w, w), 0).astype(F32)
    return jnp.where(rows == rank_row, 1.0, 0.0).astype(BF16)


def pair_pieces(xs):
    hx, hy, hz = (split3(x) for x in xs)
    n = xs[0] * xs[0] + xs[1] * xs[1] + xs[2] * xs[2]
    parts = [hx[0], hy[0], hz[0], hx[1], hy[1], hz[1], hx[2], hy[2], hz[2]]
    parts += list(split3(n)) + [jnp.ones_like(n)]
    return jnp.concatenate(parts, 0).astype(BF16)


def center_of(xs, count):
    w = xs[0].shape[1]
    return [jnp.sum(x[:count], keepdims=True) * (1.0 / (count * w)) for x in xs]


def columns(misc):
    al = misc[1:2]
    good = al > 0.0
    inv = jnp.where(good, lax.rsqrt(jnp.where(good, al, 1.0)), 0.0)
    return jnp.concatenate([inv, misc[2:3], jnp.zeros_like(misc[:6])], 0)


def ranges(x, al, count, w):
    good = al > 0.0
    lo = jnp.where(good, x[:count], 1e30)
    hi = jnp.where(good, x[:count], -1e30)
    out = []
    for i in range(w // L):
        out.append((jnp.min(lo[:, i * L : (i + 1) * L]), jnp.max(hi[:, i * L : (i + 1) * L])))
    return out


def set_flags(flags, trange, sranges, nt):
    sj = 0
    for slab in sranges:
        for smin, smax in slab:
            for ti, (tmin, tmax) in enumerate(trange):
                near = (smin - tmax < CUTOFF) & (tmin - smax < CUTOFF)
                flags[sj * nt + ti] = near.astype(jnp.int32)
            sj += 1


def pair_basis(r2, q):
    safe = jnp.maximum(r2, 1e-4)
    inv = lax.rsqrt(safe)
    c = (safe * inv) * (safe * q)
    decay = jnp.exp2(c)
    v = jnp.maximum(CUT2 - r2, 0.0) * inv
    return c, decay, inv, v


def two(x):
    hi = x.astype(BF16)
    return hi, (x - hi.astype(F32)).astype(BF16)


def pack_kernel(nb, nbp, w, pos, charge, polar, mol, out, rank_out, scr):
    scr[...] = jnp.zeros_like(scr)
    for a in range(3):
        scr[a * nbp : a * nbp + nb, :] = pos[:, a, :]
    base = 3 * nbp
    scr[base : base + 1, :] = charge[...]
    scr[base + 1 : base + 2, :] = polar[...]
    scr[base + 2 : base + 3, :] = mol[...].astype(F32)
    x = scr[...]
    key = jnp.sum(x[:nbp], 0, keepdims=True)
    col = jnp.transpose(jnp.broadcast_to(key, (8, w)))[:, :1]
    jj = lax.broadcasted_iota(jnp.int32, (w, w), 0)
    ii = lax.broadcasted_iota(jnp.int32, (w, w), 1)
    before = (col < key) | ((col == key) & (jj < ii))
    rank = jnp.sum(jnp.where(before, 1.0, 0.0), 0, keepdims=True)
    rank_out[...] = jnp.broadcast_to(rank, (8, w))
    out[...] = dot3(x, perm_matrix(rank, w), 1)


def perm_kernel(nsrc, own, nb, nbp, w, *refs):
    tgt = refs[0]
    srcs = refs[1 : 1 + nsrc]
    refs = refs[1 + nsrc :]
    if own:
        sel_t, sel_s, sel_r, acc_out = refs[:4]
        refs = refs[4:]
    else:
        sel_t, sel_s, sel_r, acc_in, rank, contract, perm_out, msg_out = refs[:8]
        refs = refs[8:]
    ft, fs, rt, cols, acc, flags = refs
    nt = w // L
    base = 3 * nbp
    coords = [tgt[a * nbp : (a + 1) * nbp, :] for a in range(3)]
    center = center_of(coords, nb)
    xt = [x - c for x, c in zip(coords, center)]
    ft[...] = dot(sel_t[...], pair_pieces(xt)).astype(BF16)
    misc_t = columns(tgt[base : base + 8, :])
    trange = ranges(xt[0], tgt[base + 1 : base + 2, :], nb, w)
    sranges = []
    for s, src in enumerate(srcs):
        xs = [src[a * nbp : (a + 1) * nbp, :] - center[a] for a in range(3)]
        misc = src[base : base + 8, :]
        fs[s * w : (s + 1) * w, :] = dot(pair_pieces(xs), sel_s[...], 0, 0).astype(BF16)
        q = jnp.broadcast_to(misc[0:1] * (1.0 / (CUT2 * CUT2)), xs[0].shape)
        feats = [split3(v) for v in (xs[0] * q, xs[1] * q, xs[2] * q, q)]
        stack = jnp.concatenate([feats[f][p] for p in range(3) for f in range(4)], 0)
        rt[:, s * w : (s + 1) * w] = dot(sel_r[...], stack.astype(BF16)).astype(BF16)
        cols[s * w : (s + 1) * w, :] = jnp.transpose(columns(misc))
        sranges.append(ranges(xs[0], misc[1:2], nb, w))
    set_flags(flags, trange, sranges, nt)
    if own:
        acc[...] = jnp.zeros_like(acc)
    else:
        acc[...] = acc_in[...]
    qt_rows = misc_t * (-THOLE * LOG2E)
    mol_rows = misc_t[1:2]

    for ti in range(nt):
        t0 = ti * L
        qrow = qt_rows[0:1, t0 : t0 + L]
        mrow = mol_rows[:, t0 : t0 + L]

        def step(sj, carry):
            @pl.when(flags[sj * nt + ti] == 1)
            def _():
                s0 = pl.multiple_of(sj * L, L)
                cc = cols[pl.ds(s0, L), :]
                q = cc[:, 0:1] * qrow
                if own:
                    q = jnp.where(cc[:, 1:2] == mrow, 0.0, q)

                def group(g, c2):
                    g0 = pl.multiple_of(g * L, L)
                    lhs = fs[pl.ds(s0, L), pl.ds(g0, L)]
                    for i in range(4):
                        b = g * 4 + i
                        rhs = ft[pl.ds(pl.multiple_of(b * L, L), L), t0 : t0 + L]
                        c, decay, inv, v = pair_basis(dot(lhs, rhs), q)
                        f = (v * v) * (inv * (1.0 - decay))
                        pair = jnp.concatenate(two(f), 0)
                        r0 = pl.multiple_of(b * 32, 32)
                        r = rt[pl.ds(r0, 32), pl.ds(s0, L)]
                        acc[pl.ds(r0, 32), t0 : t0 + L] += dot(jnp.concatenate([r, r], 1), pair)
                    return c2

                lax.fori_loop(0, nb // 4, group, 0)

            return carry

        lax.fori_loop(0, nsrc * nt, step, 0)
    if own:
        acc_out[...] = acc[...]
        return
    for a in range(3):
        perm_out[a * nbp : (a + 1) * nbp, :] = jnp.zeros((nbp, w), F32)
    for b in range(nb):
        s = acc[b * 32 : b * 32 + 8, :] + acc[b * 32 + 8 : b * 32 + 16, :]
        s = s + acc[b * 32 + 16 : b * 32 + 24, :]
        for a in range(3):
            row = xt[a][b : b + 1] * s[3:4] - s[a : a + 1]
            perm_out[a * nbp + b : a * nbp + b + 1, :] = row
    wc = contract[lax.axis_index("bead")]
    parts = []
    for a in range(3):
        parts.append(
            jnp.dot(wc, perm_out[a * nbp : (a + 1) * nbp, :], precision=lax.Precision.HIGHEST, preferred_element_type=F32)
        )
    for a in range(3):
        parts.append(jnp.dot(wc, coords[a], precision=lax.Precision.HIGHEST, preferred_element_type=F32))
    msg_out[...] = dot3(jnp.concatenate(parts, 0), perm_matrix(rank[0:1, :], w), 0)


def start_kernel(nbp, w, msg, other, rank, pack, m0, cf):
    both = dot3(msg[...] + other[...], perm_matrix(rank[0:1, :], w), 1)
    n = 3 * KP
    cf[...] = both[:n]
    m0[:n, :] = both[:n] * pack[3 * nbp + 1 : 3 * nbp + 2, :]
    m0[n:, :] = both[n:]


def tensor_blocks(w, own, tgt_m, tgt_misc, srcs, sel_t, sel_s, tensors, flags, ft, fs, cols):
    nt = w // L
    n = 3 * KP
    coords = [tgt_m[n + a * KP : n + (a + 1) * KP, :] for a in range(3)]
    center = center_of(coords, CONTR)
    xt = [x - c for x, c in zip(coords, center)]
    ft[...] = dot(sel_t[...], pair_pieces(xt)).astype(BF16)
    misc_t = columns(tgt_misc)
    trange = ranges(xt[0], tgt_misc[1:2], CONTR, w)
    sranges = []
    for s, (sm, misc) in enumerate(srcs):
        xs = [sm[n + a * KP : n + (a + 1) * KP, :] - center[a] for a in range(3)]
        fs[s * w : (s + 1) * w, :] = dot(pair_pieces(xs), sel_s[...], 0, 0).astype(BF16)
        cols[s * w : (s + 1) * w, :] = jnp.transpose(columns(misc))
        sranges.append(ranges(xs[0], misc[1:2], CONTR, w))
    set_flags(flags, trange, sranges, nt)
    qt_rows = misc_t * (-THOLE * LOG2E)
    for ti in range(nt):
        t0 = ti * L
        qrow = qt_rows[0:1, t0 : t0 + L]
        mrow = misc_t[1:2, t0 : t0 + L]

        def step(sj, carry):
            blk = sj * nt + ti

            @pl.when(flags[blk] == 1)
            def _():
                s0 = pl.multiple_of(sj * L, L)
                cc = cols[pl.ds(s0, L), :]
                q = cc[:, 0:1] * qrow
                if own:
                    q = jnp.where(cc[:, 1:2] == mrow, 0.0, q)
                lhs = fs[pl.ds(s0, L), :]
                for k in range(CONTR):
                    c, decay, inv, v = pair_basis(dot(lhs, ft[k * L : (k + 1) * L, t0 : t0 + L]), q)
                    l3 = 1.0 - decay
                    l5 = l3 + (c * LN2) * decay
                    w3 = (v * v) * inv
                    w5 = w3 * (inv * inv)
                    a_hi, a_lo = two(w5 * l5)
                    b_hi, b_lo = two(w3 * l3)
                    tensors[k, blk, 0:L, :] = a_hi
                    tensors[k, blk, L : 2 * L, :] = a_lo
                    tensors[k, blk, 2 * L : 3 * L, :] = b_hi
                    tensors[k, blk, 3 * L : 4 * L, :] = b_lo

            return carry

        lax.fori_loop(0, len(srcs) * nt, step, 0)


def own_tensor_kernel(nbp, w, m0, pack, sel_t, sel_s, tensors, flags_out, ft, fs, cols):
    misc = pack[3 * nbp : 3 * nbp + 8, :]
    tensor_blocks(w, True, m0, misc, [(m0, misc)], sel_t, sel_s, tensors, flags_out, ft, fs, cols)


def induce_sums(w, mus, cps, sel_e, groups, le, acc_a, acc_b, ev):
    nt = w // L
    n = 3 * KP
    own = [cps[0][n + a * KP : n + (a + 1) * KP, :] for a in range(3)]
    center = center_of(own, CONTR)
    scale = 1.0 / (CUT2 * CUT2)
    for s, (mu, cp) in enumerate(zip(mus, cps)):
        m = [mu[a * KP : (a + 1) * KP, :] * scale for a in range(3)]
        x = [cp[n + a * KP : n + (a + 1) * KP, :] - center[a] for a in range(3)]
        dotted = x[0] * m[0] + x[1] * m[1] + x[2] * m[2]
        feats = m + [dotted] + [x[a] * m[b] for a in range(3) for b in range(3)]
        feats += [x[a] * dotted for a in range(3)]
        split = [split3(f) for f in feats]
        stack = jnp.concatenate([split[f][p] for p in range(3) for f in range(16)], 0)
        le[:, s * w : (s + 1) * w] = dot(sel_e[...], stack.astype(BF16)).astype(BF16)
    acc_a[...] = jnp.zeros_like(acc_a)
    acc_b[...] = jnp.zeros_like(acc_b)
    for first, nsrc, tensors, flags in groups:
        for ti in range(nt):
            t0 = ti * L

            def step(sj, carry):
                blk = sj * nt + ti

                @pl.when(flags[blk] == 1)
                def _():
                    s0 = pl.multiple_of((first * nt + sj) * L, L)
                    for k in range(CONTR):
                        fa = le[k * L : k * L + 48, pl.ds(s0, L)]
                        fb = le[k * L + 64 : k * L + 96, pl.ds(s0, L)]
                        acc_a[k * 48 : (k + 1) * 48, t0 : t0 + L] += dot(
                            jnp.concatenate([fa, fa], 1), tensors[k, blk, 0 : 2 * L, :]
                        )
                        acc_b[k * 32 : (k + 1) * 32, t0 : t0 + L] += dot(
                            jnp.concatenate([fb, fb], 1), tensors[k, blk, 2 * L : 4 * L, :]
                        )

                return carry

            lax.fori_loop(0, nsrc * nt, step, 0)
    ev[...] = jnp.zeros_like(ev)
    for k in range(CONTR):
        o = k * 48
        sa = acc_a[o : o + 16, :] + acc_a[o + 16 : o + 32, :] + acc_a[o + 32 : o + 48, :]
        o = k * 32
        sb = acc_b[o : o + 8, :] + acc_b[o + 8 : o + 16, :] + acc_b[o + 16 : o + 24, :]
        x = [own[a][k : k + 1] - center[a] for a in range(3)]
        mm = [sa[a : a + 1] for a in range(3)]
        along = x[0] * mm[0] + x[1] * mm[1] + x[2] * mm[2] - sa[3:4]
        for a in range(3):
            cross = sum(x[b] * sa[4 + 3 * a + b : 5 + 3 * a + b] for b in range(3))
            full = x[a] * along - cross + sa[13 + a : 14 + a]
            ev[a * KP + k : a * KP + k + 1, :] = 3.0 * full - sb[a : a + 1]


def update(pack, nbp, cf, ev):
    al = pack[3 * nbp + 1 : 3 * nbp + 2, :]
    return al * (cf[...] + ev[...])


def first_induce_kernel(
    nbp, w, m0, m0a, m0b, pack, packa, packb, cf, t_own, f_own, sel_t, sel_s, sel_e,
    mu_out, t_nbr, f_nbr, ft, fs, cols, le, acc_a, acc_b, ev,
):
    base = 3 * nbp
    tensor_blocks(
        w, False, m0, pack[base : base + 8, :],
        [(m0a, packa[base : base + 8, :]), (m0b, packb[base : base + 8, :])],
        sel_t, sel_s, t_nbr, f_nbr, ft, fs, cols,
    )
    m = [m0, m0a, m0b]
    induce_sums(w, m, m, sel_e, [(0, 1, t_own, f_own), (1, 2, t_nbr, f_nbr)], le, acc_a, acc_b, ev)
    mu_out[...] = update(pack, nbp, cf, ev)


def induce_kernel(
    nbp, w, mu, mua, mub, m0, m0a, m0b, pack, cf, t_own, f_own, t_nbr, f_nbr, sel_e,
    mu_out, le, acc_a, acc_b, ev,
):
    induce_sums(
        w, [mu, mua, mub], [m0, m0a, m0b], sel_e,
        [(0, 1, t_own, f_own), (1, 2, t_nbr, f_nbr)], le, acc_a, acc_b, ev,
    )
    mu_out[...] = update(pack, nbp, cf, ev)


def final_kernel(
    nb, nbp, w, mu, mua, mub, m0, m0a, m0b, perm, rank, t_own, f_own, t_nbr, f_nbr, sel_e, spread,
    total_out, dip_out, le, acc_a, acc_b, ev,
):
    induce_sums(
        w, [mu, mua, mub], [m0, m0a, m0b], sel_e,
        [(0, 1, t_own, f_own), (1, 2, t_nbr, f_nbr)], le, acc_a, acc_b, ev,
    )
    us = spread[lax.axis_index("bead")]
    parts = []
    for a in range(3):
        part = jnp.dot(us, ev[a * KP : (a + 1) * KP, :], precision=lax.Precision.HIGHEST, preferred_element_type=F32)
        parts.append(perm[a * nbp : (a + 1) * nbp, :] + part)
    parts.append(mu[...])
    out = dot3(jnp.concatenate(parts, 0), perm_matrix(rank[0:1, :], w), 0)
    for a in range(3):
        total_out[:, a, :] = out[a * nbp : a * nbp + nb]
        d0 = 3 * nbp + a * KP
        dip_out[:, a, :] = out[d0 : d0 + CONTR]


def swap_pairs(count, first):
    pairs = []
    for i in range(first, count - 1, 2):
        pairs += [(i, i + 1), (i + 1, i)]
    return pairs


def call(kernel, outs, name, scratch=(), smem_in=(), smem_out=(), nin=0):
    smem = pl.BlockSpec(memory_space=pltpu.SMEM)
    vmem = pl.BlockSpec(memory_space=pltpu.VMEM)
    return pl.pallas_call(
        kernel,
        out_shape=[jax.ShapeDtypeStruct(s, d) for s, d in outs],
        in_specs=[smem if i in smem_in else vmem for i in range(nin)],
        out_specs=[smem if i in smem_out else vmem for i in range(len(outs))],
        scratch_shapes=list(scratch),
        compiler_params=pltpu.CompilerParams(vmem_limit_bytes=VMEM_LIMIT),
        name=name,
    )


def body(positions, charges, polar, molecule):
    nb, _, w = positions.shape
    nbp = -(-nb // 16) * 16
    nt = w // L
    nbead = lax.axis_size("bead")
    nspace = lax.axis_size("space")
    rows = 3 * nbp + 8
    n = 3 * KP

    contract = np.zeros((nbead, KP, nbp), np.float32)
    spread = np.zeros((nbead, nbp, KP), np.float32)
    for r in range(nbead):
        for b in range(nb):
            for k in range(CONTR):
                theta = 2.0 * math.pi * (k / CONTR - (r * nb + b) / BEADS)
                series = 1.0 + 2.0 * math.cos(theta) + math.cos(2.0 * theta)
                contract[r, k, b] = series / BEADS
                spread[r, b, k] = series / CONTR
    contract = jnp.asarray(contract)
    spread = jnp.asarray(spread)
    sel_t, sel_s = sel_pair(nbp, nb)
    sel_r = sel_sum(nbp, nb)
    ksel_t, ksel_s = sel_pair(KP, CONTR)
    sel_e = sel_induce()

    def exchange(x):
        near = lax.ppermute(x, "space", swap_pairs(nspace, 0))
        far = lax.ppermute(x, "space", swap_pairs(nspace, 1))
        return near, far

    pack, rank = call(
        functools.partial(pack_kernel, nb, nbp, w), [((rows, w), F32), ((8, w), F32)], "pack",
        [pltpu.VMEM((rows, w), F32)], nin=4,
    )(positions, charges[None], polar[None], molecule[None])
    packa, packb = exchange(pack)

    groups = -(-nb // 4)

    def perm_scratch(nsrc):
        return [
            pltpu.VMEM((nb * L, w), BF16),
            pltpu.VMEM((nsrc * w, groups * L), BF16),
            pltpu.VMEM((nb * 32, nsrc * w), BF16),
            pltpu.VMEM((nsrc * w, 8), F32),
            pltpu.VMEM((nb * 32, w), F32),
            pltpu.SMEM((nsrc * nt * nt,), jnp.int32),
        ]

    (acc,) = call(
        functools.partial(perm_kernel, 1, True, nb, nbp, w), [((nb * 32, w), F32)], "perm_own",
        perm_scratch(1), nin=5,
    )(pack, pack, sel_t, sel_s, sel_r)
    perm, msg = call(
        functools.partial(perm_kernel, 2, False, nb, nbp, w), [((3 * nbp, w), F32), ((2 * n, w), F32)],
        "perm_near", perm_scratch(2), nin=9,
    )(pack, packa, packb, sel_t, sel_s, sel_r, acc, rank, contract)

    if nbead == 2:
        other = lax.ppermute(msg, "bead", [(0, 1), (1, 0)])
    else:
        other = lax.psum(msg, "bead") - msg
    m0, cf = call(
        functools.partial(start_kernel, nbp, w), [((2 * n, w), F32), ((n, w), F32)], "start", nin=4,
    )(msg, other, rank, pack)
    m0a, m0b = exchange(m0)

    def tensor_scratch(nsrc):
        return [
            pltpu.VMEM((CONTR * L, w), BF16),
            pltpu.VMEM((nsrc * w, L), BF16),
            pltpu.VMEM((nsrc * w, 8), F32),
        ]

    def tensor_shape(nsrc):
        return ((CONTR, nsrc * nt * nt, 4 * L, L), BF16)

    sum_scratch = [
        pltpu.VMEM((CONTR * L, 3 * w), BF16),
        pltpu.VMEM((CONTR * 48, w), F32),
        pltpu.VMEM((CONTR * 32, w), F32),
        pltpu.VMEM((n, w), F32),
    ]
    t_own, f_own = call(
        functools.partial(own_tensor_kernel, nbp, w), [tensor_shape(1), ((nt * nt,), jnp.int32)], "tensor_own",
        tensor_scratch(1), smem_out=(1,), nin=4,
    )(m0, pack, ksel_t, ksel_s)
    mu, t_nbr, f_nbr = call(
        functools.partial(first_induce_kernel, nbp, w),
        [((n, w), F32), tensor_shape(2), ((2 * nt * nt,), jnp.int32)], "induce_first",
        tensor_scratch(2) + sum_scratch, smem_in=(8,), smem_out=(2,), nin=12,
    )(m0, m0a, m0b, pack, packa, packb, cf, t_own, f_own, ksel_t, ksel_s, sel_e)
    for step in range(ITERS - 1):
        mua, mub = exchange(mu)
        (mu,) = call(
            functools.partial(induce_kernel, nbp, w), [((n, w), F32)], f"induce_{step + 1}",
            sum_scratch, smem_in=(9, 11), nin=13,
        )(mu, mua, mub, m0, m0a, m0b, pack, cf, t_own, f_own, t_nbr, f_nbr, sel_e)
    mua, mub = exchange(mu)
    total, dipoles = call(
        functools.partial(final_kernel, nb, nbp, w), [((nb, 3, w), F32), ((CONTR, 3, w), F32)], "final",
        sum_scratch, smem_in=(9, 11), nin=14,
    )(mu, mua, mub, m0, m0a, m0b, perm, rank, t_own, f_own, t_nbr, f_nbr, sel_e, spread)
    return (total, dipoles)


def solution(mesh):
    in_specs = (P("bead", None, "space"), P("space"), P("space"), P("space"))
    out_specs = (P("bead", None, "space"), P(None, None, "space"))
    return jax.shard_map(body, mesh=mesh, in_specs=in_specs, out_specs=out_specs, check_vma=False)
```

```python
import functools
import math

import jax
import jax.numpy as jnp
from jax import lax
from jax.experimental import pallas as pl
from jax.experimental.pallas import tpu as pltpu
from jax.sharding import PartitionSpec as P

BEADS = 32
CONTR = 4
ITERS = 2
CUTOFF = 9.0
CUT2 = CUTOFF * CUTOFF
THOLE = 0.39
LOG2E = 1.4426950408889634
LN2 = 0.6931471805599453
L = 128
KP = 8
F32 = jnp.float32
BF16 = jnp.bfloat16
VMEM_LIMIT = 20 * 1024 * 1024


def split3(x):
    h = x.astype(BF16).astype(F32)
    r = x - h
    m = r.astype(BF16).astype(F32)
    return h, m, r - m


def dot(a, b, ca=1, cb=0):
    return lax.dot_general(a, b, (((ca,), (cb,)), ((), ())), preferred_element_type=F32)


def dot3(x, mat, cb):
    rows = x.shape[0]
    out = dot(jnp.concatenate(split3(x), 0).astype(BF16), mat, 1, cb)
    return (out[:rows] + out[rows : 2 * rows]) + out[2 * rows :]


TYPES = 13


def lanes(n):
    return lax.broadcasted_iota(jnp.int32, (1, n), 1)


def select(kind, coef, stride, slot, depth):
    rows = lax.broadcasted_iota(jnp.int32, (depth, kind.shape[1]), 0)
    want = jnp.where(kind < 0, -1, kind * stride + slot)
    return jnp.where(rows == want, coef, 0.0).astype(BF16)


def pair_selects(rows, count):
    lane = lanes(max(count * 32, L))
    b, f = lane // 32, lane % 32
    a, j = f // 6, f % 6
    t_kind = jnp.where(j < 3, a, jnp.where(j < 5, 3 + a, 6 + a))
    s_level = jnp.where(j < 3, j, jnp.where(j == 4, 1, 0))
    s_kind = 3 * s_level + a
    t_kind = jnp.where(f < 18, t_kind, jnp.where(f < 21, f - 9, 12))
    s_kind = jnp.where(f < 18, s_kind, jnp.where(f < 21, 12, f - 12))
    none = (f >= 24) | (b >= count)
    t_kind = jnp.where(none, -1, t_kind)
    s_kind = jnp.where(none, -1, s_kind)
    s_coef = jnp.where(f < 18, -2.0, 1.0)
    depth = TYPES * rows
    return select(t_kind, jnp.ones_like(s_coef), rows, b, depth), select(s_kind, s_coef, rows, b, depth)


def sum_select(rows, count):
    lane = lanes(max(count * 32, L))
    b, r = lane // 32, lane % 32
    p, f = r // 8, r % 8
    kind = jnp.where((f < 4) & (p < 3) & (b < count), p * 4 + f, -1)
    return select(kind, 1.0, rows, b, 12 * rows)


def induce_select():
    lane = lanes(CONTR * L)
    k, r = lane // L, lane % L
    p, f = (r - 64) // 8, (r - 64) % 8
    second = jnp.where((r >= 64) & (r < 88) & (f < 3), p * 16 + f, -1)
    kind = jnp.where(r < 48, r, second)
    return select(kind, 1.0, KP, k, 48 * KP)


def perm_matrix(rank_row, w):
    rows = lax.broadcasted_iota(jnp.int32, (w, w), 0).astype(F32)
    return jnp.where(rows == rank_row, 1.0, 0.0).astype(BF16)


def pair_pieces(xs):
    hx, hy, hz = (split3(x) for x in xs)
    n = xs[0] * xs[0] + xs[1] * xs[1] + xs[2] * xs[2]
    parts = [hx[0], hy[0], hz[0], hx[1], hy[1], hz[1], hx[2], hy[2], hz[2]]
    parts += list(split3(n)) + [jnp.ones_like(n)]
    return jnp.concatenate(parts, 0).astype(BF16)


def center_of(xs, count):
    w = xs[0].shape[1]
    return [jnp.sum(x[:count], keepdims=True) * (1.0 / (count * w)) for x in xs]


def columns(misc):
    al = misc[1:2]
    good = al > 0.0
    inv = jnp.where(good, lax.rsqrt(jnp.where(good, al, 1.0)), 0.0)
    return jnp.concatenate([inv, misc[2:3], jnp.zeros_like(misc[:6])], 0)


def ranges(x, al, count, w):
    good = al > 0.0
    lo = jnp.where(good, x[:count], 1e30)
    hi = jnp.where(good, x[:count], -1e30)
    out = []
    for i in range(w // L):
        out.append((jnp.min(lo[:, i * L : (i + 1) * L]), jnp.max(hi[:, i * L : (i + 1) * L])))
    return out


def near_list(lst, size, trange, sranges):
    lst[1] = 0
    lst[1 + size] = 0
    count = jnp.int32(0)
    sj = 0
    for slab in sranges:
        for smin, smax in slab:
            for ti, (tmin, tmax) in enumerate(trange):
                near = (smin - tmax < CUTOFF) & (tmin - smax < CUTOFF)
                lst[1 + count] = sj * L
                lst[1 + size + count] = ti * L
                count = count + near.astype(jnp.int32)
            sj += 1
    lst[0] = count


def own_blocks(nt):
    return [(i, i) for i in range(nt)], [(i, j) for i in range(nt) for j in range(i + 1, nt)]


def pair_basis(r2, q):
    safe = jnp.maximum(r2, 1e-4)
    inv = lax.rsqrt(safe)
    c = (safe * inv) * (safe * q)
    decay = jnp.exp2(c)
    v = jnp.maximum(CUT2 - r2, 0.0) * inv
    return c, decay, inv, v


def two(x):
    hi = x.astype(BF16)
    return hi, (x - hi.astype(F32)).astype(BF16)


def weights(nb, shape, rank, bead_dim):
    b = lax.broadcasted_iota(jnp.int32, shape, bead_dim)
    k = lax.broadcasted_iota(jnp.int32, shape, 1 - bead_dim)
    turn = k * (BEADS // CONTR) - (rank * nb + b) + 2 * BEADS
    turn = (turn + BEADS // 2) % BEADS - BEADS // 2
    cos = jnp.cos(turn.astype(F32) * (2.0 * math.pi / BEADS))
    return jnp.where((k < CONTR) & (b < nb), 2.0 * cos * (1.0 + cos), 0.0)


def hdot(a, b):
    return jnp.dot(a, b, precision=lax.Precision.HIGHEST, preferred_element_type=F32)


def pack_kernel(nb, nbp, w, pos, charge, polar, mol, out, rank_out, scr):
    scr[...] = jnp.zeros_like(scr)
    for a in range(3):
        scr[a * nbp : a * nbp + nb, :] = pos[a]
    base = 3 * nbp
    scr[base : base + 1, :] = charge[...].reshape(1, w)
    scr[base + 1 : base + 2, :] = polar[...].reshape(1, w)
    scr[base + 2 : base + 3, :] = mol[...].reshape(1, w).astype(F32)
    x = scr[...]
    key = jnp.sum(x[:nbp], 0, keepdims=True)
    col = jnp.transpose(jnp.broadcast_to(key, (8, w)))[:, :1]
    jj = lax.broadcasted_iota(jnp.int32, (w, w), 0)
    ii = lax.broadcasted_iota(jnp.int32, (w, w), 1)
    before = (col < key) | ((col == key) & (jj < ii))
    rank = jnp.sum(jnp.where(before, 1.0, 0.0), 0, keepdims=True)
    rank_out[...] = jnp.broadcast_to(rank, (8, w))
    out[...] = dot3(x, perm_matrix(rank, w), 1)


def perm_sources(nbp, w, src, center, s, sel_s, sel_r, fs, rt, cols):
    base = 3 * nbp
    xs = [src[a * nbp : (a + 1) * nbp, :] - center[a] for a in range(3)]
    misc = src[base : base + 8, :]
    fs[s * w : (s + 1) * w, :] = dot(pair_pieces(xs), sel_s, 0, 0).astype(BF16)
    q = jnp.broadcast_to(misc[0:1] * (1.0 / (CUT2 * CUT2)), xs[0].shape)
    feats = [split3(v) for v in (xs[0] * q, xs[1] * q, xs[2] * q, q)]
    stack = jnp.concatenate([feats[f][p] for p in range(3) for f in range(4)], 0)
    rt[:, s * w : (s + 1) * w] = dot(sel_r, stack.astype(BF16), 0, 0).astype(BF16)
    cols[s * w : (s + 1) * w, :] = jnp.transpose(columns(misc))
    return xs[0], misc[1:2]


def perm_pairs(n, first, lst, size, sym, groups, fs, ft, rt, qbuf, acc, r2buf, fbuf):
    r2buf[...] = jnp.full_like(r2buf, 2.0 * CUT2)
    fbuf[...] = jnp.zeros_like(fbuf)
    total = n * groups

    def where_is(i):
        i = jnp.maximum(jnp.minimum(i, total - 1), 0)
        e = first + i // groups
        s0 = pl.multiple_of(lst[1 + e], L)
        t0 = pl.multiple_of(lst[1 + size + e], L)
        return e, s0, t0, i % groups

    def step(i, carry):
        e, s0, t0, g = where_is(i - 2)
        for j in range(4):
            r0 = pl.multiple_of((g * 4 + j) * 32, 32)
            r = rt[pl.ds(r0, 32), pl.ds(s0, L)]
            pair = fbuf[j]
            acc[pl.ds(r0, 32), pl.ds(t0, L)] += dot(jnp.concatenate([r, r], 1), pair)
            if sym:
                back = dot(rt[pl.ds(r0, 32), pl.ds(t0, L)], pair, 1, 1)
                acc[pl.ds(r0, 32), pl.ds(s0, L)] += back[:, :L] + back[:, L:]
        e, s0, t0, g = where_is(i - 1)
        for j in range(4):
            c, decay, inv, v = pair_basis(r2buf[j], qbuf[e])
            hi, lo = two((v * v) * (inv * (1.0 - decay)))
            fbuf[j, :L, :] = hi
            fbuf[j, L:, :] = lo
        e, s0, t0, g = where_is(i)
        lhs = fs[pl.ds(s0, L), pl.ds(pl.multiple_of(g * L, L), L)]
        for j in range(4):
            b0 = pl.multiple_of((g * 4 + j) * L, L)
            r2buf[j] = dot(lhs, ft[pl.ds(b0, L), pl.ds(t0, L)])
        return carry

    lax.fori_loop(0, total + 2, step, 0)


def block_q(n, first, lst, size, own, cols, qrow, qbuf):
    def one(i, carry):
        e = first + i
        s0 = pl.multiple_of(lst[1 + e], L)
        t0 = pl.multiple_of(lst[1 + size + e], L)
        cc = cols[pl.ds(s0, L), :]
        row = qrow[:, pl.ds(t0, L)]
        q = cc[:, 0:1] * row[0:1]
        if own:
            q = jnp.where(cc[:, 1:2] == row[1:2], 0.0, q)
        qbuf[e] = q
        return carry

    lax.fori_loop(0, n, one, 0)


def q_rows(misc, qrow):
    c = columns(misc)
    qrow[...] = c
    qrow[0:1, :] = c[0:1] * (-THOLE * LOG2E)


def fixed_list(lst, size, blocks):
    lst[0] = len(blocks)
    for e, (s, t) in enumerate(blocks):
        lst[1 + e] = s * L
        lst[1 + size + e] = t * L


def perm_own_kernel(nb, nbp, w, tgt, acc, ft, fs, rt, cols, qrow, qbuf, r2buf, fbuf, lst):
    nt = w // L
    base = 3 * nbp
    sel_t, sel_s = pair_selects(nbp, nb)
    coords = [tgt[a * nbp : (a + 1) * nbp, :] for a in range(3)]
    center = center_of(coords, nb)
    compact = dot(sel_t, pair_pieces([x - c for x, c in zip(coords, center)]), 0, 0).astype(BF16)
    ft[...] = jnp.zeros_like(ft)
    for b in range(nb):
        r0 = b * L + (b % 4) * 32
        ft[r0 : r0 + 32, :] = compact[b * 32 : (b + 1) * 32]
    perm_sources(nbp, w, tgt, center, 0, sel_s, sum_select(nbp, nb), fs, rt, cols)
    q_rows(tgt[base : base + 8, :], qrow)
    acc[...] = jnp.zeros_like(acc)
    diag, off = own_blocks(nt)
    size = len(diag) + len(off)
    fixed_list(lst, size, diag + off)
    block_q(size, 0, lst, size, True, cols, qrow, qbuf)
    groups = nb // 4
    perm_pairs(len(diag), 0, lst, size, False, groups, fs, ft, rt, qbuf, acc, r2buf, fbuf)
    perm_pairs(len(off), len(diag), lst, size, True, groups, fs, ft, rt, qbuf, acc, r2buf, fbuf)


def perm_near_kernel(
    nb, nbp, w, tgt, srca, srcb, ft, acc_in, rank, perm_out, msg_out,
    fs, rt, cols, qrow, qbuf, r2buf, fbuf, acc, lst,
):
    nt = w // L
    base = 3 * nbp
    _, sel_s = pair_selects(nbp, nb)
    sel_r = sum_select(nbp, nb)
    coords = [tgt[a * nbp : (a + 1) * nbp, :] for a in range(3)]
    center = center_of(coords, nb)
    xt = [x - c for x, c in zip(coords, center)]
    sranges = []
    for s, src in enumerate((srca, srcb)):
        x, al = perm_sources(nbp, w, src, center, s, sel_s, sel_r, fs, rt, cols)
        sranges.append(ranges(x, al, nb, w))
    size = 2 * nt * nt
    near_list(lst, size, ranges(xt[0], tgt[base + 1 : base + 2, :], nb, w), sranges)
    q_rows(tgt[base : base + 8, :], qrow)
    n = lst[0]
    block_q(n, 0, lst, size, False, cols, qrow, qbuf)
    acc[...] = acc_in[...]
    perm_pairs(n, 0, lst, size, False, nb // 4, fs, ft, rt, qbuf, acc, r2buf, fbuf)
    if nb < nbp:
        perm_out[...] = jnp.zeros_like(perm_out)
    for b in range(nb):
        s = acc[b * 32 : b * 32 + 8, :] + acc[b * 32 + 8 : b * 32 + 16, :]
        s = s + acc[b * 32 + 16 : b * 32 + 24, :]
        for a in range(3):
            row = xt[a][b : b + 1] * s[3:4] - s[a : a + 1]
            perm_out[a * nbp + b : a * nbp + b + 1, :] = row
    wc = weights(nb, (KP, nbp), lax.axis_index("bead"), 1) * (1.0 / BEADS)
    parts = [hdot(wc, perm_out[a * nbp : (a + 1) * nbp, :]) for a in range(3)]
    parts += [hdot(wc, coords[a]) for a in range(3)]
    msg_out[...] = dot3(jnp.concatenate(parts, 0), perm_matrix(rank[0:1, :], w), 0)


def start_kernel(nbp, w, msg, other, rank, pack, m0, cf):
    both = dot3(msg[...] + other[...], perm_matrix(rank[0:1, :], w), 1)
    n = 3 * KP
    cf[...] = both[:n]
    m0[:n, :] = both[:n] * pack[3 * nbp + 1 : 3 * nbp + 2, :]
    m0[n:, :] = both[n:]


def centered(m, center):
    n = 3 * KP
    return [m[n + a * KP : n + (a + 1) * KP, :] - center[a] for a in range(3)]


def own_center(m):
    n = 3 * KP
    return center_of([m[n + a * KP : n + (a + 1) * KP, :] for a in range(3)], CONTR)


def tensor_targets(xt, sel_t, ft):
    compact = dot(sel_t, pair_pieces(xt), 0, 0).astype(BF16)
    ft[...] = jnp.zeros_like(ft)
    for k in range(CONTR):
        r0 = k * L + k * 32
        ft[r0 : r0 + 32, :] = compact[k * 32 : (k + 1) * 32]


def tensor_pairs(n, lst, size, fs, ft, qbuf, r2buf, tensors):
    def where_is(i):
        e = jnp.maximum(jnp.minimum(i, n - 1), 0)
        return e, pl.multiple_of(lst[1 + e], L), pl.multiple_of(lst[1 + size + e], L)

    def step(i, carry):
        e, s0, t0 = where_is(i - 1)
        for k in range(CONTR):
            c, decay, inv, v = pair_basis(r2buf[k], qbuf[e])
            l3 = 1.0 - decay
            l5 = l3 + (c * LN2) * decay
            w3 = (v * v) * inv
            w5 = w3 * (inv * inv)
            a_hi, a_lo = two(w5 * l5)
            b_hi, b_lo = two(w3 * l3)
            tensors[k, e, 0:L, :] = a_hi
            tensors[k, e, L : 2 * L, :] = a_lo
            tensors[k, e, 2 * L : 3 * L, :] = b_hi
            tensors[k, e, 3 * L : 4 * L, :] = b_lo
        e, s0, t0 = where_is(i)
        lhs = fs[pl.ds(s0, L), :]
        for k in range(CONTR):
            r2buf[k] = dot(lhs, ft[k * L : (k + 1) * L, pl.ds(t0, L)])
        return carry

    r2buf[...] = jnp.full_like(r2buf, 2.0 * CUT2)
    lax.fori_loop(0, n + 1, step, 0)


def induce_features(mu, x, sel_e):
    scale = 1.0 / (CUT2 * CUT2)
    m = [mu[a * KP : (a + 1) * KP, :] * scale for a in range(3)]
    dotted = x[0] * m[0] + x[1] * m[1] + x[2] * m[2]
    feats = m + [dotted] + [x[a] * m[b] for a in range(3) for b in range(3)]
    feats += [x[a] * dotted for a in range(3)]
    split = [split3(f) for f in feats]
    stack = jnp.concatenate([split[f][p] for p in range(3) for f in range(16)], 0)
    return dot(sel_e, stack.astype(BF16), 0, 0).astype(BF16)


def twice(x):
    return jnp.concatenate([x, x], 1)


def own_sums(w, mu, m0, tensors, acc_a, acc_b, le):
    nt = w // L
    le[...] = induce_features(mu, centered(m0, own_center(m0)), induce_select())
    acc_a[...] = jnp.zeros_like(acc_a)
    acc_b[...] = jnp.zeros_like(acc_b)
    diag, off = own_blocks(nt)
    for e, (s, t) in enumerate(diag + off):
        s0, t0 = s * L, t * L
        for k in range(CONTR):
            ra, rb = k * L, k * L + 64
            pa, pb = tensors[k, e, 0 : 2 * L, :], tensors[k, e, 2 * L : 4 * L, :]
            a0, b0 = k * 48, k * 32
            acc_a[a0 : a0 + 48, t0 : t0 + L] += dot(twice(le[ra : ra + 48, s0 : s0 + L]), pa)
            acc_b[b0 : b0 + 32, t0 : t0 + L] += dot(twice(le[rb : rb + 32, s0 : s0 + L]), pb)
            if s != t:
                back = dot(le[ra : ra + 48, t0 : t0 + L], pa, 1, 1)
                acc_a[a0 : a0 + 48, s0 : s0 + L] += back[:, :L] + back[:, L:]
                back = dot(le[rb : rb + 32, t0 : t0 + L], pb, 1, 1)
                acc_b[b0 : b0 + 32, s0 : s0 + L] += back[:, :L] + back[:, L:]


def near_sums(w, mus, cps, m0, tensors, lst, acc_a_in, acc_b_in, acc_a, acc_b, le, ev):
    nt = w // L
    center = own_center(m0)
    sel_e = induce_select()
    for s, (mu, cp) in enumerate(zip(mus, cps)):
        le[:, s * w : (s + 1) * w] = induce_features(mu, centered(cp, center), sel_e)
    acc_a[...] = acc_a_in[...]
    acc_b[...] = acc_b_in[...]
    size = 2 * nt * nt

    def step(e, carry):
        s0 = pl.multiple_of(lst[1 + e], L)
        t0 = pl.multiple_of(lst[1 + size + e], L)
        for k in range(CONTR):
            ra, rb = k * L, k * L + 64
            a0, b0 = k * 48, k * 32
            fa, fb = twice(le[ra : ra + 48, pl.ds(s0, L)]), twice(le[rb : rb + 32, pl.ds(s0, L)])
            acc_a[a0 : a0 + 48, pl.ds(t0, L)] += dot(fa, tensors[k, e, 0 : 2 * L, :])
            acc_b[b0 : b0 + 32, pl.ds(t0, L)] += dot(fb, tensors[k, e, 2 * L : 4 * L, :])
        return carry

    lax.fori_loop(0, lst[0], step, 0)
    ev[...] = jnp.zeros_like(ev)
    xt = centered(m0, center)
    for k in range(CONTR):
        o = k * 48
        sa = acc_a[o : o + 16, :] + acc_a[o + 16 : o + 32, :] + acc_a[o + 32 : o + 48, :]
        o = k * 32
        sb = acc_b[o : o + 8, :] + acc_b[o + 8 : o + 16, :] + acc_b[o + 16 : o + 24, :]
        x = [v[k : k + 1] for v in xt]
        along = x[0] * sa[0:1] + x[1] * sa[1:2] + x[2] * sa[2:3] - sa[3:4]
        for a in range(3):
            cross = sum(x[b] * sa[4 + 3 * a + b : 5 + 3 * a + b] for b in range(3))
            full = x[a] * along - cross + sa[13 + a : 14 + a]
            ev[a * KP + k : a * KP + k + 1, :] = 3.0 * full - sb[a : a + 1]


def own_first_kernel(nbp, w, m0, pack, tensors, acc_a, acc_b, le, fs, ft, cols, qrow, qbuf, r2buf, lst):
    misc = pack[3 * nbp : 3 * nbp + 8, :]
    sel_t, sel_s = pair_selects(KP, CONTR)
    xt = centered(m0, own_center(m0))
    tensor_targets(xt, sel_t, ft)
    fs[...] = dot(pair_pieces(xt), sel_s, 0, 0).astype(BF16)
    cols[...] = jnp.transpose(columns(misc))
    q_rows(misc, qrow)
    diag, off = own_blocks(w // L)
    size = len(diag) + len(off)
    fixed_list(lst, size, diag + off)
    block_q(size, 0, lst, size, True, cols, qrow, qbuf)
    tensor_pairs(size, lst, size, fs, ft, qbuf, r2buf, tensors)
    own_sums(w, m0, m0, tensors, acc_a, acc_b, le)


def own_kernel(w, mu, m0, tensors, acc_a, acc_b, le):
    own_sums(w, mu, m0, tensors, acc_a, acc_b, le)


def update(pack, nbp, cf, ev):
    return pack[3 * nbp + 1 : 3 * nbp + 2, :] * (cf[...] + ev[...])


def near_first_kernel(
    nbp, w, m0, m0a, m0b, pack, packa, packb, cf, acc_a_in, acc_b_in,
    mu_out, tensors, lst, fs, ft, cols, qrow, qbuf, r2buf, acc_a, acc_b, le, ev,
):
    nt = w // L
    base = 3 * nbp
    sel_t, sel_s = pair_selects(KP, CONTR)
    center = own_center(m0)
    xt = centered(m0, center)
    tensor_targets(xt, sel_t, ft)
    sranges = []
    for s, (m, pk) in enumerate(((m0a, packa), (m0b, packb))):
        misc = pk[base : base + 8, :]
        xs = centered(m, center)
        fs[s * w : (s + 1) * w, :] = dot(pair_pieces(xs), sel_s, 0, 0).astype(BF16)
        cols[s * w : (s + 1) * w, :] = jnp.transpose(columns(misc))
        sranges.append(ranges(xs[0], misc[1:2], CONTR, w))
    misc = pack[base : base + 8, :]
    size = 2 * nt * nt
    near_list(lst, size, ranges(xt[0], misc[1:2], CONTR, w), sranges)
    q_rows(misc, qrow)
    n = lst[0]
    block_q(n, 0, lst, size, False, cols, qrow, qbuf)
    tensor_pairs(n, lst, size, fs, ft, qbuf, r2buf, tensors)
    near_sums(w, [m0a, m0b], [m0a, m0b], m0, tensors, lst, acc_a_in, acc_b_in, acc_a, acc_b, le, ev)
    mu_out[...] = update(pack, nbp, cf, ev)


def near_kernel(
    nbp, w, mua, mub, m0, m0a, m0b, pack, cf, acc_a_in, acc_b_in, tensors, lst, mu_out, acc_a, acc_b, le, ev,
):
    near_sums(w, [mua, mub], [m0a, m0b], m0, tensors, lst, acc_a_in, acc_b_in, acc_a, acc_b, le, ev)
    mu_out[...] = update(pack, nbp, cf, ev)


def final_kernel(
    nb, nbp, w, mua, mub, m0, m0a, m0b, mu, perm, rank, acc_a_in, acc_b_in, tensors, lst,
    total_out, dip_out, acc_a, acc_b, le, ev,
):
    near_sums(w, [mua, mub], [m0a, m0b], m0, tensors, lst, acc_a_in, acc_b_in, acc_a, acc_b, le, ev)
    us = weights(nb, (nbp, KP), lax.axis_index("bead"), 0) * (1.0 / CONTR)
    parts = [perm[a * nbp : (a + 1) * nbp, :] + hdot(us, ev[a * KP : (a + 1) * KP, :]) for a in range(3)]
    parts.append(mu[...])
    out = dot3(jnp.concatenate(parts, 0), perm_matrix(rank[0:1, :], w), 0)
    for a in range(3):
        total_out[a] = out[a * nbp : a * nbp + nb]
        d0 = 3 * nbp + a * KP
        dip_out[a] = out[d0 : d0 + CONTR]


def swap_pairs(count, first):
    pairs = []
    for i in range(first, count - 1, 2):
        pairs += [(i, i + 1), (i + 1, i)]
    return pairs


def call(kernel, outs, name, scratch, args, smem_in=(), smem_out=()):
    smem = pl.BlockSpec(memory_space=pltpu.SMEM)
    vmem = pl.BlockSpec(memory_space=pltpu.VMEM)
    return pl.pallas_call(
        kernel,
        out_shape=[jax.ShapeDtypeStruct(s, d) for s, d in outs],
        in_specs=[smem if i in smem_in else vmem for i in range(len(args))],
        out_specs=[smem if i in smem_out else vmem for i in range(len(outs))],
        scratch_shapes=list(scratch),
        compiler_params=pltpu.CompilerParams(vmem_limit_bytes=VMEM_LIMIT),
        name=name,
    )(*args)


def body(positions, charges, polar, molecule):
    nb, _, w = positions.shape
    nbp = -(-nb // 16) * 16
    nt = w // L
    nbead = lax.axis_size("bead")
    nspace = lax.axis_size("space")
    rows = 3 * nbp + 8
    n = 3 * KP
    own_size = nt * (nt + 1) // 2
    near_size = 2 * nt * nt
    part = functools.partial

    def exchange(x):
        near = lax.ppermute(x, "space", swap_pairs(nspace, 0))
        far = lax.ppermute(x, "space", swap_pairs(nspace, 1))
        return near, far

    pack, rank = call(
        part(pack_kernel, nb, nbp, w), [((rows, w), F32), ((8, w), F32)], "pack",
        [pltpu.VMEM((rows, w), F32)],
        (jnp.transpose(positions, (1, 0, 2)), charges, polar, molecule),
    )
    packa, packb = exchange(pack)

    def perm_scratch(nsrc, blocks):
        return [
            pltpu.VMEM((nsrc * w, nb * 32), BF16),
            pltpu.VMEM((nb * 32, nsrc * w), BF16),
            pltpu.VMEM((nsrc * w, 8), F32),
            pltpu.VMEM((8, w), F32),
            pltpu.VMEM((blocks, L, L), F32),
            pltpu.VMEM((4, L, L), F32),
            pltpu.VMEM((4, 2 * L, L), BF16),
        ]

    acc, ft = call(
        part(perm_own_kernel, nb, nbp, w), [((nb * 32, w), F32), ((nb * L, w), BF16)], "perm_own",
        perm_scratch(1, own_size) + [pltpu.SMEM((1 + 2 * own_size,), jnp.int32)], (pack,),
    )
    perm, msg = call(
        part(perm_near_kernel, nb, nbp, w), [((3 * nbp, w), F32), ((2 * n, w), F32)], "perm_near",
        perm_scratch(2, near_size)
        + [pltpu.VMEM((nb * 32, w), F32), pltpu.SMEM((1 + 2 * near_size,), jnp.int32)],
        (pack, packa, packb, ft, acc, rank),
    )

    if nbead == 2:
        other = lax.ppermute(msg, "bead", [(0, 1), (1, 0)])
    else:
        other = lax.psum(msg, "bead") - msg
    m0, cf = call(
        part(start_kernel, nbp, w), [((2 * n, w), F32), ((n, w), F32)], "start", [], (msg, other, rank, pack),
    )
    m0a, m0b = exchange(m0)

    def tensor_scratch(nsrc, blocks):
        return [
            pltpu.VMEM((nsrc * w, L), BF16),
            pltpu.VMEM((CONTR * L, w), BF16),
            pltpu.VMEM((nsrc * w, 8), F32),
            pltpu.VMEM((8, w), F32),
            pltpu.VMEM((blocks, L, L), F32),
            pltpu.VMEM((CONTR, L, L), F32),
        ]

    accs = [((CONTR * 48, w), F32), ((CONTR * 32, w), F32)]
    near_scratch = [pltpu.VMEM(s, d) for s, d in accs]
    near_scratch += [pltpu.VMEM((CONTR * L, 2 * w), BF16), pltpu.VMEM((n, w), F32)]
    own_scratch = [pltpu.VMEM((CONTR * L, w), BF16)]
    t_own, acc_a, acc_b = call(
        part(own_first_kernel, nbp, w), [((CONTR, own_size, 4 * L, L), BF16)] + accs, "own_0",
        own_scratch + tensor_scratch(1, own_size) + [pltpu.SMEM((1 + 2 * own_size,), jnp.int32)],
        (m0, pack),
    )
    mu, t_nbr, lst = call(
        part(near_first_kernel, nbp, w),
        [((n, w), F32), ((CONTR, near_size, 4 * L, L), BF16), ((1 + 2 * near_size,), jnp.int32)], "near_0",
        tensor_scratch(2, near_size) + near_scratch,
        (m0, m0a, m0b, pack, packa, packb, cf, acc_a, acc_b), smem_out=(2,),
    )
    for step in range(1, ITERS + 1):
        mua, mub = exchange(mu)
        acc_a, acc_b = call(part(own_kernel, w), accs, f"own_{step}", own_scratch, (mu, m0, t_own))
        if step < ITERS:
            (mu,) = call(
                part(near_kernel, nbp, w), [((n, w), F32)], f"near_{step}", near_scratch,
                (mua, mub, m0, m0a, m0b, pack, cf, acc_a, acc_b, t_nbr, lst), smem_in=(10,),
            )
    total, dipoles = call(
        part(final_kernel, nb, nbp, w), [((3, nb, w), F32), ((3, CONTR, w), F32)], "final", near_scratch,
        (mua, mub, m0, m0a, m0b, mu, perm, rank, acc_a, acc_b, t_nbr, lst), smem_in=(11,),
    )
    return (jnp.transpose(total, (1, 0, 2)), jnp.transpose(dipoles, (1, 0, 2)))


def solution(mesh):
    in_specs = (P("bead", None, "space"), P("space"), P("space"), P("space"))
    out_specs = (P("bead", None, "space"), P(None, None, "space"))
    return jax.shard_map(body, mesh=mesh, in_specs=in_specs, out_specs=out_specs, check_vma=False)
```

```python
import functools
import math

import jax
import jax.numpy as jnp
from jax import lax
from jax.experimental import pallas as pl
from jax.experimental.pallas import tpu as pltpu
from jax.sharding import PartitionSpec as P

BEADS = 32
CONTR = 4
ITERS = 2
CUTOFF = 9.0
CUT2 = CUTOFF * CUTOFF
THOLE = 0.39
LOG2E = 1.4426950408889634
LN2 = 0.6931471805599453
L = 128
KP = 8
F32 = jnp.float32
BF16 = jnp.bfloat16
VMEM_LIMIT = 20 * 1024 * 1024


def split3(x):
    h = x.astype(BF16).astype(F32)
    r = x - h
    m = r.astype(BF16).astype(F32)
    return h, m, r - m


def dot(a, b, ca=1, cb=0):
    return lax.dot_general(a, b, (((ca,), (cb,)), ((), ())), preferred_element_type=F32)


def dot3(x, mat, cb):
    rows = x.shape[0]
    out = dot(jnp.concatenate(split3(x), 0).astype(BF16), mat, 1, cb)
    return (out[:rows] + out[rows : 2 * rows]) + out[2 * rows :]


T_SLOTS, S_SLOTS = [], []
for _a in range(3):
    T_SLOTS += [(_a, 1)] * 3 + [(3 + _a, 1)] * 2 + [(6 + _a, 1)]
    S_SLOTS += [(_a, -2), (3 + _a, -2), (6 + _a, -2), (_a, -2), (3 + _a, -2), (_a, -2)]
T_SLOTS += [(9, 1), (10, 1), (11, 1), (12, 1), (12, 1), (12, 1)]
S_SLOTS += [(12, 1), (12, 1), (12, 1), (9, 1), (10, 1), (11, 1)]
SLOT = 32
DEEP = 4 * len(T_SLOTS)
TYPES = 13


def perm_matrix(rank_row, w):
    rows = lax.broadcasted_iota(jnp.int32, (w, w), 0).astype(F32)
    return jnp.where(rows == rank_row, 1.0, 0.0).astype(BF16)


def pair_pieces(xs):
    hx, hy, hz = (split3(x) for x in xs)
    n = xs[0] * xs[0] + xs[1] * xs[1] + xs[2] * xs[2]
    parts = [hx[0], hy[0], hz[0], hx[1], hy[1], hz[1], hx[2], hy[2], hz[2]]
    return parts + list(split3(n)) + [jnp.ones_like(n)]


def store_rows(ref, tile, row, stride, value):
    for i in range(value.shape[1] // L):
        ref[tile + i, pl.ds(row, value.shape[0], stride=stride), :] = value[:, i * L : (i + 1) * L]


def slot_stack(pieces, slots, g):
    lo = g // 2 * 8
    top = lax.broadcasted_iota(jnp.int32, (8, pieces[0].shape[1]), 0) < 4
    here, there = {}, {}
    for kind, coef in slots:
        if (kind, coef) not in here:
            x = pieces[kind][lo : lo + 8]
            here[kind, coef] = x if coef == 1 else x * float(coef)
            there[kind, coef] = here[kind, coef] if kind == TYPES - 1 else pltpu.roll(here[kind, coef], 4, 0)
    first, second = (here, there) if g % 2 == 0 else (there, here)
    return jnp.concatenate(
        [jnp.where(top, first[slots[f]], second[slots[f + 1]]) for f in range(0, len(slots), 2)], 0
    )


def target_features(pieces, ft, count):
    for g in range(-(-count // 4)):
        stack = slot_stack(pieces, T_SLOTS, g)
        row = lax.broadcasted_iota(jnp.int32, stack.shape, 0) % 4
        for i in range(min(4, count - g * 4)):
            ft[g * 4 + i] = jnp.where(row == i, stack, 0.0).astype(BF16)


def source_features(pieces, fs, s, w, count):
    for g in range(-(-count // 4)):
        fs[g, s * w : (s + 1) * w, :] = jnp.transpose(slot_stack(pieces, S_SLOTS, g)).astype(BF16)


def sum_select(rows, count):
    lane = lax.broadcasted_iota(jnp.int32, (1, max(count * SLOT, L)), 1)
    b, r = lane // SLOT, lane % SLOT
    p, f = r // 8, r % 8
    want = jnp.where((f < 4) & (p < 3) & (b < count), (p * 4 + f) * rows + b, -1)
    row = lax.broadcasted_iota(jnp.int32, (12 * rows, lane.shape[1]), 0)
    return jnp.where(row == want, 1.0, 0.0).astype(BF16)


def center_of(xs, count):
    w = xs[0].shape[1]
    return [jnp.sum(x[:count], keepdims=True) * (1.0 / (count * w)) for x in xs]


def columns(misc):
    al = misc[1:2]
    good = al > 0.0
    inv = jnp.where(good, lax.rsqrt(jnp.where(good, al, 1.0)), 0.0)
    return jnp.concatenate([inv, misc[2:3], jnp.zeros_like(misc[:6])], 0)


def ranges(x, al, count, w):
    good = al > 0.0
    lo = jnp.where(good, x[:count], 1e30)
    hi = jnp.where(good, x[:count], -1e30)
    out = []
    for i in range(w // L):
        out.append((jnp.min(lo[:, i * L : (i + 1) * L]), jnp.max(hi[:, i * L : (i + 1) * L])))
    return out


def near_list(lst, size, trange, sranges):
    lst[1] = 0
    lst[1 + size] = 0
    count = jnp.int32(0)
    sj = 0
    for slab in sranges:
        for smin, smax in slab:
            for ti, (tmin, tmax) in enumerate(trange):
                near = (smin - tmax < CUTOFF) & (tmin - smax < CUTOFF)
                lst[1 + count] = sj * L
                lst[1 + size + count] = ti * L
                count = count + near.astype(jnp.int32)
            sj += 1
    lst[0] = count


def own_blocks(nt):
    return [(i, i) for i in range(nt)], [(i, j) for i in range(nt) for j in range(i + 1, nt)]


def pair_basis(r2, q):
    safe = jnp.maximum(r2, 1e-4)
    inv = lax.rsqrt(safe)
    c = (safe * inv) * (safe * q)
    decay = jnp.exp2(c)
    v = jnp.maximum(CUT2 - r2, 0.0) * inv
    return c, decay, inv, v


def comps(ref, first, count=3):
    out = []
    for c in range(first, first + count):
        block = ref[c // 2 * 8 : c // 2 * 8 + 8]
        out.append(block if c % 2 == 0 else pltpu.roll(block, 4, 0))
    return out


def stack_comps(parts):
    top = lax.broadcasted_iota(jnp.int32, parts[0].shape, 0) < 4
    return jnp.concatenate(
        [jnp.where(top, parts[i], pltpu.roll(parts[i + 1], 4, 0)) for i in range(0, len(parts), 2)], 0
    )


def two(x):
    hi = x.astype(BF16)
    return hi, (x - hi.astype(F32)).astype(BF16)


def weights(nb, shape, rank, bead_dim):
    b = lax.broadcasted_iota(jnp.int32, shape, bead_dim)
    k = lax.broadcasted_iota(jnp.int32, shape, 1 - bead_dim)
    turn = k * (BEADS // CONTR) - (rank * nb + b) + 2 * BEADS
    turn = (turn + BEADS // 2) % BEADS - BEADS // 2
    cos = jnp.cos(turn.astype(F32) * (2.0 * math.pi / BEADS))
    return jnp.where((k < CONTR) & (b < nb), 2.0 * cos * (1.0 + cos), 0.0)


def hdot(a, b):
    return jnp.dot(a, b, precision=lax.Precision.HIGHEST, preferred_element_type=F32)


def pack_kernel(nb, nbp, w, pos, charge, polar, mol, out, scr, posv, chargev, polarv, molv, sem):
    copies = [
        pltpu.make_async_copy(src, dst, sem.at[i])
        for i, (src, dst) in enumerate(((pos, posv), (charge, chargev), (polar, polarv), (mol, molv)))
    ]
    for c in copies:
        c.start()
    scr[...] = jnp.zeros_like(scr)
    for c in copies:
        c.wait()
    for a in range(3):
        scr[a * nbp : a * nbp + nb, :] = posv[a]
    base = 3 * nbp
    scr[base : base + 1, :] = chargev[...].reshape(1, w)
    scr[base + 1 : base + 2, :] = polarv[...].reshape(1, w)
    scr[base + 2 : base + 3, :] = molv[...].reshape(1, w).astype(F32)
    x = scr[...]
    key = jnp.sum(x[:nbp], 0, keepdims=True)
    col = jnp.transpose(jnp.broadcast_to(key, (8, w)))[:, :1]
    jj = lax.broadcasted_iota(jnp.int32, (w, w), 0)
    ii = lax.broadcasted_iota(jnp.int32, (w, w), 1)
    before = (col < key) | ((col == key) & (jj < ii))
    rank = jnp.sum(jnp.where(before, 1.0, 0.0), 0, keepdims=True)
    out[...] = dot3(x, perm_matrix(rank, w), 1)
    out[base + 3 : base + 4, :] = rank


def perm_sources(nb, nbp, w, src, pieces, xs, s, sel_r, fs, rt, cols):
    base = 3 * nbp
    misc = src[base : base + 8, :]
    source_features(pieces, fs, s, w, nb)
    q = jnp.broadcast_to(misc[0:1] * (1.0 / (CUT2 * CUT2)), xs[0].shape)
    feats = [split3(v) for v in (xs[0] * q, xs[1] * q, xs[2] * q, q)]
    stack = jnp.concatenate([feats[f][p] for p in range(3) for f in range(4)], 0)
    rt[:, s * w : (s + 1) * w] = dot(sel_r, stack.astype(BF16), 0, 0).astype(BF16)
    cols[s * w : (s + 1) * w, :] = jnp.transpose(columns(misc))
    return misc[1:2]


class Item:
    def __init__(self, e, s0, t0, g=0, sym=False):
        self.e, self.s0, self.t0, self.g, self.sym = e, s0, t0, g, sym

    def at(self, g):
        return Item(self.e, self.s0, self.t0, g, self.sym)


def perm_run(items, head, tail, nb, fs, ft, rt, qbuf, acc, r2s, fbs):
    def sums(it, f):
        for j in range(4):
            r0 = (it.g * 4 + j) * SLOT
            r = rt[r0 : r0 + SLOT, pl.ds(it.s0, L)]
            pair = f[j]
            acc[r0 : r0 + SLOT, pl.ds(it.t0, L)] += dot(jnp.concatenate([r, r], 1), pair)
            if it.sym:
                back = dot(rt[r0 : r0 + SLOT, pl.ds(it.t0, L)], pair, 1, 1)
                acc[r0 : r0 + SLOT, pl.ds(it.s0, L)] += back[:, :L] + back[:, L:]

    def functions(it, r2, f):
        for j in range(4):
            c, decay, inv, v = pair_basis(r2[j], qbuf[it.e])
            hi, lo = two((v * v) * (inv * (1.0 - decay)))
            f[j, :L, :] = hi
            f[j, L:, :] = lo

    def distances(it, r2):
        lhs = fs[it.g, pl.ds(it.s0, L), :]
        for j in range(4):
            r2[j] = dot(lhs, ft[it.g * 4 + j, :, pl.ds(it.t0, L)])

    if not items:
        if tail is not None:
            distances(tail, r2s[0])
        if head is not None:
            sums(head, fbs[1])
        return
    for i, it in enumerate(items):
        functions(it, r2s[i % 2], fbs[i % 2])
        after = items[i + 1] if i + 1 < len(items) else tail
        if after is not None:
            distances(after, r2s[(i + 1) % 2])
        before = items[i - 1] if i > 0 else head
        if before is not None:
            sums(before, fbs[(i - 1) % 2])


def perm_own_pairs(blocks, nb, *rest):
    items = [
        Item(e, s * L, t * L, g, s != t) for e, (s, t) in enumerate(blocks) for g in range(nb // 4)
    ]
    args = rest
    perm_run([], None, items[0], nb, *args)
    odd = len(items) % 2
    perm_run(items[: len(items) - odd], None, items[-1] if odd else None, nb, *args)
    if odd:
        perm_run([items[-1]], items[-2] if len(items) > 1 else None, None, nb, *args)
        fbs = args[-1]
        fbs[1][...] = fbs[0][...]
    perm_run([], items[-1], None, nb, *args)


def perm_near_pairs(n, lst, size, nb, *rest):
    fbs = rest[-1]
    fbs[1][...] = jnp.zeros_like(fbs[1])
    groups = nb // 4

    def entry(i):
        good = i < n
        e = jnp.where(good, i, 0)
        return jnp.where(good, e, size), lst[1 + e], lst[1 + size + e]

    def item(it):
        return Item(it[0], pl.multiple_of(it[1], L), pl.multiple_of(it[2], L))

    def step(i, carry):
        before, first, second, after = carry
        later = (entry(2 * i + 3), entry(2 * i + 4))
        items = [item(it).at(g) for it in (first, second) for g in range(groups)]
        perm_run(items, item(before).at(groups - 1), item(after).at(0), nb, *rest)
        return (second, after) + later

    start = entry(0)
    perm_run([], None, item(start).at(0), nb, *rest)
    last = lax.fori_loop(0, (n + 1) // 2, step, (start, start, entry(1), entry(2)))[0]
    perm_run([], item(last).at(groups - 1), None, nb, *rest)


def block_q(n, first, lst, size, own, cols, qrow, qbuf):
    def one(i, carry):
        e = first + i
        s0 = pl.multiple_of(lst[1 + e], L)
        t0 = pl.multiple_of(lst[1 + size + e], L)
        cc = cols[pl.ds(s0, L), :]
        row = qrow[:, pl.ds(t0, L)]
        q = cc[:, 0:1] * row[0:1]
        if own:
            q = jnp.where(cc[:, 1:2] == row[1:2], 0.0, q)
        qbuf[e] = q
        return carry

    lax.fori_loop(0, n, one, 0)
    qbuf[size] = jnp.zeros_like(qbuf[size])


def q_rows(misc, qrow):
    c = columns(misc)
    qrow[...] = c
    qrow[0:1, :] = c[0:1] * (-THOLE * LOG2E)


def fixed_list(lst, size, blocks):
    lst[0] = len(blocks)
    for e, (s, t) in enumerate(blocks):
        lst[1 + e] = s * L
        lst[1 + size + e] = t * L


def perm_own_kernel(nb, nbp, w, tgt, acc, ft, order, keep, fs, rt, cols, qrow, qbuf, r2a, r2b, fa, fb, lst):
    nt = w // L
    base = 3 * nbp
    sel_r = sum_select(nbp, nb)
    acc[...] = jnp.zeros_like(acc)
    order[...] = perm_matrix(tgt[base + 3 : base + 4, :], w)
    keep[...] = tgt[...]
    coords = [tgt[a * nbp : (a + 1) * nbp, :] for a in range(3)]
    xt = [x - c for x, c in zip(coords, center_of(coords, nb))]
    pieces = pair_pieces(xt)
    target_features(pieces, ft, nb)
    perm_sources(nb, nbp, w, tgt, pieces, xt, 0, sel_r, fs, rt, cols)
    q_rows(tgt[base : base + 8, :], qrow)
    diag, off = own_blocks(nt)
    size = len(diag) + len(off)
    fixed_list(lst, size, diag + off)
    block_q(size, 0, lst, size, True, cols, qrow, qbuf)
    perm_own_pairs(diag + off, nb, fs, ft, rt, qbuf, acc, (r2a, r2b), (fa, fb))


def perm_near_kernel(
    nb, nbp, w, tgt, srca, srcb, ft, acc_in, order, perm_out, msg_out, acc,
    fs, rt, cols, qrow, qbuf, r2a, r2b, fa, fb, lst,
):
    nt = w // L
    base = 3 * nbp
    coords = [tgt[a * nbp : (a + 1) * nbp, :] for a in range(3)]
    center = center_of(coords, nb)
    xt = [x - c for x, c in zip(coords, center)]
    sel_r = sum_select(nbp, nb)
    sranges = []
    for s, src in enumerate((srca, srcb)):
        xs = [src[a * nbp : (a + 1) * nbp, :] - center[a] for a in range(3)]
        al = perm_sources(nb, nbp, w, src, pair_pieces(xs), xs, s, sel_r, fs, rt, cols)
        sranges.append(ranges(xs[0], al, nb, w))
    size = 2 * nt * nt
    near_list(lst, size, ranges(xt[0], tgt[base + 1 : base + 2, :], nb, w), sranges)
    q_rows(tgt[base : base + 8, :], qrow)
    n = lst[0]
    block_q(n, 0, lst, size, False, cols, qrow, qbuf)
    perm_near_pairs(n, lst, size, nb, fs, ft, rt, qbuf, acc, (r2a, r2b), (fa, fb))
    if nb < nbp:
        perm_out[...] = jnp.zeros_like(perm_out)
    for b in range(nb):
        s = acc[b * 32 : b * 32 + 8, :] + acc[b * 32 + 8 : b * 32 + 16, :]
        s = s + acc[b * 32 + 16 : b * 32 + 24, :]
        for a in range(3):
            row = xt[a][b : b + 1] * s[3:4] - s[a : a + 1]
            perm_out[a * nbp + b : a * nbp + b + 1, :] = row
    wc = weights(nb, (KP, nbp), lax.axis_index("bead"), 1) * (1.0 / BEADS)
    parts = [hdot(wc, perm_out[a * nbp : (a + 1) * nbp, :]) for a in range(3)]
    parts += [hdot(wc, coords[a]) for a in range(3)]
    msg_out[...] = dot3(stack_comps(parts), order[...], 0)


def start_kernel(nbp, w, msg, other, order, pack, m0, cf):
    both = dot3(msg[...] + other[...], order[...], 1)
    cf[...] = both[: 2 * KP]
    row = lax.broadcasted_iota(jnp.int32, both.shape, 0)
    m0[...] = jnp.where(row < 3 * CONTR, both * pack[3 * nbp + 1 : 3 * nbp + 2, :], both)


def centered(m, center):
    return [x - c for x, c in zip(comps(m, 3), center)]


def own_center(m):
    return center_of(comps(m, 3), CONTR)


def tensor_pairs(n, lst, size, fs, ft, qbuf, r2a, r2b, tensors):
    def where_is(i):
        e = jnp.maximum(jnp.minimum(i, n - 1), 0)
        return e, pl.multiple_of(lst[1 + e], L), pl.multiple_of(lst[1 + size + e], L)

    def tensor(i, r2):
        e, _, _ = where_is(i)
        for k in range(CONTR):
            c, decay, inv, v = pair_basis(r2[k], qbuf[e])
            l3 = 1.0 - decay
            l5 = l3 + (c * LN2) * decay
            w3 = (v * v) * inv
            w5 = w3 * (inv * inv)
            a_hi, a_lo = two(w5 * l5)
            b_hi, b_lo = two(w3 * l3)
            tensors[k, e, 0:L, :] = a_hi
            tensors[k, e, L : 2 * L, :] = a_lo
            tensors[k, e, 2 * L : 3 * L, :] = b_hi
            tensors[k, e, 3 * L : 4 * L, :] = b_lo

    def distances(i, r2):
        _, s0, t0 = where_is(i)
        lhs = fs[0, pl.ds(s0, L), :]
        for k in range(CONTR):
            r2[k] = dot(lhs, ft[k, :, pl.ds(t0, L)])

    def step(p, carry):
        distances(2 * p + 1, r2b)
        tensor(2 * p, r2a)
        distances(2 * p + 2, r2a)
        tensor(2 * p + 1, r2b)
        return carry

    distances(0, r2a)
    lax.fori_loop(0, (n + 1) // 2, step, 0)


def induce_features(mu, x, le, s, w):
    scale = 1.0 / (CUT2 * CUT2)
    m = [v * scale for v in comps(mu, 0)]
    dotted = x[0] * m[0] + x[1] * m[1] + x[2] * m[2]
    feats = m + [dotted] + [x[a] * m[b] for a in range(3) for b in range(3)]
    feats += [x[a] * dotted for a in range(3)]
    tile = s * (w // L)
    for f, v in enumerate(feats):
        for p, piece in enumerate(split3(v)):
            store_rows(le, tile, p * 16 + f, L, piece[:CONTR])
            if f < 3:
                store_rows(le, tile, 64 + p * 8 + f, L, piece[:CONTR])


def twice(x):
    x = x.astype(BF16)
    return jnp.concatenate([x, x], 1)


def own_sums(w, mu, m0, tensors, acc_a, acc_b, le):
    nt = w // L
    induce_features(mu, centered(m0, own_center(m0)), le, 0, w)
    acc_a[...] = jnp.zeros_like(acc_a)
    acc_b[...] = jnp.zeros_like(acc_b)
    diag, off = own_blocks(nt)
    for e, (s, t) in enumerate(diag + off):
        s0, t0 = s * L, t * L
        for k in range(CONTR):
            ra, rb = k * L, k * L + 64
            pa, pb = tensors[k, e, 0 : 2 * L, :], tensors[k, e, 2 * L : 4 * L, :]
            a0, b0 = k * 48, k * 32
            acc_a[a0 : a0 + 48, t0 : t0 + L] += dot(twice(le[s, ra : ra + 48, :]), pa)
            acc_b[b0 : b0 + 32, t0 : t0 + L] += dot(twice(le[s, rb : rb + 32, :]), pb)
            if s != t:
                back = dot(le[t, ra : ra + 48, :].astype(BF16), pa, 1, 1)
                acc_a[a0 : a0 + 48, s0 : s0 + L] += back[:, :L] + back[:, L:]
                back = dot(le[t, rb : rb + 32, :].astype(BF16), pb, 1, 1)
                acc_b[b0 : b0 + 32, s0 : s0 + L] += back[:, :L] + back[:, L:]


def near_sums(w, mus, cps, m0, tensors, lst, acc_a, acc_b, le, ev, bring=None):
    nt = w // L
    center = own_center(m0)
    for s, (mu, cp) in enumerate(zip(mus, cps)):
        induce_features(mu, centered(cp, center), le, s, w)
    size = 2 * nt * nt
    if bring is not None:
        bring.wait()

    def step(e, carry):
        tile = lst[1 + e] // L
        t0 = pl.multiple_of(lst[1 + size + e], L)
        for k in range(CONTR):
            ra, rb = k * L, k * L + 64
            a0, b0 = k * 48, k * 32
            fa, fb = twice(le[tile, ra : ra + 48, :]), twice(le[tile, rb : rb + 32, :])
            acc_a[a0 : a0 + 48, pl.ds(t0, L)] += dot(fa, tensors[k, e, 0 : 2 * L, :])
            acc_b[b0 : b0 + 32, pl.ds(t0, L)] += dot(fb, tensors[k, e, 2 * L : 4 * L, :])
        return carry

    lax.fori_loop(0, lst[0], step, 0)
    ev[...] = jnp.zeros_like(ev)
    xt = centered(m0, center)
    for k in range(CONTR):
        o = k * 48
        sa = acc_a[o : o + 16, :] + acc_a[o + 16 : o + 32, :] + acc_a[o + 32 : o + 48, :]
        o = k * 32
        sb = acc_b[o : o + 8, :] + acc_b[o + 8 : o + 16, :] + acc_b[o + 16 : o + 24, :]
        x = [v[k : k + 1] for v in xt]
        along = x[0] * sa[0:1] + x[1] * sa[1:2] + x[2] * sa[2:3] - sa[3:4]
        for a in range(3):
            cross = sum(x[b] * sa[4 + 3 * a + b : 5 + 3 * a + b] for b in range(3))
            full = x[a] * along - cross + sa[13 + a : 14 + a]
            ev[a * CONTR + k : a * CONTR + k + 1, :] = 3.0 * full - sb[a : a + 1]


def own_first_kernel(nbp, w, m0, pack, tensors, acc_a, acc_b, le, fs, ft, cols, qrow, qbuf, r2a, r2b, lst):
    misc = pack[3 * nbp : 3 * nbp + 8, :]
    pieces = pair_pieces(centered(m0, own_center(m0)))
    target_features(pieces, ft, CONTR)
    source_features(pieces, fs, 0, w, CONTR)
    cols[...] = jnp.transpose(columns(misc))
    q_rows(misc, qrow)
    diag, off = own_blocks(w // L)
    size = len(diag) + len(off)
    fixed_list(lst, size, diag + off)
    block_q(size, 0, lst, size, True, cols, qrow, qbuf)
    tensor_pairs(size, lst, size, fs, ft, qbuf, r2a, r2b, tensors)
    own_sums(w, m0, m0, tensors, acc_a, acc_b, le)


def own_kernel(w, mu, m0, tensors, acc_a, acc_b, le):
    own_sums(w, mu, m0, tensors, acc_a, acc_b, le)


def update(pack, nbp, cf, ev):
    return pack[3 * nbp + 1 : 3 * nbp + 2, :] * (cf[...] + ev[...])


def near_first_kernel(
    nbp, w, m0, m0a, m0b, pack, packa, packb, cf, acc_a_in, acc_b_in,
    mu_out, tensors, lst, acc_a, acc_b, fs, ft, cols, qrow, qbuf, r2a, r2b, le, ev,
):
    nt = w // L
    base = 3 * nbp
    center = own_center(m0)
    xt = centered(m0, center)
    target_features(pair_pieces(xt), ft, CONTR)
    sranges = []
    for s, (m, pk) in enumerate(((m0a, packa), (m0b, packb))):
        misc = pk[base : base + 8, :]
        xs = centered(m, center)
        source_features(pair_pieces(xs), fs, s, w, CONTR)
        cols[s * w : (s + 1) * w, :] = jnp.transpose(columns(misc))
        sranges.append(ranges(xs[0], misc[1:2], CONTR, w))
    misc = pack[base : base + 8, :]
    size = 2 * nt * nt
    near_list(lst, size, ranges(xt[0], misc[1:2], CONTR, w), sranges)
    q_rows(misc, qrow)
    n = lst[0]
    block_q(n, 0, lst, size, False, cols, qrow, qbuf)
    tensor_pairs(n, lst, size, fs, ft, qbuf, r2a, r2b, tensors)
    near_sums(w, [m0a, m0b], [m0a, m0b], m0, tensors, lst, acc_a, acc_b, le, ev)
    mu_out[...] = update(pack, nbp, cf, ev)


def near_kernel(
    nbp, w, mua, mub, m0, m0a, m0b, pack, cf, acc_a_in, acc_b_in, tensors, lst_hbm, mu_out, acc_a, acc_b, le, ev, lst, sem,
):
    bring = pltpu.make_async_copy(lst_hbm, lst, sem)
    bring.start()
    near_sums(w, [mua, mub], [m0a, m0b], m0, tensors, lst, acc_a, acc_b, le, ev, bring)
    mu_out[...] = update(pack, nbp, cf, ev)


def last_own_kernel(w, mu, m0, tensors, perm, order, acc_a, acc_b, perm_out, le):
    own_sums(w, mu, m0, tensors, acc_a, acc_b, le)
    perm_out[...] = dot3(perm[...], order[...], 0)


def final_kernel(
    nb, nbp, w, mua, mub, m0, m0a, m0b, mu, perm, order, acc_a_in, acc_b_in, tensors, lst_hbm,
    total_out, dip_out, acc_a, acc_b, le, ev, lst, sem,
):
    bring = pltpu.make_async_copy(lst_hbm, lst, sem)
    bring.start()
    near_sums(w, [mua, mub], [m0a, m0b], m0, tensors, lst, acc_a, acc_b, le, ev, bring)
    out = dot3(jnp.concatenate([ev[...], mu[...]], 0), order[...], 0)
    us = weights(nb, (nbp, KP), lax.axis_index("bead"), 0) * (1.0 / CONTR)
    for a, v in enumerate(comps(out, 0)):
        total_out[a] = (perm[a * nbp : (a + 1) * nbp, :] + hdot(us, v))[:nb]
        d0 = 2 * KP + a * CONTR
        dip_out[a] = out[d0 : d0 + CONTR]


def swap_pairs(count, first):
    pairs = []
    for i in range(first, count - 1, 2):
        pairs += [(i, i + 1), (i + 1, i)]
    return pairs


def call(kernel, outs, name, scratch, args, any_in=(), smem_out=(), hbm_in=(), alias=None):
    smem = pl.BlockSpec(memory_space=pltpu.SMEM)
    vmem = pl.BlockSpec(memory_space=pltpu.VMEM)
    hbm = pl.BlockSpec(memory_space=pltpu.HBM)
    return pl.pallas_call(
        kernel,
        out_shape=[jax.ShapeDtypeStruct(s, d) for s, d in outs],
        in_specs=[pl.BlockSpec(memory_space=pl.ANY) if i in any_in else hbm if i in hbm_in else vmem for i in range(len(args))],
        out_specs=[smem if i in smem_out else vmem for i in range(len(outs))],
        scratch_shapes=list(scratch),
        input_output_aliases=alias or {},
        compiler_params=pltpu.CompilerParams(vmem_limit_bytes=VMEM_LIMIT),
        name=name,
    )(*args)


def body(positions, charges, polar, molecule):
    nb, _, w = positions.shape
    nbp = -(-nb // 16) * 16
    nt = w // L
    nbead = lax.axis_size("bead")
    nspace = lax.axis_size("space")
    rows = 3 * nbp + 8
    own_size = nt * (nt + 1) // 2
    near_size = 2 * nt * nt
    part = functools.partial

    def exchange(x):
        near = lax.ppermute(x, "space", swap_pairs(nspace, 0))
        far = lax.ppermute(x, "space", swap_pairs(nspace, 1))
        return near, far

    raw = (jnp.transpose(positions, (1, 0, 2)), charges, polar, molecule)
    (pack,) = call(
        part(pack_kernel, nb, nbp, w), [((rows, w), F32)], "pack",
        [
            pltpu.VMEM((rows, w), F32),
            pltpu.VMEM((3, nb, w), F32),
            pltpu.VMEM((w,), F32),
            pltpu.VMEM((w,), F32),
            pltpu.VMEM((w,), jnp.int32),
            pltpu.SemaphoreType.DMA((4,)),
        ],
        tuple(pltpu.with_memory_space_constraint(v, pltpu.HBM) for v in raw), hbm_in=(0, 1, 2, 3),
    )
    packa, packb = exchange(pack)

    def pair_scratch(nsrc, blocks):
        return [
            pltpu.VMEM((nsrc * w, 8), F32),
            pltpu.VMEM((8, w), F32),
            pltpu.VMEM((blocks + 1, L, L), F32),
            pltpu.VMEM((4, L, L), F32),
            pltpu.VMEM((4, L, L), F32),
        ]

    def perm_scratch(nsrc, blocks):
        return [
            pltpu.VMEM((-(-nb // 4), nsrc * w, DEEP), BF16),
            pltpu.VMEM((nb * SLOT, nsrc * w), BF16),
            *pair_scratch(nsrc, blocks),
            pltpu.VMEM((4, 2 * L, L), BF16),
            pltpu.VMEM((4, 2 * L, L), BF16),
            pltpu.SMEM((2 + 2 * blocks,), jnp.int32),
        ]

    acc, ft, order, pack = call(
        part(perm_own_kernel, nb, nbp, w),
        [((nb * SLOT, w), F32), ((nb, DEEP, w), BF16), ((w, w), BF16), ((rows, w), F32)], "perm_own",
        perm_scratch(1, own_size), (pack,),
    )
    perm, msg, _ = call(
        part(perm_near_kernel, nb, nbp, w), [((3 * nbp, w), F32), ((6 * CONTR, w), F32), ((nb * SLOT, w), F32)],
        "perm_near", perm_scratch(2, near_size), (pack, packa, packb, ft, acc, order), alias={4: 2},
    )

    if nbead == 2:
        other = lax.ppermute(msg, "bead", [(0, 1), (1, 0)])
    else:
        other = lax.psum(msg, "bead") - msg
    m0, cf = call(
        part(start_kernel, nbp, w), [((6 * CONTR, w), F32), ((2 * KP, w), F32)], "start", [], (msg, other, order, pack),
    )
    m0a, m0b = exchange(m0)

    def tensor_scratch(nsrc, blocks):
        return [
            pltpu.VMEM((1, nsrc * w, DEEP), BF16),
            pltpu.VMEM((CONTR, DEEP, w), BF16),
            *pair_scratch(nsrc, blocks),
        ]

    accs = [((CONTR * 48, w), F32), ((CONTR * 32, w), F32)]
    near_scratch = [pltpu.VMEM((2 * nt, CONTR * L, L), F32), pltpu.VMEM((2 * KP, w), F32)]
    list_scratch = [pltpu.SMEM((2 + 2 * near_size,), jnp.int32), pltpu.SemaphoreType.DMA]
    own_scratch = [pltpu.VMEM((nt, CONTR * L, L), F32)]
    t_own, acc_a, acc_b = call(
        part(own_first_kernel, nbp, w), [((CONTR, own_size, 4 * L, L), BF16)] + accs, "own_0",
        own_scratch + tensor_scratch(1, own_size) + [pltpu.SMEM((2 + 2 * own_size,), jnp.int32)],
        (m0, pack),
    )
    mu, t_nbr, lst, _, _ = call(
        part(near_first_kernel, nbp, w),
        [((2 * KP, w), F32), ((CONTR, near_size, 4 * L, L), BF16), ((2 + 2 * near_size,), jnp.int32)] + accs, "near_0",
        tensor_scratch(2, near_size) + near_scratch,
        (m0, m0a, m0b, pack, packa, packb, cf, acc_a, acc_b), smem_out=(2,), alias={7: 3, 8: 4},
    )
    for step in range(1, ITERS):
        mua, mub = exchange(mu)
        acc_a, acc_b = call(part(own_kernel, w), accs, f"own_{step}", own_scratch, (mu, m0, t_own))
        mu, _, _ = call(
            part(near_kernel, nbp, w), [((2 * KP, w), F32)] + accs, f"near_{step}", near_scratch + list_scratch,
            (mua, mub, m0, m0a, m0b, pack, cf, acc_a, acc_b, t_nbr, lst), any_in=(10,), alias={7: 1, 8: 2},
        )
    mua, mub = exchange(mu)
    acc_a, acc_b, perm = call(
        part(last_own_kernel, w), accs + [((3 * nbp, w), F32)], "own_last", own_scratch,
        (mu, m0, t_own, perm, order),
    )
    total, dipoles, _, _ = call(
        part(final_kernel, nb, nbp, w), [((3, nb, w), F32), ((3, CONTR, w), F32)] + accs, "final",
        near_scratch + list_scratch,
        (mua, mub, m0, m0a, m0b, mu, perm, order, acc_a, acc_b, t_nbr, lst), any_in=(11,), alias={8: 2, 9: 3},
    )
    return (jnp.transpose(total, (1, 0, 2)), jnp.transpose(dipoles, (1, 0, 2)))


def solution(mesh):
    in_specs = (P("bead", None, "space"), P("space"), P("space"), P("space"))
    out_specs = (P("bead", None, "space"), P(None, None, "space"))
    return jax.shard_map(body, mesh=mesh, in_specs=in_specs, out_specs=out_specs, check_vma=False)
```

```python
import functools
import math

import jax
import jax.numpy as jnp
from jax import lax
from jax.experimental import pallas as pl
from jax.experimental.pallas import tpu as pltpu
from jax.sharding import PartitionSpec as P

BEADS = 32
CONTR = 4
ITERS = 2
CUTOFF = 9.0
CUT2 = CUTOFF * CUTOFF
THOLE = 0.39
LOG2E = 1.4426950408889634
LN2 = 0.6931471805599453
L = 128
KP = 8
F32 = jnp.float32
BF16 = jnp.bfloat16
VMEM_LIMIT = 20 * 1024 * 1024


def split3(x):
    h = x.astype(BF16).astype(F32)
    r = x - h
    m = r.astype(BF16).astype(F32)
    return h, m, r - m


def dot(a, b, ca=1, cb=0):
    return lax.dot_general(a, b, (((ca,), (cb,)), ((), ())), preferred_element_type=F32)


def dot3(x, mat, cb):
    rows = x.shape[0]
    out = dot(jnp.concatenate(split3(x), 0).astype(BF16), mat, 1, cb)
    return (out[:rows] + out[rows : 2 * rows]) + out[2 * rows :]


T_SLOTS, S_SLOTS = [], []
for _a in range(3):
    T_SLOTS += [(_a, 1)] * 3 + [(3 + _a, 1)] * 2 + [(6 + _a, 1)]
    S_SLOTS += [(_a, -2), (3 + _a, -2), (6 + _a, -2), (_a, -2), (3 + _a, -2), (_a, -2)]
T_SLOTS += [(9, 1), (10, 1), (11, 1), (12, 1), (12, 1), (12, 1)]
S_SLOTS += [(12, 1), (12, 1), (12, 1), (9, 1), (10, 1), (11, 1)]
SLOT = 32
DEEP = 4 * len(T_SLOTS)
TYPES = 13


def perm_matrix(rank_row, w):
    rows = lax.broadcasted_iota(jnp.int32, (w, w), 0).astype(F32)
    return jnp.where(rows == rank_row, 1.0, 0.0).astype(BF16)


def pair_pieces(xs):
    hx, hy, hz = (split3(x) for x in xs)
    n = xs[0] * xs[0] + xs[1] * xs[1] + xs[2] * xs[2]
    parts = [hx[0], hy[0], hz[0], hx[1], hy[1], hz[1], hx[2], hy[2], hz[2]]
    return parts + list(split3(n)) + [jnp.ones_like(n)]


def slot_stack(pieces, slots, g):
    lo = g // 2 * 8
    top = lax.broadcasted_iota(jnp.int32, (8, pieces[0].shape[1]), 0) < 4
    here, there = {}, {}
    for kind, coef in slots:
        if (kind, coef) not in here:
            x = pieces[kind][lo : lo + 8]
            here[kind, coef] = x if coef == 1 else x * float(coef)
            there[kind, coef] = here[kind, coef] if kind == TYPES - 1 else pltpu.roll(here[kind, coef], 4, 0)
    first, second = (here, there) if g % 2 == 0 else (there, here)
    return jnp.concatenate(
        [jnp.where(top, first[slots[f]], second[slots[f + 1]]) for f in range(0, len(slots), 2)], 0
    )


def target_features(pieces, ft, count):
    for g in range(-(-count // 4)):
        stack = slot_stack(pieces, T_SLOTS, g)
        row = lax.broadcasted_iota(jnp.int32, stack.shape, 0) % 4
        for i in range(min(4, count - g * 4)):
            ft[g * 4 + i] = jnp.where(row == i, stack, 0.0).astype(BF16)


def source_features(pieces, fs, s, w, count):
    for g in range(-(-count // 4)):
        fs[g, s * w : (s + 1) * w, :] = jnp.transpose(slot_stack(pieces, S_SLOTS, g).astype(BF16))


def sum_select(rows, count):
    lane = lax.broadcasted_iota(jnp.int32, (1, max(count * SLOT, L)), 1)
    b, r = lane // SLOT, lane % SLOT
    p, f = r // 8, r % 8
    want = jnp.where((f < 4) & (p < 3) & (b < count), (p * 4 + f) * rows + b, -1)
    row = lax.broadcasted_iota(jnp.int32, (12 * rows, lane.shape[1]), 0)
    return jnp.where(row == want, 1.0, 0.0).astype(BF16)


def center_of(xs, count):
    w = xs[0].shape[1]
    return [jnp.sum(x[:count], keepdims=True) * (1.0 / (count * w)) for x in xs]


def columns(misc):
    al = misc[1:2]
    good = al > 0.0
    inv = jnp.where(good, lax.rsqrt(jnp.where(good, al, 1.0)), 0.0)
    return jnp.concatenate([inv, misc[2:3], jnp.zeros_like(misc[:6])], 0)


def ranges(x, al, count, w):
    good = al > 0.0
    lo = jnp.where(good, x[:count], 1e30)
    hi = jnp.where(good, x[:count], -1e30)
    out = []
    for i in range(w // L):
        out.append((jnp.min(lo[:, i * L : (i + 1) * L]), jnp.max(hi[:, i * L : (i + 1) * L])))
    return out


def near_list(lst, size, trange, sranges):
    lst[1] = 0
    lst[1 + size] = 0
    count = jnp.int32(0)
    sj = 0
    for slab in sranges:
        for smin, smax in slab:
            for ti, (tmin, tmax) in enumerate(trange):
                near = (smin - tmax < CUTOFF) & (tmin - smax < CUTOFF)
                lst[1 + count] = sj * L
                lst[1 + size + count] = ti * L
                count = count + near.astype(jnp.int32)
            sj += 1
    lst[0] = count


def own_blocks(nt):
    return [(i, i) for i in range(nt)], [(i, j) for i in range(nt) for j in range(i + 1, nt)]


def pair_basis(r2, q):
    safe = jnp.maximum(r2, 1e-4)
    inv = lax.rsqrt(safe)
    c = (safe * inv) * (safe * q)
    decay = jnp.exp2(c)
    v = jnp.maximum(CUT2 - r2, 0.0) * inv
    return c, decay, inv, v


def comps(ref, first, count=3):
    out = []
    for c in range(first, first + count):
        block = ref[c // 2 * 8 : c // 2 * 8 + 8]
        out.append(block if c % 2 == 0 else pltpu.roll(block, 4, 0))
    return out


def stack_comps(parts):
    top = lax.broadcasted_iota(jnp.int32, parts[0].shape, 0) < 4
    return jnp.concatenate(
        [jnp.where(top, parts[i], pltpu.roll(parts[i + 1], 4, 0)) for i in range(0, len(parts), 2)], 0
    )


def two(x):
    hi = x.astype(BF16)
    return hi, (x - hi.astype(F32)).astype(BF16)


def weights(nb, shape, rank, bead_dim):
    b = lax.broadcasted_iota(jnp.int32, shape, bead_dim)
    k = lax.broadcasted_iota(jnp.int32, shape, 1 - bead_dim)
    turn = k * (BEADS // CONTR) - (rank * nb + b) + 2 * BEADS
    turn = (turn + BEADS // 2) % BEADS - BEADS // 2
    cos = jnp.cos(turn.astype(F32) * (2.0 * math.pi / BEADS))
    return jnp.where((k < CONTR) & (b < nb), 2.0 * cos * (1.0 + cos), 0.0)


def hdot(a, b):
    return jnp.dot(a, b, precision=lax.Precision.HIGHEST, preferred_element_type=F32)


def pack_kernel(nb, nbp, w, pos, charge, polar, mol, out, sel, scr, posv, chargev, polarv, molv, sem):
    copies = [
        pltpu.make_async_copy(src, dst, sem.at[i])
        for i, (src, dst) in enumerate(((pos, posv), (charge, chargev), (polar, polarv), (mol, molv)))
    ]
    for c in copies:
        c.start()
    sel[...] = sum_select(nbp, nb)
    scr[...] = jnp.zeros_like(scr)
    for c in copies:
        c.wait()
    for a in range(3):
        scr[a * nbp : a * nbp + nb, :] = posv[a]
    base = 3 * nbp
    scr[base : base + 1, :] = chargev[...].reshape(1, w)
    scr[base + 1 : base + 2, :] = polarv[...].reshape(1, w)
    scr[base + 2 : base + 3, :] = molv[...].reshape(1, w).astype(F32)
    x = scr[...]
    key = jnp.sum(x[:nbp], 0, keepdims=True)
    col = jnp.transpose(jnp.broadcast_to(key, (8, w)))[:, :1]
    jj = lax.broadcasted_iota(jnp.int32, (w, w), 0)
    ii = lax.broadcasted_iota(jnp.int32, (w, w), 1)
    before = (col < key) | ((col == key) & (jj < ii))
    rank = jnp.sum(jnp.where(before, 1.0, 0.0), 0, keepdims=True)
    out[...] = dot3(x, perm_matrix(rank, w), 1)
    out[base + 3 : base + 4, :] = rank


def perm_sources(nb, nbp, w, src, pieces, xs, s, sel_r, fs, rt, cols):
    base = 3 * nbp
    misc = src[base : base + 8, :]
    source_features(pieces, fs, s, w, nb)
    q = jnp.broadcast_to(misc[0:1] * (1.0 / (CUT2 * CUT2)), xs[0].shape)
    feats = [split3(v) for v in (xs[0] * q, xs[1] * q, xs[2] * q, q)]
    stack = jnp.concatenate([feats[f][p] for p in range(3) for f in range(4)], 0)
    rt[:, s * w : (s + 1) * w] = dot(sel_r, stack.astype(BF16), 0, 0).astype(BF16)
    cols[s * w : (s + 1) * w, :] = jnp.transpose(columns(misc))
    return misc[1:2]


class Item:
    def __init__(self, e, s0, t0, g=0, sym=False):
        self.e, self.s0, self.t0, self.g, self.sym = e, s0, t0, g, sym

    def at(self, g):
        return Item(self.e, self.s0, self.t0, g, self.sym)


def perm_run(items, head, tail, nb, fs, ft, rt, qbuf, acc, r2s, fbs):
    def sums(it, f):
        for j in range(4):
            r0 = (it.g * 4 + j) * SLOT
            r = rt[r0 : r0 + SLOT, pl.ds(it.s0, L)]
            pair = f[j]
            acc[it.t0 // L, r0 : r0 + SLOT, :] += dot(jnp.concatenate([r, r], 1), pair)
            if it.sym:
                back = dot(rt[r0 : r0 + SLOT, pl.ds(it.t0, L)], pair, 1, 1)
                acc[it.s0 // L, r0 : r0 + SLOT, :] += back[:, :L] + back[:, L:]

    def functions(it, r2, f):
        for j in range(4):
            c, decay, inv, v = pair_basis(r2[j], qbuf[it.e])
            hi, lo = two((v * v) * (inv * (1.0 - decay)))
            f[j, :L, :] = hi
            f[j, L:, :] = lo

    def distances(it, r2):
        lhs = fs[it.g, pl.ds(it.s0, L), :]
        for j in range(4):
            r2[j] = dot(lhs, ft[it.g * 4 + j, :, pl.ds(it.t0, L)])

    if not items:
        if tail is not None:
            distances(tail, r2s[0])
        if head is not None:
            sums(head, fbs[1])
        return
    for i, it in enumerate(items):
        functions(it, r2s[i % 2], fbs[i % 2])
        after = items[i + 1] if i + 1 < len(items) else tail
        if after is not None:
            distances(after, r2s[(i + 1) % 2])
        before = items[i - 1] if i > 0 else head
        if before is not None:
            sums(before, fbs[(i - 1) % 2])


def perm_own_pairs(blocks, nb, *rest):
    items = [
        Item(e, s * L, t * L, g, s != t) for e, (s, t) in enumerate(blocks) for g in range(nb // 4)
    ]
    args = rest
    perm_run([], None, items[0], nb, *args)
    odd = len(items) % 2
    perm_run(items[: len(items) - odd], None, items[-1] if odd else None, nb, *args)
    if odd:
        perm_run([items[-1]], items[-2] if len(items) > 1 else None, None, nb, *args)
        fbs = args[-1]
        fbs[1][...] = fbs[0][...]
    perm_run([], items[-1], None, nb, *args)


def perm_near_pairs(n, lst, size, nb, *rest):
    fbs = rest[-1]
    fbs[1][...] = jnp.zeros_like(fbs[1])
    groups = nb // 4

    def entry(i):
        good = i < n
        e = jnp.where(good, i, 0)
        return jnp.where(good, e, size), lst[1 + e], lst[1 + size + e]

    def item(it):
        return Item(it[0], pl.multiple_of(it[1], L), pl.multiple_of(it[2], L))

    def step(i, carry):
        before, first, second, after = carry
        later = (entry(2 * i + 3), entry(2 * i + 4))
        items = [item(it).at(g) for it in (first, second) for g in range(groups)]
        perm_run(items, item(before).at(groups - 1), item(after).at(0), nb, *rest)
        return (second, after) + later

    start = entry(0)
    perm_run([], None, item(start).at(0), nb, *rest)
    last = lax.fori_loop(0, (n + 1) // 2, step, (start, start, entry(1), entry(2)))[0]
    perm_run([], item(last).at(groups - 1), None, nb, *rest)


def block_q(n, first, lst, size, own, cols, qrow, qbuf):
    def one(i, carry):
        e = first + i
        s0 = pl.multiple_of(lst[1 + e], L)
        t0 = pl.multiple_of(lst[1 + size + e], L)
        cc = cols[pl.ds(s0, L), :]
        row = qrow[:, pl.ds(t0, L)]
        q = cc[:, 0:1] * row[0:1]
        if own:
            q = jnp.where(cc[:, 1:2] == row[1:2], 0.0, q)
        qbuf[e] = q
        return carry

    lax.fori_loop(0, n, one, 0)
    qbuf[size] = jnp.zeros_like(qbuf[size])


def q_rows(misc, qrow):
    c = columns(misc)
    qrow[...] = c
    qrow[0:1, :] = c[0:1] * (-THOLE * LOG2E)


def fixed_list(lst, size, blocks):
    lst[0] = len(blocks)
    for e, (s, t) in enumerate(blocks):
        lst[1 + e] = s * L
        lst[1 + size + e] = t * L


def perm_own_kernel(nb, nbp, w, tgt, sel, acc, ft, order, keep, fs, rt, cols, qrow, qbuf, r2a, r2b, fa, fb, lst):
    nt = w // L
    base = 3 * nbp
    sel_r = sel[...]
    acc[...] = jnp.zeros_like(acc)
    order[...] = perm_matrix(tgt[base + 3 : base + 4, :], w)
    keep[...] = tgt[...]
    coords = [tgt[a * nbp : (a + 1) * nbp, :] for a in range(3)]
    xt = [x - c for x, c in zip(coords, center_of(coords, nb))]
    pieces = pair_pieces(xt)
    target_features(pieces, ft, nb)
    perm_sources(nb, nbp, w, tgt, pieces, xt, 0, sel_r, fs, rt, cols)
    q_rows(tgt[base : base + 8, :], qrow)
    diag, off = own_blocks(nt)
    size = len(diag) + len(off)
    fixed_list(lst, size, diag + off)
    block_q(size, 0, lst, size, True, cols, qrow, qbuf)
    perm_own_pairs(diag + off, nb, fs, ft, rt, qbuf, acc, (r2a, r2b), (fa, fb))


def perm_near_kernel(
    nb, nbp, w, tgt, srca, srcb, sel, ft, acc_in, order, perm_out, msg_out, acc,
    fs, rt, cols, qrow, qbuf, r2a, r2b, fa, fb, lst,
):
    nt = w // L
    base = 3 * nbp
    coords = [tgt[a * nbp : (a + 1) * nbp, :] for a in range(3)]
    center = center_of(coords, nb)
    xt = [x - c for x, c in zip(coords, center)]
    sel_r = sel[...]
    sranges = []
    for s, src in enumerate((srca, srcb)):
        xs = [src[a * nbp : (a + 1) * nbp, :] - center[a] for a in range(3)]
        al = perm_sources(nb, nbp, w, src, pair_pieces(xs), xs, s, sel_r, fs, rt, cols)
        sranges.append(ranges(xs[0], al, nb, w))
    size = 2 * nt * nt
    near_list(lst, size, ranges(xt[0], tgt[base + 1 : base + 2, :], nb, w), sranges)
    q_rows(tgt[base : base + 8, :], qrow)
    n = lst[0]
    block_q(n, 0, lst, size, False, cols, qrow, qbuf)
    perm_near_pairs(n, lst, size, nb, fs, ft, rt, qbuf, acc, (r2a, r2b), (fa, fb))
    if nb < nbp:
        perm_out[...] = jnp.zeros_like(perm_out)
    for i in range(nt):
        tile = slice(i * L, (i + 1) * L)
        sums = []
        for f in range(4):
            h, m, l = (acc[i, pl.ds(p * 8 + f, nb, stride=SLOT), :] for p in range(3))
            sums.append((h + m) + l)
        for a in range(3):
            perm_out[a * nbp : a * nbp + nb, tile] = xt[a][:nb, tile] * sums[3] - sums[a]
    wc = weights(nb, (KP, nbp), lax.axis_index("bead"), 1) * (1.0 / BEADS)
    parts = [hdot(wc, perm_out[a * nbp : (a + 1) * nbp, :]) for a in range(3)]
    parts += [hdot(wc, coords[a]) for a in range(3)]
    msg_out[...] = dot3(stack_comps(parts), order[...], 0)


def start_kernel(nbp, w, msg, other, order, pack, m0, cf):
    both = dot3(msg[...] + other[...], order[...], 1)
    cf[...] = both[: 2 * KP]
    row = lax.broadcasted_iota(jnp.int32, both.shape, 0)
    m0[...] = jnp.where(row < 3 * CONTR, both * pack[3 * nbp + 1 : 3 * nbp + 2, :], both)


def centered(m, center):
    return [x - c for x, c in zip(comps(m, 3), center)]


def own_center(m):
    return center_of(comps(m, 3), CONTR)


def tensor_pairs(n, lst, size, fs, ft, qbuf, r2a, r2b, tensors):
    def where_is(i):
        e = jnp.maximum(jnp.minimum(i, n - 1), 0)
        return e, pl.multiple_of(lst[1 + e], L), pl.multiple_of(lst[1 + size + e], L)

    def tensor(i, r2):
        e, _, _ = where_is(i)
        for k in range(CONTR):
            c, decay, inv, v = pair_basis(r2[k], qbuf[e])
            l3 = 1.0 - decay
            l5 = l3 + (c * LN2) * decay
            w3 = (v * v) * inv
            w5 = w3 * (inv * inv)
            a_hi, a_lo = two(w5 * l5)
            b_hi, b_lo = two(w3 * l3)
            tensors[k, e, 0:L, :] = a_hi
            tensors[k, e, L : 2 * L, :] = a_lo
            tensors[k, e, 2 * L : 3 * L, :] = b_hi
            tensors[k, e, 3 * L : 4 * L, :] = b_lo

    def distances(i, r2):
        _, s0, t0 = where_is(i)
        lhs = fs[0, pl.ds(s0, L), :]
        for k in range(CONTR):
            r2[k] = dot(lhs, ft[k, :, pl.ds(t0, L)])

    def step(p, carry):
        distances(2 * p + 1, r2b)
        tensor(2 * p, r2a)
        distances(2 * p + 2, r2a)
        tensor(2 * p + 1, r2b)
        return carry

    distances(0, r2a)
    lax.fori_loop(0, (n + 1) // 2, step, 0)


def induce_features(mu, x, le, s, w):
    scale = 1.0 / (CUT2 * CUT2)
    m = [v * scale for v in comps(mu, 0)]
    dotted = x[0] * m[0] + x[1] * m[1] + x[2] * m[2]
    feats = m + [dotted] + [x[a] * m[b] for a in range(3) for b in range(3)]
    feats += [x[a] * dotted for a in range(3)]
    nt = w // L
    for f, v in enumerate(feats):
        for p, piece in enumerate(split3(v)):
            row = (p * 16 + f) * KP
            for i in range(nt):
                le[s * nt + i, row : row + KP, :] = piece[:, i * L : (i + 1) * L]


def features_of(le, tile, k):
    first = le[tile, pl.ds(k, 48, stride=KP), :]
    second = [le[tile, pl.ds(p * 16 * KP + k, 8, stride=KP), :] for p in range(3)]
    return first.astype(BF16), jnp.concatenate(second, 0).astype(BF16)


def twice(x):
    return jnp.concatenate([x, x], 1)


def own_sums(w, mu, m0, tensors, acc_a, acc_b, le):
    nt = w // L
    induce_features(mu, centered(m0, own_center(m0)), le, 0, w)
    acc_a[...] = jnp.zeros_like(acc_a)
    acc_b[...] = jnp.zeros_like(acc_b)
    diag, off = own_blocks(nt)
    for e, (s, t) in enumerate(diag + off):
        s0, t0 = s * L, t * L
        for k in range(CONTR):
            pa, pb = tensors[k, e, 0 : 2 * L, :], tensors[k, e, 2 * L : 4 * L, :]
            a0, b0 = k * 48, k * 24
            fa, fb = features_of(le, s, k)
            acc_a[a0 : a0 + 48, t0 : t0 + L] += dot(twice(fa), pa)
            acc_b[b0 : b0 + 24, t0 : t0 + L] += dot(twice(fb), pb)
            if s != t:
                fa, fb = features_of(le, t, k)
                back = dot(fa, pa, 1, 1)
                acc_a[a0 : a0 + 48, s0 : s0 + L] += back[:, :L] + back[:, L:]
                back = dot(fb, pb, 1, 1)
                acc_b[b0 : b0 + 24, s0 : s0 + L] += back[:, :L] + back[:, L:]


def near_sums(w, mus, cps, m0, tensors, lst, acc_a, acc_b, le, ev, bring=None):
    nt = w // L
    center = own_center(m0)
    for s, (mu, cp) in enumerate(zip(mus, cps)):
        induce_features(mu, centered(cp, center), le, s, w)
    size = 2 * nt * nt
    if bring is not None:
        bring.wait()

    def add(e):
        tile = lst[1 + e] // L
        t0 = pl.multiple_of(lst[1 + size + e], L)
        for k in range(CONTR):
            a0, b0 = k * 48, k * 24
            fa, fb = features_of(le, tile, k)
            acc_a[a0 : a0 + 48, pl.ds(t0, L)] += dot(twice(fa), tensors[k, e, 0 : 2 * L, :])
            acc_b[b0 : b0 + 24, pl.ds(t0, L)] += dot(twice(fb), tensors[k, e, 2 * L : 4 * L, :])

    def both(i, carry):
        add(2 * i)
        add(2 * i + 1)
        return carry

    def single(i, carry):
        add(lst[0] - 1)
        return carry

    lax.fori_loop(0, lst[0] // 2, both, 0)
    lax.fori_loop(0, lst[0] % 2, single, 0)
    ev[...] = jnp.zeros_like(ev)
    xt = centered(m0, center)
    for k in range(CONTR):
        o = k * 48
        sa = acc_a[o : o + 16, :] + acc_a[o + 16 : o + 32, :] + acc_a[o + 32 : o + 48, :]
        o = k * 24
        sb = acc_b[o : o + 8, :] + acc_b[o + 8 : o + 16, :] + acc_b[o + 16 : o + 24, :]
        x = [v[k : k + 1] for v in xt]
        along = x[0] * sa[0:1] + x[1] * sa[1:2] + x[2] * sa[2:3] - sa[3:4]
        for a in range(3):
            cross = sum(x[b] * sa[4 + 3 * a + b : 5 + 3 * a + b] for b in range(3))
            full = x[a] * along - cross + sa[13 + a : 14 + a]
            ev[a * CONTR + k : a * CONTR + k + 1, :] = 3.0 * full - sb[a : a + 1]


def own_first_kernel(nbp, w, m0, pack, tensors, acc_a, acc_b, le, fs, ft, cols, qrow, qbuf, r2a, r2b, lst):
    misc = pack[3 * nbp : 3 * nbp + 8, :]
    pieces = pair_pieces(centered(m0, own_center(m0)))
    target_features(pieces, ft, CONTR)
    source_features(pieces, fs, 0, w, CONTR)
    cols[...] = jnp.transpose(columns(misc))
    q_rows(misc, qrow)
    diag, off = own_blocks(w // L)
    size = len(diag) + len(off)
    fixed_list(lst, size, diag + off)
    block_q(size, 0, lst, size, True, cols, qrow, qbuf)
    tensor_pairs(size, lst, size, fs, ft, qbuf, r2a, r2b, tensors)
    own_sums(w, m0, m0, tensors, acc_a, acc_b, le)


def own_kernel(w, mu, m0, tensors, acc_a, acc_b, le):
    own_sums(w, mu, m0, tensors, acc_a, acc_b, le)


def update(pack, nbp, cf, ev):
    return pack[3 * nbp + 1 : 3 * nbp + 2, :] * (cf[...] + ev[...])


def near_first_kernel(
    nbp, w, m0, m0a, m0b, pack, packa, packb, cf, acc_a_in, acc_b_in,
    mu_out, tensors, lst_out, acc_a, acc_b, fs, ft, cols, qrow, qbuf, r2a, r2b, le, ev, lst, sem,
):
    nt = w // L
    base = 3 * nbp
    center = own_center(m0)
    xt = centered(m0, center)
    target_features(pair_pieces(xt), ft, CONTR)
    sranges = []
    for s, (m, pk) in enumerate(((m0a, packa), (m0b, packb))):
        misc = pk[base : base + 8, :]
        xs = centered(m, center)
        source_features(pair_pieces(xs), fs, s, w, CONTR)
        cols[s * w : (s + 1) * w, :] = jnp.transpose(columns(misc))
        sranges.append(ranges(xs[0], misc[1:2], CONTR, w))
    misc = pack[base : base + 8, :]
    size = 2 * nt * nt
    near_list(lst, size, ranges(xt[0], misc[1:2], CONTR, w), sranges)
    leave = pltpu.make_async_copy(lst, lst_out, sem)
    leave.start()
    q_rows(misc, qrow)
    n = lst[0]
    block_q(n, 0, lst, size, False, cols, qrow, qbuf)
    tensor_pairs(n, lst, size, fs, ft, qbuf, r2a, r2b, tensors)
    near_sums(w, [m0a, m0b], [m0a, m0b], m0, tensors, lst, acc_a, acc_b, le, ev)
    mu_out[...] = update(pack, nbp, cf, ev)
    leave.wait()


def near_kernel(
    nbp, w, mua, mub, m0, m0a, m0b, pack, cf, acc_a_in, acc_b_in, tensors, lst_hbm, mu_out, acc_a, acc_b, le, ev, lst, sem,
):
    bring = pltpu.make_async_copy(lst_hbm, lst, sem)
    bring.start()
    near_sums(w, [mua, mub], [m0a, m0b], m0, tensors, lst, acc_a, acc_b, le, ev, bring)
    mu_out[...] = update(pack, nbp, cf, ev)


def last_own_kernel(w, mu, m0, tensors, perm, order, acc_a, acc_b, perm_out, le):
    own_sums(w, mu, m0, tensors, acc_a, acc_b, le)
    perm_out[...] = dot3(perm[...], order[...], 0)


def final_kernel(
    nb, nbp, w, mua, mub, m0, m0a, m0b, mu, perm, order, acc_a_in, acc_b_in, tensors, lst_hbm,
    total_out, dip_out, acc_a, acc_b, le, ev, lst, sem,
):
    bring = pltpu.make_async_copy(lst_hbm, lst, sem)
    bring.start()
    near_sums(w, [mua, mub], [m0a, m0b], m0, tensors, lst, acc_a, acc_b, le, ev, bring)
    out = dot3(jnp.concatenate([ev[...], mu[...]], 0), order[...], 0)
    us = weights(nb, (nbp, KP), lax.axis_index("bead"), 0) * (1.0 / CONTR)
    for a, v in enumerate(comps(out, 0)):
        total_out[a] = (perm[a * nbp : (a + 1) * nbp, :] + hdot(us, v))[:nb]
        d0 = 2 * KP + a * CONTR
        dip_out[a] = out[d0 : d0 + CONTR]


def swap_pairs(count, first):
    pairs = []
    for i in range(first, count - 1, 2):
        pairs += [(i, i + 1), (i + 1, i)]
    return pairs


def call(kernel, outs, name, scratch, args, any_in=(), any_out=(), hbm_in=(), alias=None):
    vmem = pl.BlockSpec(memory_space=pltpu.VMEM)
    hbm = pl.BlockSpec(memory_space=pltpu.HBM)
    return pl.pallas_call(
        kernel,
        out_shape=[jax.ShapeDtypeStruct(s, d) for s, d in outs],
        in_specs=[pl.BlockSpec(memory_space=pl.ANY) if i in any_in else hbm if i in hbm_in else vmem for i in range(len(args))],
        out_specs=[pl.BlockSpec(memory_space=pl.ANY) if i in any_out else vmem for i in range(len(outs))],
        scratch_shapes=list(scratch),
        input_output_aliases=alias or {},
        compiler_params=pltpu.CompilerParams(vmem_limit_bytes=VMEM_LIMIT),
        name=name,
    )(*args)


def body(positions, charges, polar, molecule):
    nb, _, w = positions.shape
    nbp = -(-nb // 16) * 16
    nt = w // L
    nbead = lax.axis_size("bead")
    nspace = lax.axis_size("space")
    rows = 3 * nbp + 8
    own_size = nt * (nt + 1) // 2
    near_size = 2 * nt * nt
    part = functools.partial

    def exchange(x):
        near = lax.ppermute(x, "space", swap_pairs(nspace, 0))
        far = lax.ppermute(x, "space", swap_pairs(nspace, 1))
        return near, far

    raw = (jnp.transpose(positions, (1, 0, 2)), charges, polar, molecule)
    pack, sel = call(
        part(pack_kernel, nb, nbp, w), [((rows, w), F32), ((12 * nbp, max(nb * SLOT, L)), BF16)], "pack",
        [
            pltpu.VMEM((rows, w), F32),
            pltpu.VMEM((3, nb, w), F32),
            pltpu.VMEM((w,), F32),
            pltpu.VMEM((w,), F32),
            pltpu.VMEM((w,), jnp.int32),
            pltpu.SemaphoreType.DMA((4,)),
        ],
        tuple(pltpu.with_memory_space_constraint(v, pltpu.HBM) for v in raw), hbm_in=(0, 1, 2, 3),
    )
    packa, packb = exchange(pack)

    def pair_scratch(nsrc, blocks):
        return [
            pltpu.VMEM((nsrc * w, 8), F32),
            pltpu.VMEM((8, w), F32),
            pltpu.VMEM((blocks + 1, L, L), F32),
            pltpu.VMEM((4, L, L), F32),
            pltpu.VMEM((4, L, L), F32),
        ]

    def perm_scratch(nsrc, blocks):
        return [
            pltpu.VMEM((-(-nb // 4), nsrc * w, DEEP), BF16),
            pltpu.VMEM((nb * SLOT, nsrc * w), BF16),
            *pair_scratch(nsrc, blocks),
            pltpu.VMEM((4, 2 * L, L), BF16),
            pltpu.VMEM((4, 2 * L, L), BF16),
            pltpu.SMEM((2 + 2 * blocks,), jnp.int32),
        ]

    acc, ft, order, pack = call(
        part(perm_own_kernel, nb, nbp, w),
        [((nt, nb * SLOT, L), F32), ((nb, DEEP, w), BF16), ((w, w), BF16), ((rows, w), F32)], "perm_own",
        perm_scratch(1, own_size), (pack, sel),
    )
    perm, msg, _ = call(
        part(perm_near_kernel, nb, nbp, w), [((3 * nbp, w), F32), ((6 * CONTR, w), F32), ((nt, nb * SLOT, L), F32)],
        "perm_near", perm_scratch(2, near_size), (pack, packa, packb, sel, ft, acc, order), alias={5: 2},
    )

    if nbead == 2:
        other = lax.ppermute(msg, "bead", [(0, 1), (1, 0)])
    else:
        other = lax.psum(msg, "bead") - msg
    m0, cf = call(
        part(start_kernel, nbp, w), [((6 * CONTR, w), F32), ((2 * KP, w), F32)], "start", [], (msg, other, order, pack),
    )
    m0a, m0b = exchange(m0)

    def tensor_scratch(nsrc, blocks):
        return [
            pltpu.VMEM((1, nsrc * w, DEEP), BF16),
            pltpu.VMEM((CONTR, DEEP, w), BF16),
            *pair_scratch(nsrc, blocks),
        ]

    accs = [((CONTR * 48, w), F32), ((CONTR * 24, w), F32)]
    near_scratch = [pltpu.VMEM((2 * nt, 48 * KP, L), F32), pltpu.VMEM((2 * KP, w), F32)]
    list_scratch = [pltpu.SMEM((2 + 2 * near_size,), jnp.int32), pltpu.SemaphoreType.DMA]
    own_scratch = [pltpu.VMEM((nt, 48 * KP, L), F32)]
    t_own, acc_a, acc_b = call(
        part(own_first_kernel, nbp, w), [((CONTR, own_size, 4 * L, L), BF16)] + accs, "own_0",
        own_scratch + tensor_scratch(1, own_size) + [pltpu.SMEM((2 + 2 * own_size,), jnp.int32)],
        (m0, pack),
    )
    mu, t_nbr, lst, _, _ = call(
        part(near_first_kernel, nbp, w),
        [((2 * KP, w), F32), ((CONTR, near_size, 4 * L, L), BF16), ((2 + 2 * near_size,), jnp.int32)] + accs, "near_0",
        tensor_scratch(2, near_size) + near_scratch + list_scratch,
        (m0, m0a, m0b, pack, packa, packb, cf, acc_a, acc_b), any_out=(2,), alias={7: 3, 8: 4},
    )
    for step in range(1, ITERS):
        mua, mub = exchange(mu)
        acc_a, acc_b = call(part(own_kernel, w), accs, f"own_{step}", own_scratch, (mu, m0, t_own))
        mu, _, _ = call(
            part(near_kernel, nbp, w), [((2 * KP, w), F32)] + accs, f"near_{step}", near_scratch + list_scratch,
            (mua, mub, m0, m0a, m0b, pack, cf, acc_a, acc_b, t_nbr, lst), any_in=(10,), alias={7: 1, 8: 2},
        )
    mua, mub = exchange(mu)
    acc_a, acc_b, perm = call(
        part(last_own_kernel, w), accs + [((3 * nbp, w), F32)], "own_last", own_scratch,
        (mu, m0, t_own, perm, order),
    )
    total, dipoles, _, _ = call(
        part(final_kernel, nb, nbp, w), [((3, nb, w), F32), ((3, CONTR, w), F32)] + accs, "final",
        near_scratch + list_scratch,
        (mua, mub, m0, m0a, m0b, mu, perm, order, acc_a, acc_b, t_nbr, lst), any_in=(11,), alias={8: 2, 9: 3},
    )
    return (jnp.transpose(total, (1, 0, 2)), jnp.transpose(dipoles, (1, 0, 2)))


def solution(mesh):
    in_specs = (P("bead", None, "space"), P("space"), P("space"), P("space"))
    out_specs = (P("bead", None, "space"), P(None, None, "space"))
    return jax.shard_map(body, mesh=mesh, in_specs=in_specs, out_specs=out_specs, check_vma=False)
```

```python
import functools
import math

import jax
import jax.numpy as jnp
from jax import lax
from jax.experimental import pallas as pl
from jax.experimental.pallas import tpu as pltpu
from jax.sharding import PartitionSpec as P

BEADS = 32
CONTR = 4
ITERS = 2
CUTOFF = 9.0
CUT2 = CUTOFF * CUTOFF
THOLE = 0.39
LOG2E = 1.4426950408889634
LN2 = 0.6931471805599453
L = 128
KP = 8
F32 = jnp.float32
BF16 = jnp.bfloat16
VMEM_LIMIT = 20 * 1024 * 1024


def split3(x):
    h = x.astype(BF16).astype(F32)
    r = x - h
    m = r.astype(BF16).astype(F32)
    return h, m, r - m


def dot(a, b, ca=1, cb=0):
    return lax.dot_general(a, b, (((ca,), (cb,)), ((), ())), preferred_element_type=F32)


def dot3(x, mat, cb):
    rows = x.shape[0]
    out = dot(jnp.concatenate(split3(x), 0).astype(BF16), mat, 1, cb)
    return (out[:rows] + out[rows : 2 * rows]) + out[2 * rows :]


T_SLOTS, S_SLOTS = [], []
for _a in range(3):
    T_SLOTS += [(_a, 1)] * 3 + [(3 + _a, 1)] * 2 + [(6 + _a, 1)]
    S_SLOTS += [(_a, -2), (3 + _a, -2), (6 + _a, -2), (_a, -2), (3 + _a, -2), (_a, -2)]
T_SLOTS += [(9, 1), (10, 1), (11, 1), (12, 1), (12, 1), (12, 1)]
S_SLOTS += [(12, 1), (12, 1), (12, 1), (9, 1), (10, 1), (11, 1)]
SLOT = 32
DEEP = 4 * len(T_SLOTS)
TYPES = 13


def perm_matrix(rank_row, w):
    rows = lax.broadcasted_iota(jnp.int32, (w, w), 0).astype(F32)
    return jnp.where(rows == rank_row, 1.0, 0.0).astype(BF16)


def pair_pieces(xs):
    hx, hy, hz = (split3(x) for x in xs)
    n = xs[0] * xs[0] + xs[1] * xs[1] + xs[2] * xs[2]
    parts = [hx[0], hy[0], hz[0], hx[1], hy[1], hz[1], hx[2], hy[2], hz[2]]
    return parts + list(split3(n)) + [jnp.ones_like(n)]


def slot_stack(pieces, slots, g):
    lo = g // 2 * 8
    top = lax.broadcasted_iota(jnp.int32, (8, pieces[0].shape[1]), 0) < 4
    here, there = {}, {}
    for kind, coef in slots:
        if (kind, coef) not in here:
            x = pieces[kind][lo : lo + 8]
            here[kind, coef] = x if coef == 1 else x * float(coef)
            there[kind, coef] = here[kind, coef] if kind == TYPES - 1 else pltpu.roll(here[kind, coef], 4, 0)
    first, second = (here, there) if g % 2 == 0 else (there, here)
    return jnp.concatenate(
        [jnp.where(top, first[slots[f]], second[slots[f + 1]]) for f in range(0, len(slots), 2)], 0
    )


def target_features(pieces, ft, count):
    for g in range(-(-count // 4)):
        stack = slot_stack(pieces, T_SLOTS, g)
        row = lax.broadcasted_iota(jnp.int32, stack.shape, 0) % 4
        for i in range(min(4, count - g * 4)):
            ft[g * 4 + i] = jnp.where(row == i, stack, 0.0).astype(BF16)


def source_features(pieces, fs, s, w, count):
    for g in range(-(-count // 4)):
        fs[g, s * w : (s + 1) * w, :] = jnp.transpose(slot_stack(pieces, S_SLOTS, g).astype(BF16))


def sum_select(rows, count):
    lane = lax.broadcasted_iota(jnp.int32, (1, max(count * SLOT, L)), 1)
    b, r = lane // SLOT, lane % SLOT
    p, f = r // 8, r % 8
    want = jnp.where((f < 4) & (p < 3) & (b < count), (p * 4 + f) * rows + b, -1)
    row = lax.broadcasted_iota(jnp.int32, (12 * rows, lane.shape[1]), 0)
    return jnp.where(row == want, 1.0, 0.0).astype(BF16)


def center_of(xs, count):
    w = xs[0].shape[1]
    return [jnp.sum(x[:count], keepdims=True) * (1.0 / (count * w)) for x in xs]


def columns(misc):
    al = misc[1:2]
    good = al > 0.0
    inv = jnp.where(good, lax.rsqrt(jnp.where(good, al, 1.0)), 0.0)
    return jnp.concatenate([inv, misc[2:3], jnp.zeros_like(misc[:6])], 0)


def ranges(x, al, count, w):
    good = al > 0.0
    lo = jnp.where(good, x[:count], 1e30)
    hi = jnp.where(good, x[:count], -1e30)
    out = []
    for i in range(w // L):
        out.append((jnp.min(lo[:, i * L : (i + 1) * L]), jnp.max(hi[:, i * L : (i + 1) * L])))
    return out


def near_list(lst, size, trange, sranges):
    lst[1] = 0
    lst[1 + size] = 0
    count = jnp.int32(0)
    sj = 0
    for slab in sranges:
        for smin, smax in slab:
            for ti, (tmin, tmax) in enumerate(trange):
                near = (smin - tmax < CUTOFF) & (tmin - smax < CUTOFF)
                lst[1 + count] = sj * L
                lst[1 + size + count] = ti * L
                count = count + near.astype(jnp.int32)
            sj += 1
    lst[0] = count


def own_blocks(nt):
    return [(i, i) for i in range(nt)], [(i, j) for i in range(nt) for j in range(i + 1, nt)]


def pair_basis(r2, q):
    safe = jnp.maximum(r2, 1e-4)
    inv = lax.rsqrt(safe)
    c = (safe * inv) * (safe * q)
    decay = jnp.exp2(c)
    v = jnp.maximum(CUT2 - r2, 0.0) * inv
    return c, decay, inv, v


def comps(ref, first, count=3):
    out = []
    for c in range(first, first + count):
        block = ref[c // 2 * 8 : c // 2 * 8 + 8]
        out.append(block if c % 2 == 0 else pltpu.roll(block, 4, 0))
    return out


def stack_comps(parts):
    top = lax.broadcasted_iota(jnp.int32, parts[0].shape, 0) < 4
    return jnp.concatenate(
        [jnp.where(top, parts[i], pltpu.roll(parts[i + 1], 4, 0)) for i in range(0, len(parts), 2)], 0
    )


def two(x):
    hi = x.astype(BF16)
    return hi, (x - hi.astype(F32)).astype(BF16)


def weights(nb, shape, rank, bead_dim):
    b = lax.broadcasted_iota(jnp.int32, shape, bead_dim)
    k = lax.broadcasted_iota(jnp.int32, shape, 1 - bead_dim)
    turn = k * (BEADS // CONTR) - (rank * nb + b) + 2 * BEADS
    turn = (turn + BEADS // 2) % BEADS - BEADS // 2
    cos = jnp.cos(turn.astype(F32) * (2.0 * math.pi / BEADS))
    return jnp.where((k < CONTR) & (b < nb), 2.0 * cos * (1.0 + cos), 0.0)


def hdot(a, b):
    return jnp.dot(a, b, precision=lax.Precision.HIGHEST, preferred_element_type=F32)


def pack_kernel(nb, nbp, w, pos, charge, polar, mol, out, sel, scr, posv, chargev, polarv, molv, sem):
    copies = [
        pltpu.make_async_copy(src, dst, sem.at[i])
        for i, (src, dst) in enumerate(((pos, posv), (charge, chargev), (polar, polarv), (mol, molv)))
    ]
    for c in copies:
        c.start()
    sel[...] = sum_select(nbp, nb)
    scr[...] = jnp.zeros_like(scr)
    for c in copies:
        c.wait()
    for a in range(3):
        scr[a * nbp : a * nbp + nb, :] = posv[a]
    base = 3 * nbp
    scr[base : base + 1, :] = chargev[...].reshape(1, w)
    scr[base + 1 : base + 2, :] = polarv[...].reshape(1, w)
    scr[base + 2 : base + 3, :] = molv[...].reshape(1, w).astype(F32)
    x = scr[...]
    key = jnp.sum(x[:nbp], 0, keepdims=True)
    col = jnp.transpose(jnp.broadcast_to(key, (8, w)))[:, :1]
    jj = lax.broadcasted_iota(jnp.int32, (w, w), 0)
    ii = lax.broadcasted_iota(jnp.int32, (w, w), 1)
    before = (col < key) | ((col == key) & (jj < ii))
    rank = jnp.sum(jnp.where(before, 1.0, 0.0), 0, keepdims=True)
    out[...] = dot3(x, perm_matrix(rank, w), 1)
    out[base + 3 : base + 4, :] = rank


def perm_sources(nb, nbp, w, src, pieces, xs, s, sel_r, fs, rt, cols):
    base = 3 * nbp
    misc = src[base : base + 8, :]
    source_features(pieces, fs, s, w, nb)
    q = jnp.broadcast_to(misc[0:1] * (1.0 / (CUT2 * CUT2)), xs[0].shape)
    feats = [split3(v) for v in (xs[0] * q, xs[1] * q, xs[2] * q, q)]
    stack = jnp.concatenate([feats[f][p] for p in range(3) for f in range(4)], 0)
    rt[:, s * w : (s + 1) * w] = dot(sel_r, stack.astype(BF16), 0, 0).astype(BF16)
    cols[s * w : (s + 1) * w, :] = jnp.transpose(columns(misc))
    return misc[1:2]


class Item:
    def __init__(self, e, s0, t0, g=0, sym=False):
        self.e, self.s0, self.t0, self.g, self.sym = e, s0, t0, g, sym

    def at(self, g):
        return Item(self.e, self.s0, self.t0, g, self.sym)


def perm_run(items, head, tail, nb, fs, ft, rt, qbuf, acc, r2s, fbs):
    def gather(tile, b, out):
        for p in range(3):
            row = (p * nb + b) * 8
            acc[tile, row : row + 8, :] += out[p * 8 : p * 8 + 8]

    def sums(it, f):
        for j in range(4):
            r0 = (it.g * 4 + j) * SLOT
            r = rt[r0 : r0 + SLOT, pl.ds(it.s0, L)]
            pair = f[j]
            gather(it.t0 // L, it.g * 4 + j, dot(jnp.concatenate([r, r], 1), pair))
            if it.sym:
                back = dot(rt[r0 : r0 + SLOT, pl.ds(it.t0, L)], pair, 1, 1)
                gather(it.s0 // L, it.g * 4 + j, back[:, :L] + back[:, L:])

    def functions(it, r2, f):
        for j in range(4):
            c, decay, inv, v = pair_basis(r2[j], qbuf[it.e])
            hi, lo = two((v * v) * (inv * (1.0 - decay)))
            f[j, :L, :] = hi
            f[j, L:, :] = lo

    def distances(it, r2):
        lhs = fs[it.g, pl.ds(it.s0, L), :]
        for j in range(4):
            r2[j] = dot(lhs, ft[it.g * 4 + j, :, pl.ds(it.t0, L)])

    if not items:
        if tail is not None:
            distances(tail, r2s[0])
        if head is not None:
            sums(head, fbs[1])
        return
    for i, it in enumerate(items):
        functions(it, r2s[i % 2], fbs[i % 2])
        after = items[i + 1] if i + 1 < len(items) else tail
        if after is not None:
            distances(after, r2s[(i + 1) % 2])
        before = items[i - 1] if i > 0 else head
        if before is not None:
            sums(before, fbs[(i - 1) % 2])


def perm_own_pairs(blocks, nb, *rest):
    items = [
        Item(e, s * L, t * L, g, s != t) for e, (s, t) in enumerate(blocks) for g in range(nb // 4)
    ]
    args = rest
    perm_run([], None, items[0], nb, *args)
    odd = len(items) % 2
    perm_run(items[: len(items) - odd], None, items[-1] if odd else None, nb, *args)
    if odd:
        perm_run([items[-1]], items[-2] if len(items) > 1 else None, None, nb, *args)
        fbs = args[-1]
        fbs[1][...] = fbs[0][...]
    perm_run([], items[-1], None, nb, *args)


def perm_near_pairs(n, lst, size, nb, cols, qrow, *rest):
    qbuf, fbs = rest[3], rest[-1]
    fbs[1][...] = jnp.zeros_like(fbs[1])
    groups = nb // 4

    def entry(i):
        good = i < n
        e = jnp.where(good, i, 0)
        return jnp.where(good, 1.0, 0.0), lst[1 + e], lst[1 + size + e]

    def item(e, it):
        return Item(e, pl.multiple_of(it[1], L), pl.multiple_of(it[2], L))

    def step(i, carry):
        before, first, second, after = carry
        later = (entry(2 * i + 3), entry(2 * i + 4))
        items = []
        for e, it in enumerate((first, second)):
            block = item(e, it)
            qbuf[e] = near_q(block.s0, block.t0, cols, qrow) * it[0]
            items += [block.at(g) for g in range(groups)]
        perm_run(items, item(1, before).at(groups - 1), item(0, after).at(0), nb, *rest)
        return (second, after) + later

    start = entry(0)
    perm_run([], None, item(0, start).at(0), nb, *rest)
    last = lax.fori_loop(0, (n + 1) // 2, step, (start, start, entry(1), entry(2)))[0]
    perm_run([], item(1, last).at(groups - 1), None, nb, *rest)


def own_q(s, t, cols, qrow):
    cc = cols[s * L : (s + 1) * L, :]
    row = qrow[:, t * L : (t + 1) * L]
    return jnp.where(cc[:, 1:2] == row[1:2], 0.0, cc[:, 0:1] * row[0:1])


def near_q(s0, t0, cols, qrow):
    return cols[pl.ds(s0, L), :][:, 0:1] * qrow[0:1, pl.ds(t0, L)]


def q_rows(misc, qrow):
    c = columns(misc)
    qrow[...] = c
    qrow[0:1, :] = c[0:1] * (-THOLE * LOG2E)


def perm_own_kernel(nb, nbp, w, tgt, sel, acc, ft, order, keep, fs, rt, cols, qrow, r2a, r2b, qbuf, fa, fb, lst):
    nt = w // L
    base = 3 * nbp
    sel_r = sel[...]
    acc[...] = jnp.zeros_like(acc)
    order[...] = perm_matrix(tgt[base + 3 : base + 4, :], w)
    keep[...] = tgt[...]
    coords = [tgt[a * nbp : (a + 1) * nbp, :] for a in range(3)]
    xt = [x - c for x, c in zip(coords, center_of(coords, nb))]
    pieces = pair_pieces(xt)
    target_features(pieces, ft, nb)
    perm_sources(nb, nbp, w, tgt, pieces, xt, 0, sel_r, fs, rt, cols)
    q_rows(tgt[base : base + 8, :], qrow)
    diag, off = own_blocks(nt)
    for e, (a, b) in enumerate(diag + off):
        qbuf[e] = own_q(a, b, cols, qrow)
    perm_own_pairs(diag + off, nb, fs, ft, rt, qbuf, acc, (r2a, r2b), (fa, fb))


def perm_near_kernel(
    nb, nbp, w, tgt, srca, srcb, sel, ft, acc_in, order, perm_out, msg_out, acc,
    fs, rt, cols, qrow, r2a, r2b, qbuf, fa, fb, lst,
):
    nt = w // L
    base = 3 * nbp
    coords = [tgt[a * nbp : (a + 1) * nbp, :] for a in range(3)]
    center = center_of(coords, nb)
    xt = [x - c for x, c in zip(coords, center)]
    sel_r = sel[...]
    sranges = []
    for s, src in enumerate((srca, srcb)):
        xs = [src[a * nbp : (a + 1) * nbp, :] - center[a] for a in range(3)]
        al = perm_sources(nb, nbp, w, src, pair_pieces(xs), xs, s, sel_r, fs, rt, cols)
        sranges.append(ranges(xs[0], al, nb, w))
    size = 2 * nt * nt
    near_list(lst, size, ranges(xt[0], tgt[base + 1 : base + 2, :], nb, w), sranges)
    q_rows(tgt[base : base + 8, :], qrow)
    n = lst[0]
    perm_near_pairs(n, lst, size, nb, cols, qrow, fs, ft, rt, qbuf, acc, (r2a, r2b), (fa, fb))
    if nb < nbp:
        perm_out[...] = jnp.zeros_like(perm_out)
    for i in range(nt):
        tile = slice(i * L, (i + 1) * L)
        sums = []
        for f in range(4):
            h, m, l = (acc[i, pl.ds(p * nb * 8 + f, nb, stride=8), :] for p in range(3))
            sums.append((h + m) + l)
        for a in range(3):
            perm_out[a * nbp : a * nbp + nb, tile] = xt[a][:nb, tile] * sums[3] - sums[a]
    wc = weights(nb, (KP, nbp), lax.axis_index("bead"), 1) * (1.0 / BEADS)
    parts = [hdot(wc, perm_out[a * nbp : (a + 1) * nbp, :]) for a in range(3)]
    parts += [hdot(wc, coords[a]) for a in range(3)]
    msg_out[...] = dot3(stack_comps(parts), order[...], 0)


def start_kernel(nbp, w, msg, other, order, pack, m0, cf):
    both = dot3(msg[...] + other[...], order[...], 1)
    cf[...] = both[: 2 * KP]
    row = lax.broadcasted_iota(jnp.int32, both.shape, 0)
    m0[...] = jnp.where(row < 3 * CONTR, both * pack[3 * nbp + 1 : 3 * nbp + 2, :], both)


def centered(m, center):
    return [x - c for x, c in zip(comps(m, 3), center)]


def own_center(m):
    return center_of(comps(m, 3), CONTR)


def tensor_of(e, r2, q, tensors):
    for k in range(CONTR):
        c, decay, inv, v = pair_basis(r2[k], q)
        l3 = 1.0 - decay
        l5 = l3 + (c * LN2) * decay
        w3 = (v * v) * inv
        w5 = w3 * (inv * inv)
        a_hi, a_lo = two(w5 * l5)
        b_hi, b_lo = two(w3 * l3)
        tensors[k, e, 0:L, :] = a_hi
        tensors[k, e, L : 2 * L, :] = a_lo
        tensors[k, e, 2 * L : 3 * L, :] = b_hi
        tensors[k, e, 3 * L : 4 * L, :] = b_lo


def tensor_distances(s0, t0, fs, ft, r2):
    lhs = fs[0, pl.ds(s0, L), :]
    for k in range(CONTR):
        r2[k] = dot(lhs, ft[k, :, pl.ds(t0, L)])


def own_tensors(blocks, fs, ft, cols, qrow, r2s, tensors):
    tensor_distances(blocks[0][0] * L, blocks[0][1] * L, fs, ft, r2s[0])
    for e, (s, t) in enumerate(blocks):
        if e + 1 < len(blocks):
            tensor_distances(blocks[e + 1][0] * L, blocks[e + 1][1] * L, fs, ft, r2s[(e + 1) % 2])
        tensor_of(e, r2s[e % 2], own_q(s, t, cols, qrow), tensors)


def near_tensors(n, lst, size, fs, ft, cols, qrow, r2a, r2b, tensors):
    def where_is(i):
        e = jnp.maximum(jnp.minimum(i, n - 1), 0)
        return e, pl.multiple_of(lst[1 + e], L), pl.multiple_of(lst[1 + size + e], L)

    def tensor(i, r2):
        e, s0, t0 = where_is(i)
        tensor_of(e, r2, near_q(s0, t0, cols, qrow), tensors)

    def distances(i, r2):
        _, s0, t0 = where_is(i)
        tensor_distances(s0, t0, fs, ft, r2)

    def step(p, carry):
        distances(2 * p + 1, r2b)
        tensor(2 * p, r2a)
        distances(2 * p + 2, r2a)
        tensor(2 * p + 1, r2b)
        return carry

    distances(0, r2a)
    lax.fori_loop(0, (n + 1) // 2, step, 0)


def induce_features(mu, x, le, s, w):
    scale = 1.0 / (CUT2 * CUT2)
    m = [v * scale for v in comps(mu, 0)]
    dotted = x[0] * m[0] + x[1] * m[1] + x[2] * m[2]
    feats = m + [dotted] + [x[a] * m[b] for a in range(3) for b in range(3)]
    feats += [x[a] * dotted for a in range(3)]
    nt = w // L
    for f, v in enumerate(feats):
        for p, piece in enumerate(split3(v)):
            row = (p * 16 + f) * KP
            for i in range(nt):
                le[s * nt + i, row : row + KP, :] = piece[:, i * L : (i + 1) * L]


def features_of(le, tile, k):
    first = le[tile, pl.ds(k, 48, stride=KP), :]
    second = [le[tile, pl.ds(p * 16 * KP + k, 8, stride=KP), :] for p in range(3)]
    return first.astype(BF16), jnp.concatenate(second, 0).astype(BF16)


def twice(x):
    return jnp.concatenate([x, x], 1)


def own_sums(w, mu, m0, tensors, acc_a, acc_b, le):
    nt = w // L
    induce_features(mu, centered(m0, own_center(m0)), le, 0, w)
    acc_a[...] = jnp.zeros_like(acc_a)
    acc_b[...] = jnp.zeros_like(acc_b)
    diag, off = own_blocks(nt)
    for e, (s, t) in enumerate(diag + off):
        s0, t0 = s * L, t * L
        for k in range(CONTR):
            pa, pb = tensors[k, e, 0 : 2 * L, :], tensors[k, e, 2 * L : 4 * L, :]
            a0, b0 = k * 48, k * 24
            fa, fb = features_of(le, s, k)
            acc_a[a0 : a0 + 48, t0 : t0 + L] += dot(twice(fa), pa)
            acc_b[b0 : b0 + 24, t0 : t0 + L] += dot(twice(fb), pb)
            if s != t:
                fa, fb = features_of(le, t, k)
                back = dot(fa, pa, 1, 1)
                acc_a[a0 : a0 + 48, s0 : s0 + L] += back[:, :L] + back[:, L:]
                back = dot(fb, pb, 1, 1)
                acc_b[b0 : b0 + 24, s0 : s0 + L] += back[:, :L] + back[:, L:]


def near_sums(w, mus, cps, m0, tensors, lst, acc_a, acc_b, le, ev, bring=None):
    nt = w // L
    center = own_center(m0)
    for s, (mu, cp) in enumerate(zip(mus, cps)):
        induce_features(mu, centered(cp, center), le, s, w)
    size = 2 * nt * nt
    if bring is not None:
        bring.wait()

    def add(e):
        tile = lst[1 + e] // L
        t0 = pl.multiple_of(lst[1 + size + e], L)
        for k in range(CONTR):
            a0, b0 = k * 48, k * 24
            fa, fb = features_of(le, tile, k)
            acc_a[a0 : a0 + 48, pl.ds(t0, L)] += dot(twice(fa), tensors[k, e, 0 : 2 * L, :])
            acc_b[b0 : b0 + 24, pl.ds(t0, L)] += dot(twice(fb), tensors[k, e, 2 * L : 4 * L, :])

    def both(i, carry):
        add(2 * i)
        add(2 * i + 1)
        return carry

    def single(i, carry):
        add(lst[0] - 1)
        return carry

    lax.fori_loop(0, lst[0] // 2, both, 0)
    lax.fori_loop(0, lst[0] % 2, single, 0)
    ev[...] = jnp.zeros_like(ev)
    xt = centered(m0, center)
    for k in range(CONTR):
        o = k * 48
        sa = acc_a[o : o + 16, :] + acc_a[o + 16 : o + 32, :] + acc_a[o + 32 : o + 48, :]
        o = k * 24
        sb = acc_b[o : o + 8, :] + acc_b[o + 8 : o + 16, :] + acc_b[o + 16 : o + 24, :]
        x = [v[k : k + 1] for v in xt]
        along = x[0] * sa[0:1] + x[1] * sa[1:2] + x[2] * sa[2:3] - sa[3:4]
        for a in range(3):
            cross = sum(x[b] * sa[4 + 3 * a + b : 5 + 3 * a + b] for b in range(3))
            full = x[a] * along - cross + sa[13 + a : 14 + a]
            ev[a * CONTR + k : a * CONTR + k + 1, :] = 3.0 * full - sb[a : a + 1]


def own_first_kernel(nbp, w, m0, pack, tensors, acc_a, acc_b, le, fs, ft, cols, qrow, r2a, r2b):
    misc = pack[3 * nbp : 3 * nbp + 8, :]
    pieces = pair_pieces(centered(m0, own_center(m0)))
    target_features(pieces, ft, CONTR)
    source_features(pieces, fs, 0, w, CONTR)
    cols[...] = jnp.transpose(columns(misc))
    q_rows(misc, qrow)
    diag, off = own_blocks(w // L)
    own_tensors(diag + off, fs, ft, cols, qrow, (r2a, r2b), tensors)
    own_sums(w, m0, m0, tensors, acc_a, acc_b, le)


def own_kernel(w, mu, m0, tensors, acc_a, acc_b, le):
    own_sums(w, mu, m0, tensors, acc_a, acc_b, le)


def update(pack, nbp, cf, ev):
    return pack[3 * nbp + 1 : 3 * nbp + 2, :] * (cf[...] + ev[...])


def near_first_kernel(
    nbp, w, m0, m0a, m0b, pack, packa, packb, cf, acc_a_in, acc_b_in,
    mu_out, tensors, lst_out, acc_a, acc_b, fs, ft, cols, qrow, r2a, r2b, le, ev, lst, sem,
):
    nt = w // L
    base = 3 * nbp
    center = own_center(m0)
    xt = centered(m0, center)
    target_features(pair_pieces(xt), ft, CONTR)
    sranges = []
    for s, (m, pk) in enumerate(((m0a, packa), (m0b, packb))):
        misc = pk[base : base + 8, :]
        xs = centered(m, center)
        source_features(pair_pieces(xs), fs, s, w, CONTR)
        cols[s * w : (s + 1) * w, :] = jnp.transpose(columns(misc))
        sranges.append(ranges(xs[0], misc[1:2], CONTR, w))
    misc = pack[base : base + 8, :]
    size = 2 * nt * nt
    near_list(lst, size, ranges(xt[0], misc[1:2], CONTR, w), sranges)
    leave = pltpu.make_async_copy(lst, lst_out, sem)
    q_rows(misc, qrow)
    n = lst[0]
    leave.start()
    near_tensors(n, lst, size, fs, ft, cols, qrow, r2a, r2b, tensors)
    near_sums(w, [m0a, m0b], [m0a, m0b], m0, tensors, lst, acc_a, acc_b, le, ev)
    mu_out[...] = update(pack, nbp, cf, ev)
    leave.wait()


def near_kernel(
    nbp, w, mua, mub, m0, m0a, m0b, pack, cf, acc_a_in, acc_b_in, tensors, lst_hbm, mu_out, acc_a, acc_b, le, ev, lst, sem,
):
    bring = pltpu.make_async_copy(lst_hbm, lst, sem)
    bring.start()
    near_sums(w, [mua, mub], [m0a, m0b], m0, tensors, lst, acc_a, acc_b, le, ev, bring)
    mu_out[...] = update(pack, nbp, cf, ev)


def last_own_kernel(w, mu, m0, tensors, perm, order, acc_a, acc_b, perm_out, le):
    own_sums(w, mu, m0, tensors, acc_a, acc_b, le)
    perm_out[...] = dot3(perm[...], order[...], 0)


def final_kernel(
    nb, nbp, w, mua, mub, m0, m0a, m0b, mu, perm, order, acc_a_in, acc_b_in, tensors, lst_hbm,
    total_out, dip_out, acc_a, acc_b, le, ev, lst, sem,
):
    bring = pltpu.make_async_copy(lst_hbm, lst, sem)
    bring.start()
    near_sums(w, [mua, mub], [m0a, m0b], m0, tensors, lst, acc_a, acc_b, le, ev, bring)
    out = dot3(jnp.concatenate([ev[...], mu[...]], 0), order[...], 0)
    us = weights(nb, (nbp, KP), lax.axis_index("bead"), 0) * (1.0 / CONTR)
    for a, v in enumerate(comps(out, 0)):
        total_out[a] = (perm[a * nbp : (a + 1) * nbp, :] + hdot(us, v))[:nb]
        d0 = 2 * KP + a * CONTR
        dip_out[a] = out[d0 : d0 + CONTR]


def swap_pairs(count, first):
    pairs = []
    for i in range(first, count - 1, 2):
        pairs += [(i, i + 1), (i + 1, i)]
    return pairs


def call(kernel, outs, name, scratch, args, any_in=(), any_out=(), hbm_in=(), alias=None):
    vmem = pl.BlockSpec(memory_space=pltpu.VMEM)
    hbm = pl.BlockSpec(memory_space=pltpu.HBM)
    return pl.pallas_call(
        kernel,
        out_shape=[jax.ShapeDtypeStruct(s, d) for s, d in outs],
        in_specs=[pl.BlockSpec(memory_space=pl.ANY) if i in any_in else hbm if i in hbm_in else vmem for i in range(len(args))],
        out_specs=[pl.BlockSpec(memory_space=pl.ANY) if i in any_out else vmem for i in range(len(outs))],
        scratch_shapes=list(scratch),
        input_output_aliases=alias or {},
        compiler_params=pltpu.CompilerParams(vmem_limit_bytes=VMEM_LIMIT),
        name=name,
    )(*args)


def body(positions, charges, polar, molecule):
    nb, _, w = positions.shape
    nbp = -(-nb // 16) * 16
    nt = w // L
    nbead = lax.axis_size("bead")
    nspace = lax.axis_size("space")
    rows = 3 * nbp + 8
    own_size = nt * (nt + 1) // 2
    near_size = 2 * nt * nt
    part = functools.partial

    def exchange(x):
        near = lax.ppermute(x, "space", swap_pairs(nspace, 0))
        far = lax.ppermute(x, "space", swap_pairs(nspace, 1))
        return near, far

    raw = (jnp.transpose(positions, (1, 0, 2)), charges, polar, molecule)
    pack, sel = call(
        part(pack_kernel, nb, nbp, w), [((rows, w), F32), ((12 * nbp, max(nb * SLOT, L)), BF16)], "pack",
        [
            pltpu.VMEM((rows, w), F32),
            pltpu.VMEM((3, nb, w), F32),
            pltpu.VMEM((w,), F32),
            pltpu.VMEM((w,), F32),
            pltpu.VMEM((w,), jnp.int32),
            pltpu.SemaphoreType.DMA((4,)),
        ],
        tuple(pltpu.with_memory_space_constraint(v, pltpu.HBM) for v in raw), hbm_in=(0, 1, 2, 3),
    )
    packa, packb = exchange(pack)

    def pair_scratch(nsrc):
        return [
            pltpu.VMEM((nsrc * w, 8), F32),
            pltpu.VMEM((8, w), F32),
            pltpu.VMEM((4, L, L), F32),
            pltpu.VMEM((4, L, L), F32),
        ]

    def perm_scratch(nsrc, blocks):
        return [
            pltpu.VMEM((-(-nb // 4), nsrc * w, DEEP), BF16),
            pltpu.VMEM((nb * SLOT, nsrc * w), BF16),
            *pair_scratch(nsrc),
            pltpu.VMEM((max(own_size, 2), L, L), F32),
            pltpu.VMEM((4, 2 * L, L), BF16),
            pltpu.VMEM((4, 2 * L, L), BF16),
            pltpu.SMEM((2 + 2 * blocks,), jnp.int32),
        ]

    acc, ft, order, pack = call(
        part(perm_own_kernel, nb, nbp, w),
        [((nt, nb * 24, L), F32), ((nb, DEEP, w), BF16), ((w, w), BF16), ((rows, w), F32)], "perm_own",
        perm_scratch(1, own_size), (pack, sel),
    )
    perm, msg, _ = call(
        part(perm_near_kernel, nb, nbp, w), [((3 * nbp, w), F32), ((6 * CONTR, w), F32), ((nt, nb * 24, L), F32)],
        "perm_near", perm_scratch(2, near_size), (pack, packa, packb, sel, ft, acc, order), alias={5: 2},
    )

    if nbead == 2:
        other = lax.ppermute(msg, "bead", [(0, 1), (1, 0)])
    else:
        other = lax.psum(msg, "bead") - msg
    m0, cf = call(
        part(start_kernel, nbp, w), [((6 * CONTR, w), F32), ((2 * KP, w), F32)], "start", [], (msg, other, order, pack),
    )
    m0a, m0b = exchange(m0)

    def tensor_scratch(nsrc):
        return [
            pltpu.VMEM((1, nsrc * w, DEEP), BF16),
            pltpu.VMEM((CONTR, DEEP, w), BF16),
            *pair_scratch(nsrc),
        ]

    accs = [((CONTR * 48, w), F32), ((CONTR * 24, w), F32)]
    near_scratch = [pltpu.VMEM((2 * nt, 48 * KP, L), F32), pltpu.VMEM((2 * KP, w), F32)]
    list_scratch = [pltpu.SMEM((2 + 2 * near_size,), jnp.int32), pltpu.SemaphoreType.DMA]
    own_scratch = [pltpu.VMEM((nt, 48 * KP, L), F32)]
    t_own, acc_a, acc_b = call(
        part(own_first_kernel, nbp, w), [((CONTR, own_size, 4 * L, L), BF16)] + accs, "own_0",
        own_scratch + tensor_scratch(1),
        (m0, pack),
    )
    mu, t_nbr, lst, _, _ = call(
        part(near_first_kernel, nbp, w),
        [((2 * KP, w), F32), ((CONTR, near_size, 4 * L, L), BF16), ((2 + 2 * near_size,), jnp.int32)] + accs, "near_0",
        tensor_scratch(2) + near_scratch + list_scratch,
        (m0, m0a, m0b, pack, packa, packb, cf, acc_a, acc_b), any_out=(2,), alias={7: 3, 8: 4},
    )
    for step in range(1, ITERS):
        mua, mub = exchange(mu)
        acc_a, acc_b = call(part(own_kernel, w), accs, f"own_{step}", own_scratch, (mu, m0, t_own))
        mu, _, _ = call(
            part(near_kernel, nbp, w), [((2 * KP, w), F32)] + accs, f"near_{step}", near_scratch + list_scratch,
            (mua, mub, m0, m0a, m0b, pack, cf, acc_a, acc_b, t_nbr, lst), any_in=(10,), alias={7: 1, 8: 2},
        )
    mua, mub = exchange(mu)
    acc_a, acc_b, perm = call(
        part(last_own_kernel, w), accs + [((3 * nbp, w), F32)], "own_last", own_scratch,
        (mu, m0, t_own, perm, order),
    )
    total, dipoles, _, _ = call(
        part(final_kernel, nb, nbp, w), [((3, nb, w), F32), ((3, CONTR, w), F32)] + accs, "final",
        near_scratch + list_scratch,
        (mua, mub, m0, m0a, m0b, mu, perm, order, acc_a, acc_b, t_nbr, lst), any_in=(11,), alias={8: 2, 9: 3},
    )
    return (jnp.transpose(total, (1, 0, 2)), jnp.transpose(dipoles, (1, 0, 2)))


def solution(mesh):
    in_specs = (P("bead", None, "space"), P("space"), P("space"), P("space"))
    out_specs = (P("bead", None, "space"), P(None, None, "space"))
    return jax.shard_map(body, mesh=mesh, in_specs=in_specs, out_specs=out_specs, check_vma=False)
```

```python
import functools
import math

import jax
import jax.numpy as jnp
from jax import lax
from jax.experimental import pallas as pl
from jax.experimental.pallas import tpu as pltpu
from jax.sharding import PartitionSpec as P

BEADS = 32
CONTR = 4
ITERS = 2
CUTOFF = 9.0
CUT2 = CUTOFF * CUTOFF
THOLE = 0.39
LOG2E = 1.4426950408889634
LN2 = 0.6931471805599453
L = 128
KP = 8
F32 = jnp.float32
BF16 = jnp.bfloat16
VMEM_LIMIT = 20 * 1024 * 1024


def split3(x):
    h = x.astype(BF16).astype(F32)
    r = x - h
    m = r.astype(BF16).astype(F32)
    return h, m, r - m


def dot(a, b, ca=1, cb=0):
    return lax.dot_general(a, b, (((ca,), (cb,)), ((), ())), preferred_element_type=F32)


def dot3(x, mat, cb):
    rows = x.shape[0]
    out = dot(jnp.concatenate(split3(x), 0).astype(BF16), mat, 1, cb)
    return (out[:rows] + out[rows : 2 * rows]) + out[2 * rows :]


T_SLOTS, S_SLOTS = [], []
for _a in range(3):
    T_SLOTS += [(_a, 1)] * 3 + [(3 + _a, 1)] * 2 + [(6 + _a, 1)]
    S_SLOTS += [(_a, -2), (3 + _a, -2), (6 + _a, -2), (_a, -2), (3 + _a, -2), (_a, -2)]
T_SLOTS += [(9, 1), (10, 1), (11, 1), (12, 1), (12, 1), (12, 1)]
S_SLOTS += [(12, 1), (12, 1), (12, 1), (9, 1), (10, 1), (11, 1)]
SLOT = 32
DEEP = 4 * len(T_SLOTS)
TYPES = 13


def perm_matrix(rank_row, w):
    rows = lax.broadcasted_iota(jnp.int32, (w, w), 0).astype(F32)
    return jnp.where(rows == rank_row, 1.0, 0.0).astype(BF16)


def pair_pieces(xs):
    hx, hy, hz = (split3(x) for x in xs)
    n = xs[0] * xs[0] + xs[1] * xs[1] + xs[2] * xs[2]
    parts = [hx[0], hy[0], hz[0], hx[1], hy[1], hz[1], hx[2], hy[2], hz[2]]
    return parts + list(split3(n)) + [jnp.ones_like(n)]


def slot_stack(pieces, slots, g):
    lo = g // 2 * 8
    top = lax.broadcasted_iota(jnp.int32, (8, pieces[0].shape[1]), 0) < 4
    here, there = {}, {}
    for kind, coef in slots:
        if (kind, coef) not in here:
            x = pieces[kind][lo : lo + 8]
            here[kind, coef] = x if coef == 1 else x * float(coef)
            there[kind, coef] = here[kind, coef] if kind == TYPES - 1 else pltpu.roll(here[kind, coef], 4, 0)
    first, second = (here, there) if g % 2 == 0 else (there, here)
    return jnp.concatenate(
        [jnp.where(top, first[slots[f]], second[slots[f + 1]]) for f in range(0, len(slots), 2)], 0
    )


def target_features(pieces, ft, count):
    for g in range(-(-count // 4)):
        stack = slot_stack(pieces, T_SLOTS, g)
        stack = stack.astype(BF16)
        row = lax.broadcasted_iota(jnp.int32, stack.shape, 0) % 4
        for i in range(min(4, count - g * 4)):
            ft[g * 4 + i] = stack * jnp.where(row == i, 1.0, 0.0).astype(BF16)


def source_features(pieces, fs, s, w, count):
    for g in range(-(-count // 4)):
        fs[g, s * w : (s + 1) * w, :] = jnp.transpose(slot_stack(pieces, S_SLOTS, g).astype(BF16))


def sum_select(rows, count):
    lane = lax.broadcasted_iota(jnp.int32, (1, max(count * SLOT, L)), 1)
    b, r = lane // SLOT, lane % SLOT
    p, f = r // 8, r % 8
    want = jnp.where((f < 4) & (p < 3) & (b < count), (p * 4 + f) * rows + b, -1)
    row = lax.broadcasted_iota(jnp.int32, (12 * rows, lane.shape[1]), 0)
    return jnp.where(row == want, 1.0, 0.0).astype(BF16)


def center_of(xs, count):
    w = xs[0].shape[1]
    return [jnp.sum(x[:count], keepdims=True) * (1.0 / (count * w)) for x in xs]


def columns(misc):
    al = misc[1:2]
    good = al > 0.0
    inv = jnp.where(good, lax.rsqrt(jnp.where(good, al, 1.0)), 0.0)
    return jnp.concatenate([inv, misc[2:3], jnp.zeros_like(misc[:6])], 0)


def ranges(x, al, count, w):
    good = al > 0.0
    lo = jnp.where(good, x[:count], 1e30)
    hi = jnp.where(good, x[:count], -1e30)
    out = []
    for i in range(w // L):
        out.append((jnp.min(lo[:, i * L : (i + 1) * L]), jnp.max(hi[:, i * L : (i + 1) * L])))
    return out


def near_list(lst, size, trange, sranges):
    lst[1] = 0
    lst[1 + size] = 0
    count = jnp.int32(0)
    sj = 0
    for slab in sranges:
        for smin, smax in slab:
            for ti, (tmin, tmax) in enumerate(trange):
                near = (smin - tmax < CUTOFF) & (tmin - smax < CUTOFF)
                lst[1 + count] = sj * L
                lst[1 + size + count] = ti * L
                count = count + near.astype(jnp.int32)
            sj += 1
    lst[0] = count


def own_blocks(nt):
    return [(i, i) for i in range(nt)], [(i, j) for i in range(nt) for j in range(i + 1, nt)]


def pair_basis(r2, q):
    safe = jnp.maximum(r2, 1e-4)
    inv = lax.rsqrt(safe)
    c = (safe * inv) * (safe * q)
    decay = jnp.exp2(c)
    v = jnp.maximum(CUT2 - r2, 0.0) * inv
    return c, decay, inv, v


def comps(ref, first, count=3):
    out = []
    for c in range(first, first + count):
        block = ref[c // 2 * 8 : c // 2 * 8 + 8]
        out.append(block if c % 2 == 0 else pltpu.roll(block, 4, 0))
    return out


def stack_comps(parts):
    top = lax.broadcasted_iota(jnp.int32, parts[0].shape, 0) < 4
    return jnp.concatenate(
        [jnp.where(top, parts[i], pltpu.roll(parts[i + 1], 4, 0)) for i in range(0, len(parts), 2)], 0
    )


def two(x):
    hi = x.astype(BF16)
    return hi, (x - hi.astype(F32)).astype(BF16)


def weights(nb, shape, rank, bead_dim):
    b = lax.broadcasted_iota(jnp.int32, shape, bead_dim)
    k = lax.broadcasted_iota(jnp.int32, shape, 1 - bead_dim)
    turn = k * (BEADS // CONTR) - (rank * nb + b) + 2 * BEADS
    turn = (turn + BEADS // 2) % BEADS - BEADS // 2
    cos = jnp.cos(turn.astype(F32) * (2.0 * math.pi / BEADS))
    return jnp.where((k < CONTR) & (b < nb), 2.0 * cos * (1.0 + cos), 0.0)


def hdot(a, b):
    return jnp.dot(a, b, precision=lax.Precision.HIGHEST, preferred_element_type=F32)


def pack_kernel(nb, nbp, w, pos, charge, polar, mol, out, sel, scr, posv, chargev, polarv, molv, sem):
    copies = [
        pltpu.make_async_copy(src, dst, sem.at[i])
        for i, (src, dst) in enumerate(((pos, posv), (charge, chargev), (polar, polarv), (mol, molv)))
    ]
    for c in copies:
        c.start()
    sel[...] = sum_select(nbp, nb)
    scr[...] = jnp.zeros_like(scr)
    for c in copies:
        c.wait()
    for a in range(3):
        scr[a * nbp : a * nbp + nb, :] = posv[a]
    base = 3 * nbp
    scr[base : base + 1, :] = chargev[...].reshape(1, w)
    scr[base + 1 : base + 2, :] = polarv[...].reshape(1, w)
    scr[base + 2 : base + 3, :] = molv[...].reshape(1, w).astype(F32)
    x = scr[...]
    key = jnp.sum(x[:nbp], 0, keepdims=True)
    col = jnp.transpose(jnp.broadcast_to(key, (8, w)))[:, :1]
    jj = lax.broadcasted_iota(jnp.int32, (w, w), 0)
    ii = lax.broadcasted_iota(jnp.int32, (w, w), 1)
    before = (col < key) | ((col == key) & (jj < ii))
    rank = jnp.sum(jnp.where(before, 1.0, 0.0), 0, keepdims=True)
    out[...] = dot3(x, perm_matrix(rank, w), 1)
    out[base + 3 : base + 4, :] = rank


def perm_sources(nb, nbp, w, src, pieces, xs, s, sel_r, fs, rt, cols):
    base = 3 * nbp
    misc = src[base : base + 8, :]
    source_features(pieces, fs, s, w, nb)
    q = jnp.broadcast_to(misc[0:1] * (1.0 / (CUT2 * CUT2)), xs[0].shape)
    feats = [split3(v) for v in (xs[0] * q, xs[1] * q, xs[2] * q, q)]
    stack = jnp.concatenate([feats[f][p] for p in range(3) for f in range(4)], 0)
    rt[:, s * w : (s + 1) * w] = dot(sel_r, stack.astype(BF16), 0, 0).astype(BF16)
    cols[s * w : (s + 1) * w, :] = jnp.transpose(columns(misc))
    return misc[1:2]


class Item:
    def __init__(self, e, s0, t0, g=0, sym=False):
        self.e, self.s0, self.t0, self.g, self.sym = e, s0, t0, g, sym

    def at(self, g):
        return Item(self.e, self.s0, self.t0, g, self.sym)


def perm_run(items, head, tail, nb, fs, ft, rt, qbuf, acc, r2s, fbs):
    def gather(tile, b, out):
        for p in range(3):
            row = (p * nb + b) * 8
            acc[tile, row : row + 8, :] += out[p * 8 : p * 8 + 8]

    def sums(it, f):
        for j in range(4):
            r0 = (it.g * 4 + j) * SLOT
            r = rt[r0 : r0 + SLOT, pl.ds(it.s0, L)]
            pair = f[j]
            gather(it.t0 // L, it.g * 4 + j, dot(jnp.concatenate([r, r], 1), pair))
            if it.sym:
                back = dot(rt[r0 : r0 + SLOT, pl.ds(it.t0, L)], pair, 1, 1)
                gather(it.s0 // L, it.g * 4 + j, back[:, :L] + back[:, L:])

    def functions(it, r2, f):
        for j in range(4):
            c, decay, inv, v = pair_basis(r2[j], qbuf[it.e])
            hi, lo = two((v * v) * (inv * (1.0 - decay)))
            f[j, :L, :] = hi
            f[j, L:, :] = lo

    def distances(it, r2):
        lhs = fs[it.g, pl.ds(it.s0, L), :]
        for j in range(4):
            r2[j] = dot(lhs, ft[it.g * 4 + j, :, pl.ds(it.t0, L)])

    if not items:
        if tail is not None:
            distances(tail, r2s[0])
        if head is not None:
            sums(head, fbs[1])
        return
    for i, it in enumerate(items):
        functions(it, r2s[i % 2], fbs[i % 2])
        after = items[i + 1] if i + 1 < len(items) else tail
        if after is not None:
            distances(after, r2s[(i + 1) % 2])
        before = items[i - 1] if i > 0 else head
        if before is not None:
            sums(before, fbs[(i - 1) % 2])


def perm_own_pairs(blocks, nb, *rest):
    items = [
        Item(e, s * L, t * L, g, s != t) for e, (s, t) in enumerate(blocks) for g in range(nb // 4)
    ]
    args = rest
    perm_run([], None, items[0], nb, *args)
    odd = len(items) % 2
    perm_run(items[: len(items) - odd], None, items[-1] if odd else None, nb, *args)
    if odd:
        perm_run([items[-1]], items[-2] if len(items) > 1 else None, None, nb, *args)
        fbs = args[-1]
        fbs[1][...] = fbs[0][...]
    perm_run([], items[-1], None, nb, *args)


def perm_near_pairs(n, lst, size, nb, cols, qrow, *rest):
    qbuf, fbs = rest[3], rest[-1]
    fbs[1][...] = jnp.zeros_like(fbs[1])
    groups = nb // 4

    def entry(i):
        good = i < n
        e = jnp.where(good, i, 0)
        return jnp.where(good, 1.0, 0.0), lst[1 + e], lst[1 + size + e]

    def item(e, it):
        return Item(e, pl.multiple_of(it[1], L), pl.multiple_of(it[2], L))

    def step(i, carry):
        before, first, second, after = carry
        later = (entry(2 * i + 3), entry(2 * i + 4))
        items = []
        for e, it in enumerate((first, second)):
            block = item(e, it)
            qbuf[e] = near_q(block.s0, block.t0, cols, qrow) * it[0]
            items += [block.at(g) for g in range(groups)]
        perm_run(items, item(1, before).at(groups - 1), item(0, after).at(0), nb, *rest)
        return (second, after) + later

    start = entry(0)
    perm_run([], None, item(0, start).at(0), nb, *rest)
    last = lax.fori_loop(0, (n + 1) // 2, step, (start, start, entry(1), entry(2)))[0]
    perm_run([], item(1, last).at(groups - 1), None, nb, *rest)


def own_q(s, t, cols, qrow):
    cc = cols[s * L : (s + 1) * L, :]
    row = qrow[:, t * L : (t + 1) * L]
    return jnp.where(cc[:, 1:2] == row[1:2], 0.0, cc[:, 0:1] * row[0:1])


def near_q(s0, t0, cols, qrow):
    return cols[pl.ds(s0, L), :][:, 0:1] * qrow[0:1, pl.ds(t0, L)]


def q_rows(misc, qrow):
    c = columns(misc)
    qrow[...] = c
    qrow[0:1, :] = c[0:1] * (-THOLE * LOG2E)


def perm_own_kernel(nb, nbp, w, tgt, sel, acc, ft, order, keep, fs, rt, cols, qrow, r2a, r2b, qbuf, fa, fb, lst):
    nt = w // L
    base = 3 * nbp
    sel_r = sel[...]
    acc[...] = jnp.zeros_like(acc)
    order[...] = perm_matrix(tgt[base + 3 : base + 4, :], w)
    keep[...] = tgt[...]
    coords = [tgt[a * nbp : (a + 1) * nbp, :] for a in range(3)]
    xt = [x - c for x, c in zip(coords, center_of(coords, nb))]
    pieces = pair_pieces(xt)
    target_features(pieces, ft, nb)
    perm_sources(nb, nbp, w, tgt, pieces, xt, 0, sel_r, fs, rt, cols)
    q_rows(tgt[base : base + 8, :], qrow)
    diag, off = own_blocks(nt)
    for e, (a, b) in enumerate(diag + off):
        qbuf[e] = own_q(a, b, cols, qrow)
    perm_own_pairs(diag + off, nb, fs, ft, rt, qbuf, acc, (r2a, r2b), (fa, fb))


def perm_near_kernel(
    nb, nbp, w, tgt, srca, srcb, sel, ft, acc_in, order, perm_out, msg_out, acc,
    fs, rt, cols, qrow, r2a, r2b, qbuf, fa, fb, lst,
):
    nt = w // L
    base = 3 * nbp
    coords = [tgt[a * nbp : (a + 1) * nbp, :] for a in range(3)]
    center = center_of(coords, nb)
    xt = [x - c for x, c in zip(coords, center)]
    sel_r = sel[...]
    sranges = []
    for s, src in enumerate((srca, srcb)):
        xs = [src[a * nbp : (a + 1) * nbp, :] - center[a] for a in range(3)]
        al = perm_sources(nb, nbp, w, src, pair_pieces(xs), xs, s, sel_r, fs, rt, cols)
        sranges.append(ranges(xs[0], al, nb, w))
    size = 2 * nt * nt
    near_list(lst, size, ranges(xt[0], tgt[base + 1 : base + 2, :], nb, w), sranges)
    q_rows(tgt[base : base + 8, :], qrow)
    n = lst[0]
    perm_near_pairs(n, lst, size, nb, cols, qrow, fs, ft, rt, qbuf, acc, (r2a, r2b), (fa, fb))
    if nb < nbp:
        perm_out[...] = jnp.zeros_like(perm_out)
    for i in range(nt):
        tile = slice(i * L, (i + 1) * L)
        sums = []
        for f in range(4):
            h, m, l = (acc[i, pl.ds(p * nb * 8 + f, nb, stride=8), :] for p in range(3))
            sums.append((h + m) + l)
        for a in range(3):
            perm_out[a * nbp : a * nbp + nb, tile] = xt[a][:nb, tile] * sums[3] - sums[a]
    wc = weights(nb, (KP, nbp), lax.axis_index("bead"), 1) * (1.0 / BEADS)
    parts = [hdot(wc, perm_out[a * nbp : (a + 1) * nbp, :]) for a in range(3)]
    parts += [hdot(wc, coords[a]) for a in range(3)]
    msg_out[...] = dot3(stack_comps(parts), order[...], 0)


def start_kernel(nbp, w, msg, other, order, pack, m0, cf):
    both = dot3(msg[...] + other[...], order[...], 1)
    cf[...] = both[: 2 * KP]
    row = lax.broadcasted_iota(jnp.int32, both.shape, 0)
    m0[...] = jnp.where(row < 3 * CONTR, both * pack[3 * nbp + 1 : 3 * nbp + 2, :], both)


def centered(m, center):
    return [x - c for x, c in zip(comps(m, 3), center)]


def own_center(m):
    return center_of(comps(m, 3), CONTR)


def tensor_of(e, r2, q, tensors):
    for k in range(CONTR):
        c, decay, inv, v = pair_basis(r2[k], q)
        l3 = 1.0 - decay
        l5 = l3 + (c * LN2) * decay
        w3 = (v * v) * inv
        w5 = w3 * (inv * inv)
        a_hi, a_lo = two(w5 * l5)
        b_hi, b_lo = two(w3 * l3)
        tensors[k, e, 0:L, :] = a_hi
        tensors[k, e, L : 2 * L, :] = a_lo
        tensors[k, e, 2 * L : 3 * L, :] = b_hi
        tensors[k, e, 3 * L : 4 * L, :] = b_lo


def tensor_distances(s0, t0, fs, ft, r2):
    lhs = fs[0, pl.ds(s0, L), :]
    for k in range(CONTR):
        r2[k] = dot(lhs, ft[k, :, pl.ds(t0, L)])


def own_tensors(blocks, fs, ft, cols, qrow, r2s, tensors):
    tensor_distances(blocks[0][0] * L, blocks[0][1] * L, fs, ft, r2s[0])
    for e, (s, t) in enumerate(blocks):
        if e + 1 < len(blocks):
            tensor_distances(blocks[e + 1][0] * L, blocks[e + 1][1] * L, fs, ft, r2s[(e + 1) % 2])
        tensor_of(e, r2s[e % 2], own_q(s, t, cols, qrow), tensors)


def near_tensors(n, lst, size, fs, ft, cols, qrow, r2a, r2b, tensors):
    def where_is(i):
        e = jnp.maximum(jnp.minimum(i, n - 1), 0)
        return e, pl.multiple_of(lst[1 + e], L), pl.multiple_of(lst[1 + size + e], L)

    def tensor(i, r2):
        e, s0, t0 = where_is(i)
        tensor_of(e, r2, near_q(s0, t0, cols, qrow), tensors)

    def distances(i, r2):
        _, s0, t0 = where_is(i)
        tensor_distances(s0, t0, fs, ft, r2)

    def step(p, carry):
        distances(2 * p + 1, r2b)
        tensor(2 * p, r2a)
        distances(2 * p + 2, r2a)
        tensor(2 * p + 1, r2b)
        return carry

    distances(0, r2a)
    lax.fori_loop(0, (n + 1) // 2, step, 0)


def induce_features(mu, x, le, s, w):
    scale = 1.0 / (CUT2 * CUT2)
    m = [v * scale for v in comps(mu, 0)]
    dotted = x[0] * m[0] + x[1] * m[1] + x[2] * m[2]
    feats = m + [dotted] + [x[a] * m[b] for a in range(3) for b in range(3)]
    feats += [x[a] * dotted for a in range(3)]
    nt = w // L
    for f, v in enumerate(feats):
        for p, piece in enumerate(split3(v)):
            row = (p * 16 + f) * KP
            for i in range(nt):
                le[s * nt + i, row : row + KP, :] = piece[:, i * L : (i + 1) * L]


def features_of(le, tile, k):
    first = le[tile, pl.ds(k, 48, stride=KP), :]
    second = [le[tile, pl.ds(p * 16 * KP + k, 8, stride=KP), :] for p in range(3)]
    return first.astype(BF16), jnp.concatenate(second, 0).astype(BF16)


def twice(x):
    return jnp.concatenate([x, x], 1)


def own_sums(w, mu, m0, tensors, acc_a, acc_b, le):
    nt = w // L
    induce_features(mu, centered(m0, own_center(m0)), le, 0, w)
    acc_a[...] = jnp.zeros_like(acc_a)
    acc_b[...] = jnp.zeros_like(acc_b)
    diag, off = own_blocks(nt)
    for e, (s, t) in enumerate(diag + off):
        s0, t0 = s * L, t * L
        for k in range(CONTR):
            pa, pb = tensors[k, e, 0 : 2 * L, :], tensors[k, e, 2 * L : 4 * L, :]
            a0, b0 = k * 48, k * 24
            fa, fb = features_of(le, s, k)
            acc_a[a0 : a0 + 48, t0 : t0 + L] += dot(twice(fa), pa)
            acc_b[b0 : b0 + 24, t0 : t0 + L] += dot(twice(fb), pb)
            if s != t:
                fa, fb = features_of(le, t, k)
                back = dot(fa, pa, 1, 1)
                acc_a[a0 : a0 + 48, s0 : s0 + L] += back[:, :L] + back[:, L:]
                back = dot(fb, pb, 1, 1)
                acc_b[b0 : b0 + 24, s0 : s0 + L] += back[:, :L] + back[:, L:]


def near_sums(w, mus, cps, m0, tensors, lst, acc_a, acc_b, le, ev, bring=None):
    nt = w // L
    center = own_center(m0)
    for s, (mu, cp) in enumerate(zip(mus, cps)):
        induce_features(mu, centered(cp, center), le, s, w)
    size = 2 * nt * nt
    if bring is not None:
        bring.wait()

    def add(e):
        tile = lst[1 + e] // L
        t0 = pl.multiple_of(lst[1 + size + e], L)
        for k in range(CONTR):
            a0, b0 = k * 48, k * 24
            fa, fb = features_of(le, tile, k)
            acc_a[a0 : a0 + 48, pl.ds(t0, L)] += dot(twice(fa), tensors[k, e, 0 : 2 * L, :])
            acc_b[b0 : b0 + 24, pl.ds(t0, L)] += dot(twice(fb), tensors[k, e, 2 * L : 4 * L, :])

    def three(i, carry):
        for j in range(3):
            add(3 * i + j)
        return carry

    def single(i, carry):
        add(lst[0] // 3 * 3 + i)
        return carry

    lax.fori_loop(0, lst[0] // 3, three, 0)
    lax.fori_loop(0, lst[0] % 3, single, 0)
    ev[...] = jnp.zeros_like(ev)
    xt = centered(m0, center)
    for k in range(CONTR):
        o = k * 48
        sa = acc_a[o : o + 16, :] + acc_a[o + 16 : o + 32, :] + acc_a[o + 32 : o + 48, :]
        o = k * 24
        sb = acc_b[o : o + 8, :] + acc_b[o + 8 : o + 16, :] + acc_b[o + 16 : o + 24, :]
        x = [v[k : k + 1] for v in xt]
        along = x[0] * sa[0:1] + x[1] * sa[1:2] + x[2] * sa[2:3] - sa[3:4]
        for a in range(3):
            cross = sum(x[b] * sa[4 + 3 * a + b : 5 + 3 * a + b] for b in range(3))
            full = x[a] * along - cross + sa[13 + a : 14 + a]
            ev[a * CONTR + k : a * CONTR + k + 1, :] = 3.0 * full - sb[a : a + 1]


def own_first_kernel(nbp, w, m0, pack, tensors, acc_a, acc_b, le, fs, ft, cols, qrow, r2a, r2b):
    misc = pack[3 * nbp : 3 * nbp + 8, :]
    pieces = pair_pieces(centered(m0, own_center(m0)))
    target_features(pieces, ft, CONTR)
    source_features(pieces, fs, 0, w, CONTR)
    cols[...] = jnp.transpose(columns(misc))
    q_rows(misc, qrow)
    diag, off = own_blocks(w // L)
    own_tensors(diag + off, fs, ft, cols, qrow, (r2a, r2b), tensors)
    own_sums(w, m0, m0, tensors, acc_a, acc_b, le)


def own_kernel(w, mu, m0, tensors, acc_a, acc_b, le):
    own_sums(w, mu, m0, tensors, acc_a, acc_b, le)


def update(pack, nbp, cf, ev):
    return pack[3 * nbp + 1 : 3 * nbp + 2, :] * (cf[...] + ev[...])


def near_first_kernel(
    nbp, w, m0, m0a, m0b, pack, packa, packb, cf, acc_a_in, acc_b_in,
    mu_out, tensors, lst_out, acc_a, acc_b, fs, ft, cols, qrow, r2a, r2b, le, ev, lst, sem,
):
    nt = w // L
    base = 3 * nbp
    center = own_center(m0)
    xt = centered(m0, center)
    target_features(pair_pieces(xt), ft, CONTR)
    sranges = []
    for s, (m, pk) in enumerate(((m0a, packa), (m0b, packb))):
        misc = pk[base : base + 8, :]
        xs = centered(m, center)
        source_features(pair_pieces(xs), fs, s, w, CONTR)
        cols[s * w : (s + 1) * w, :] = jnp.transpose(columns(misc))
        sranges.append(ranges(xs[0], misc[1:2], CONTR, w))
    misc = pack[base : base + 8, :]
    size = 2 * nt * nt
    near_list(lst, size, ranges(xt[0], misc[1:2], CONTR, w), sranges)
    leave = pltpu.make_async_copy(lst, lst_out, sem)
    q_rows(misc, qrow)
    n = lst[0]
    leave.start()
    near_tensors(n, lst, size, fs, ft, cols, qrow, r2a, r2b, tensors)
    near_sums(w, [m0a, m0b], [m0a, m0b], m0, tensors, lst, acc_a, acc_b, le, ev)
    mu_out[...] = update(pack, nbp, cf, ev)
    leave.wait()


def near_kernel(
    nbp, w, mua, mub, m0, m0a, m0b, pack, cf, acc_a_in, acc_b_in, tensors, lst_hbm, mu_out, acc_a, acc_b, le, ev, lst, sem,
):
    bring = pltpu.make_async_copy(lst_hbm, lst, sem)
    bring.start()
    near_sums(w, [mua, mub], [m0a, m0b], m0, tensors, lst, acc_a, acc_b, le, ev, bring)
    mu_out[...] = update(pack, nbp, cf, ev)


def last_own_kernel(w, mu, m0, tensors, perm, order, acc_a, acc_b, perm_out, le):
    own_sums(w, mu, m0, tensors, acc_a, acc_b, le)
    perm_out[...] = dot3(perm[...], order[...], 0)


def final_kernel(
    nb, nbp, w, mua, mub, m0, m0a, m0b, mu, perm, order, acc_a_in, acc_b_in, tensors, lst_hbm,
    total_out, dip_out, acc_a, acc_b, le, ev, lst, sem,
):
    bring = pltpu.make_async_copy(lst_hbm, lst, sem)
    bring.start()
    near_sums(w, [mua, mub], [m0a, m0b], m0, tensors, lst, acc_a, acc_b, le, ev, bring)
    out = dot3(jnp.concatenate([ev[...], mu[...]], 0), order[...], 0)
    us = weights(nb, (nbp, KP), lax.axis_index("bead"), 0) * (1.0 / CONTR)
    for a, v in enumerate(comps(out, 0)):
        total_out[a] = (perm[a * nbp : (a + 1) * nbp, :] + hdot(us, v))[:nb]
        d0 = 2 * KP + a * CONTR
        dip_out[a] = out[d0 : d0 + CONTR]


def swap_pairs(count, first):
    pairs = []
    for i in range(first, count - 1, 2):
        pairs += [(i, i + 1), (i + 1, i)]
    return pairs


def call(kernel, outs, name, scratch, args, any_in=(), any_out=(), hbm_in=(), alias=None):
    vmem = pl.BlockSpec(memory_space=pltpu.VMEM)
    hbm = pl.BlockSpec(memory_space=pltpu.HBM)
    return pl.pallas_call(
        kernel,
        out_shape=[jax.ShapeDtypeStruct(s, d) for s, d in outs],
        in_specs=[pl.BlockSpec(memory_space=pl.ANY) if i in any_in else hbm if i in hbm_in else vmem for i in range(len(args))],
        out_specs=[pl.BlockSpec(memory_space=pl.ANY) if i in any_out else vmem for i in range(len(outs))],
        scratch_shapes=list(scratch),
        input_output_aliases=alias or {},
        compiler_params=pltpu.CompilerParams(vmem_limit_bytes=VMEM_LIMIT),
        name=name,
    )(*args)


def body(positions, charges, polar, molecule):
    nb, _, w = positions.shape
    nbp = -(-nb // 16) * 16
    nt = w // L
    nbead = lax.axis_size("bead")
    nspace = lax.axis_size("space")
    rows = 3 * nbp + 8
    own_size = nt * (nt + 1) // 2
    near_size = 2 * nt * nt
    part = functools.partial

    def exchange(x):
        near = lax.ppermute(x, "space", swap_pairs(nspace, 0))
        far = lax.ppermute(x, "space", swap_pairs(nspace, 1))
        return near, far

    raw = (jnp.transpose(positions, (1, 0, 2)), charges, polar, molecule)
    pack, sel = call(
        part(pack_kernel, nb, nbp, w), [((rows, w), F32), ((12 * nbp, max(nb * SLOT, L)), BF16)], "pack",
        [
            pltpu.VMEM((rows, w), F32),
            pltpu.VMEM((3, nb, w), F32),
            pltpu.VMEM((w,), F32),
            pltpu.VMEM((w,), F32),
            pltpu.VMEM((w,), jnp.int32),
            pltpu.SemaphoreType.DMA((4,)),
        ],
        tuple(pltpu.with_memory_space_constraint(v, pltpu.HBM) for v in raw), hbm_in=(0, 1, 2, 3),
    )
    packa, packb = exchange(pack)

    def pair_scratch(nsrc):
        return [
            pltpu.VMEM((nsrc * w, 8), F32),
            pltpu.VMEM((8, w), F32),
            pltpu.VMEM((4, L, L), F32),
            pltpu.VMEM((4, L, L), F32),
        ]

    def perm_scratch(nsrc, blocks):
        return [
            pltpu.VMEM((-(-nb // 4), nsrc * w, DEEP), BF16),
            pltpu.VMEM((nb * SLOT, nsrc * w), BF16),
            *pair_scratch(nsrc),
            pltpu.VMEM((max(own_size, 2), L, L), F32),
            pltpu.VMEM((4, 2 * L, L), BF16),
            pltpu.VMEM((4, 2 * L, L), BF16),
            pltpu.SMEM((2 + 2 * blocks,), jnp.int32),
        ]

    acc, ft, order, pack = call(
        part(perm_own_kernel, nb, nbp, w),
        [((nt, nb * 24, L), F32), ((nb, DEEP, w), BF16), ((w, w), BF16), ((rows, w), F32)], "perm_own",
        perm_scratch(1, own_size), (pack, sel),
    )
    perm, msg, _ = call(
        part(perm_near_kernel, nb, nbp, w), [((3 * nbp, w), F32), ((6 * CONTR, w), F32), ((nt, nb * 24, L), F32)],
        "perm_near", perm_scratch(2, near_size), (pack, packa, packb, sel, ft, acc, order), alias={5: 2},
    )

    if nbead == 2:
        other = lax.ppermute(msg, "bead", [(0, 1), (1, 0)])
    else:
        other = lax.psum(msg, "bead") - msg
    m0, cf = call(
        part(start_kernel, nbp, w), [((6 * CONTR, w), F32), ((2 * KP, w), F32)], "start", [], (msg, other, order, pack),
    )
    m0a, m0b = exchange(m0)

    def tensor_scratch(nsrc):
        return [
            pltpu.VMEM((1, nsrc * w, DEEP), BF16),
            pltpu.VMEM((CONTR, DEEP, w), BF16),
            *pair_scratch(nsrc),
        ]

    accs = [((CONTR * 48, w), F32), ((CONTR * 24, w), F32)]
    near_scratch = [pltpu.VMEM((2 * nt, 48 * KP, L), F32), pltpu.VMEM((2 * KP, w), F32)]
    list_scratch = [pltpu.SMEM((2 + 2 * near_size,), jnp.int32), pltpu.SemaphoreType.DMA]
    own_scratch = [pltpu.VMEM((nt, 48 * KP, L), F32)]
    t_own, acc_a, acc_b = call(
        part(own_first_kernel, nbp, w), [((CONTR, own_size, 4 * L, L), BF16)] + accs, "own_0",
        own_scratch + tensor_scratch(1),
        (m0, pack),
    )
    mu, t_nbr, lst, _, _ = call(
        part(near_first_kernel, nbp, w),
        [((2 * KP, w), F32), ((CONTR, near_size, 4 * L, L), BF16), ((2 + 2 * near_size,), jnp.int32)] + accs, "near_0",
        tensor_scratch(2) + near_scratch + list_scratch,
        (m0, m0a, m0b, pack, packa, packb, cf, acc_a, acc_b), any_out=(2,), alias={7: 3, 8: 4},
    )
    for step in range(1, ITERS):
        mua, mub = exchange(mu)
        acc_a, acc_b = call(part(own_kernel, w), accs, f"own_{step}", own_scratch, (mu, m0, t_own))
        mu, _, _ = call(
            part(near_kernel, nbp, w), [((2 * KP, w), F32)] + accs, f"near_{step}", near_scratch + list_scratch,
            (mua, mub, m0, m0a, m0b, pack, cf, acc_a, acc_b, t_nbr, lst), any_in=(10,), alias={7: 1, 8: 2},
        )
    mua, mub = exchange(mu)
    acc_a, acc_b, perm = call(
        part(last_own_kernel, w), accs + [((3 * nbp, w), F32)], "own_last", own_scratch,
        (mu, m0, t_own, perm, order),
    )
    total, dipoles, _, _ = call(
        part(final_kernel, nb, nbp, w), [((3, nb, w), F32), ((3, CONTR, w), F32)] + accs, "final",
        near_scratch + list_scratch,
        (mua, mub, m0, m0a, m0b, mu, perm, order, acc_a, acc_b, t_nbr, lst), any_in=(11,), alias={8: 2, 9: 3},
    )
    return (jnp.transpose(total, (1, 0, 2)), jnp.transpose(dipoles, (1, 0, 2)))


def solution(mesh):
    in_specs = (P("bead", None, "space"), P("space"), P("space"), P("space"))
    out_specs = (P("bead", None, "space"), P(None, None, "space"))
    return jax.shard_map(body, mesh=mesh, in_specs=in_specs, out_specs=out_specs, check_vma=False)
```

```python
import functools
import math

import jax
import jax.numpy as jnp
from jax import lax
from jax.experimental import pallas as pl
from jax.experimental.pallas import tpu as pltpu
from jax.sharding import PartitionSpec as P

BEADS = 32
CONTR = 4
ITERS = 2
CUTOFF = 9.0
CUT2 = CUTOFF * CUTOFF
THOLE = 0.39
LOG2E = 1.4426950408889634
LN2 = 0.6931471805599453
L = 128
KP = 8
F32 = jnp.float32
BF16 = jnp.bfloat16
VMEM_LIMIT = 20 * 1024 * 1024


def split3(x):
    h = x.astype(BF16).astype(F32)
    r = x - h
    m = r.astype(BF16).astype(F32)
    return h, m, r - m


def dot(a, b, ca=1, cb=0):
    return lax.dot_general(a, b, (((ca,), (cb,)), ((), ())), preferred_element_type=F32)


def dot3(x, mat, cb):
    rows = x.shape[0]
    out = dot(jnp.concatenate(split3(x), 0).astype(BF16), mat, 1, cb)
    return (out[:rows] + out[rows : 2 * rows]) + out[2 * rows :]


T_SLOTS, S_SLOTS = [], []
for _a in range(3):
    T_SLOTS += [(_a, 1)] * 3 + [(3 + _a, 1)] * 2 + [(6 + _a, 1)]
    S_SLOTS += [(_a, -2), (3 + _a, -2), (6 + _a, -2), (_a, -2), (3 + _a, -2), (_a, -2)]
T_SLOTS += [(9, 1), (10, 1), (11, 1), (12, 1), (12, 1), (12, 1)]
S_SLOTS += [(12, 1), (12, 1), (12, 1), (9, 1), (10, 1), (11, 1)]
SLOT = 32
DEEP = 4 * len(T_SLOTS)
TYPES = 13


def perm_matrix(rank_row, w):
    rows = lax.broadcasted_iota(jnp.int32, (w, w), 0).astype(F32)
    return jnp.where(rows == rank_row, 1.0, 0.0).astype(BF16)


def pair_pieces(xs):
    hx, hy, hz = (split3(x) for x in xs)
    n = xs[0] * xs[0] + xs[1] * xs[1] + xs[2] * xs[2]
    parts = [hx[0], hy[0], hz[0], hx[1], hy[1], hz[1], hx[2], hy[2], hz[2]]
    return parts + list(split3(n)) + [jnp.ones_like(n)]


def slot_stack(pieces, slots, g):
    lo = g // 2 * 8
    top = lax.broadcasted_iota(jnp.int32, (8, pieces[0].shape[1]), 0) < 4
    here, there = {}, {}
    for kind, coef in slots:
        if (kind, coef) not in here:
            x = pieces[kind][lo : lo + 8]
            here[kind, coef] = x if coef == 1 else x * float(coef)
            there[kind, coef] = here[kind, coef] if kind == TYPES - 1 else pltpu.roll(here[kind, coef], 4, 0)
    first, second = (here, there) if g % 2 == 0 else (there, here)
    return jnp.concatenate(
        [jnp.where(top, first[slots[f]], second[slots[f + 1]]) for f in range(0, len(slots), 2)], 0
    )


def target_features(pieces, ft, count):
    for g in range(-(-count // 4)):
        stack = slot_stack(pieces, T_SLOTS, g)
        stack = stack.astype(BF16)
        row = lax.broadcasted_iota(jnp.int32, stack.shape, 0) % 4
        for i in range(min(4, count - g * 4)):
            ft[g * 4 + i] = stack * jnp.where(row == i, 1.0, 0.0).astype(BF16)


def source_features(pieces, fs, s, w, count):
    for g in range(-(-count // 4)):
        fs[g, s * w : (s + 1) * w, :] = jnp.transpose(slot_stack(pieces, S_SLOTS, g).astype(BF16))


def sum_select(rows, count):
    lane = lax.broadcasted_iota(jnp.int32, (1, max(count * SLOT, L)), 1)
    b, r = lane // SLOT, lane % SLOT
    p, f = r // 8, r % 8
    want = jnp.where((f < 4) & (p < 3) & (b < count), (p * 4 + f) * rows + b, -1)
    row = lax.broadcasted_iota(jnp.int32, (12 * rows, lane.shape[1]), 0)
    return jnp.where(row == want, 1.0, 0.0).astype(BF16)


def center_of(xs, count):
    w = xs[0].shape[1]
    return [jnp.sum(x[:count], keepdims=True) * (1.0 / (count * w)) for x in xs]


def columns(misc):
    al = misc[1:2]
    good = al > 0.0
    inv = jnp.where(good, lax.rsqrt(jnp.where(good, al, 1.0)), 0.0)
    return jnp.concatenate([inv, misc[2:3], jnp.zeros_like(misc[:6])], 0)


def ranges(x, al, count, w):
    good = al > 0.0
    lo = jnp.where(good, x[:count], 1e30)
    hi = jnp.where(good, x[:count], -1e30)
    out = []
    for i in range(w // L):
        out.append((jnp.min(lo[:, i * L : (i + 1) * L]), jnp.max(hi[:, i * L : (i + 1) * L])))
    return out


def near_list(lst, size, trange, sranges):
    lst[1] = 0
    lst[1 + size] = 0
    count = jnp.int32(0)
    sj = 0
    for slab in sranges:
        for smin, smax in slab:
            for ti, (tmin, tmax) in enumerate(trange):
                near = (smin - tmax < CUTOFF) & (tmin - smax < CUTOFF)
                lst[1 + count] = sj * L
                lst[1 + size + count] = ti * L
                count = count + near.astype(jnp.int32)
            sj += 1
    lst[0] = count


def own_blocks(nt):
    return [(i, i) for i in range(nt)], [(i, j) for i in range(nt) for j in range(i + 1, nt)]


def pair_basis(r2, q):
    safe = jnp.maximum(r2, 1e-4)
    inv = lax.rsqrt(safe)
    c = (safe * inv) * (safe * q)
    decay = jnp.exp2(c)
    v = jnp.maximum(CUT2 - r2, 0.0) * inv
    return c, decay, inv, v


def comps(ref, first, count=3):
    out = []
    for c in range(first, first + count):
        block = ref[c // 2 * 8 : c // 2 * 8 + 8]
        out.append(block if c % 2 == 0 else pltpu.roll(block, 4, 0))
    return out


def stack_comps(parts):
    top = lax.broadcasted_iota(jnp.int32, parts[0].shape, 0) < 4
    return jnp.concatenate(
        [jnp.where(top, parts[i], pltpu.roll(parts[i + 1], 4, 0)) for i in range(0, len(parts), 2)], 0
    )


def two(x):
    hi = x.astype(BF16)
    return hi, (x - hi.astype(F32)).astype(BF16)


def weights(nb, shape, rank, bead_dim):
    b = lax.broadcasted_iota(jnp.int32, shape, bead_dim)
    k = lax.broadcasted_iota(jnp.int32, shape, 1 - bead_dim)
    turn = k * (BEADS // CONTR) - (rank * nb + b) + 2 * BEADS
    turn = (turn + BEADS // 2) % BEADS - BEADS // 2
    cos = jnp.cos(turn.astype(F32) * (2.0 * math.pi / BEADS))
    return jnp.where((k < CONTR) & (b < nb), 2.0 * cos * (1.0 + cos), 0.0)


def hdot(a, b):
    return jnp.dot(a, b, precision=lax.Precision.HIGHEST, preferred_element_type=F32)


def pack_kernel(nb, nbp, w, pos, charge, polar, mol, out, sel, scr, posv, chargev, polarv, molv, sem):
    copies = [
        pltpu.make_async_copy(src, dst, sem.at[i])
        for i, (src, dst) in enumerate(((pos, posv), (charge, chargev), (polar, polarv), (mol, molv)))
    ]
    for c in copies:
        c.start()
    sel[...] = sum_select(nbp, nb)
    scr[...] = jnp.zeros_like(scr)
    for c in copies:
        c.wait()
    for a in range(3):
        scr[a * nbp : a * nbp + nb, :] = posv[a]
    base = 3 * nbp
    scr[base : base + 1, :] = chargev[...].reshape(1, w)
    scr[base + 1 : base + 2, :] = polarv[...].reshape(1, w)
    scr[base + 2 : base + 3, :] = molv[...].reshape(1, w).astype(F32)
    x = scr[...]
    key = jnp.sum(x[:nbp], 0, keepdims=True)
    col = jnp.transpose(jnp.broadcast_to(key, (8, w)))[:, :1]
    jj = lax.broadcasted_iota(jnp.int32, (w, w), 0)
    ii = lax.broadcasted_iota(jnp.int32, (w, w), 1)
    before = (col < key) | ((col == key) & (jj < ii))
    rank = jnp.sum(jnp.where(before, 1.0, 0.0), 0, keepdims=True)
    out[...] = dot3(x, perm_matrix(rank, w), 1)
    out[base + 3 : base + 4, :] = rank


def perm_sources(nb, nbp, w, src, pieces, xs, s, sel_r, fs, rt, cols):
    base = 3 * nbp
    misc = src[base : base + 8, :]
    source_features(pieces, fs, s, w, nb)
    q = jnp.broadcast_to(misc[0:1] * (1.0 / (CUT2 * CUT2)), xs[0].shape)
    feats = [split3(v) for v in (xs[0] * q, xs[1] * q, xs[2] * q, q)]
    stack = jnp.concatenate([feats[f][p] for p in range(3) for f in range(4)], 0)
    rt[:, s * w : (s + 1) * w] = dot(sel_r, stack.astype(BF16), 0, 0).astype(BF16)
    cols[s * w : (s + 1) * w, :] = jnp.transpose(columns(misc))
    return misc[1:2]


class Item:
    def __init__(self, e, s0, t0, g=0, sym=False):
        self.e, self.s0, self.t0, self.g, self.sym = e, s0, t0, g, sym

    def at(self, g):
        return Item(self.e, self.s0, self.t0, g, self.sym)


def perm_run(items, head, tail, nb, fs, ft, rt, qbuf, acc, r2s, fbs):
    def gather(tile, b, out):
        for p in range(3):
            row = (p * nb + b) * 8
            acc[tile, row : row + 8, :] += out[p * 8 : p * 8 + 8]

    def sums(it, f):
        for j in range(4):
            r0 = (it.g * 4 + j) * SLOT
            r = rt[r0 : r0 + SLOT, pl.ds(it.s0, L)]
            pair = f[j]
            gather(it.t0 // L, it.g * 4 + j, dot(jnp.concatenate([r, r], 1), pair))
            if it.sym:
                back = dot(rt[r0 : r0 + SLOT, pl.ds(it.t0, L)], pair, 1, 1)
                gather(it.s0 // L, it.g * 4 + j, back[:, :L] + back[:, L:])

    def functions(it, r2, f):
        for j in range(4):
            c, decay, inv, v = pair_basis(r2[j], qbuf[it.e])
            hi, lo = two((v * v) * (inv * (1.0 - decay)))
            f[j, :L, :] = hi
            f[j, L:, :] = lo

    def distances(it, r2):
        lhs = fs[it.g, pl.ds(it.s0, L), :]
        for j in range(4):
            r2[j] = dot(lhs, ft[it.g * 4 + j, :, pl.ds(it.t0, L)])

    if not items:
        if tail is not None:
            distances(tail, r2s[0])
        if head is not None:
            sums(head, fbs[1])
        return
    for i, it in enumerate(items):
        functions(it, r2s[i % 2], fbs[i % 2])
        after = items[i + 1] if i + 1 < len(items) else tail
        if after is not None:
            distances(after, r2s[(i + 1) % 2])
        before = items[i - 1] if i > 0 else head
        if before is not None:
            sums(before, fbs[(i - 1) % 2])


def perm_own_pairs(blocks, nb, *rest):
    items = [
        Item(e, s * L, t * L, g, s != t) for e, (s, t) in enumerate(blocks) for g in range(nb // 4)
    ]
    args = rest
    perm_run([], None, items[0], nb, *args)
    odd = len(items) % 2
    perm_run(items[: len(items) - odd], None, items[-1] if odd else None, nb, *args)
    if odd:
        perm_run([items[-1]], items[-2] if len(items) > 1 else None, None, nb, *args)
        fbs = args[-1]
        fbs[1][...] = fbs[0][...]
    perm_run([], items[-1], None, nb, *args)


def perm_near_pairs(n, lst, size, nb, cols, qrow, *rest):
    qbuf, fbs = rest[3], rest[-1]
    fbs[1][...] = jnp.zeros_like(fbs[1])
    groups = nb // 4

    def entry(i):
        good = i < n
        e = jnp.where(good, i, 0)
        return jnp.where(good, 1.0, 0.0), lst[1 + e], lst[1 + size + e]

    def item(e, it):
        return Item(e, pl.multiple_of(it[1], L), pl.multiple_of(it[2], L))

    def step(i, carry):
        before, first, second, after = carry
        later = (entry(2 * i + 3), entry(2 * i + 4))
        items = []
        for e, it in enumerate((first, second)):
            block = item(e, it)
            qbuf[e] = near_q(block.s0, block.t0, cols, qrow) * it[0]
            items += [block.at(g) for g in range(groups)]
        perm_run(items, item(1, before).at(groups - 1), item(0, after).at(0), nb, *rest)
        return (second, after) + later

    start = entry(0)
    perm_run([], None, item(0, start).at(0), nb, *rest)
    last = lax.fori_loop(0, (n + 1) // 2, step, (start, start, entry(1), entry(2)))[0]
    perm_run([], item(1, last).at(groups - 1), None, nb, *rest)


def own_q(s, t, cols, qrow):
    cc = cols[s * L : (s + 1) * L, :]
    row = qrow[:, t * L : (t + 1) * L]
    return jnp.where(cc[:, 1:2] == row[1:2], 0.0, cc[:, 0:1] * row[0:1])


def near_q(s0, t0, cols, qrow):
    return cols[pl.ds(s0, L), :][:, 0:1] * qrow[0:1, pl.ds(t0, L)]


def q_rows(misc, qrow):
    c = columns(misc)
    qrow[...] = c
    qrow[0:1, :] = c[0:1] * (-THOLE * LOG2E)


def perm_own_kernel(nb, nbp, w, tgt, sel, acc, ft, order, keep, fs, rt, cols, qrow, r2a, r2b, qbuf, fa, fb, lst):
    nt = w // L
    base = 3 * nbp
    sel_r = sel[...]
    acc[...] = jnp.zeros_like(acc)
    order[...] = perm_matrix(tgt[base + 3 : base + 4, :], w)
    keep[...] = tgt[...]
    coords = [tgt[a * nbp : (a + 1) * nbp, :] for a in range(3)]
    xt = [x - c for x, c in zip(coords, center_of(coords, nb))]
    pieces = pair_pieces(xt)
    target_features(pieces, ft, nb)
    perm_sources(nb, nbp, w, tgt, pieces, xt, 0, sel_r, fs, rt, cols)
    q_rows(tgt[base : base + 8, :], qrow)
    diag, off = own_blocks(nt)
    for e, (a, b) in enumerate(diag + off):
        qbuf[e] = own_q(a, b, cols, qrow)
    perm_own_pairs(diag + off, nb, fs, ft, rt, qbuf, acc, (r2a, r2b), (fa, fb))


def perm_near_kernel(
    nb, nbp, w, tgt, srca, srcb, sel, ft, acc_in, order, perm_out, msg_out, acc,
    fs, rt, cols, qrow, r2a, r2b, qbuf, fa, fb, lst,
):
    nt = w // L
    base = 3 * nbp
    coords = [tgt[a * nbp : (a + 1) * nbp, :] for a in range(3)]
    center = center_of(coords, nb)
    xt = [x - c for x, c in zip(coords, center)]
    sel_r = sel[...]
    sranges = []
    for s, src in enumerate((srca, srcb)):
        xs = [src[a * nbp : (a + 1) * nbp, :] - center[a] for a in range(3)]
        al = perm_sources(nb, nbp, w, src, pair_pieces(xs), xs, s, sel_r, fs, rt, cols)
        sranges.append(ranges(xs[0], al, nb, w))
    size = 2 * nt * nt
    near_list(lst, size, ranges(xt[0], tgt[base + 1 : base + 2, :], nb, w), sranges)
    q_rows(tgt[base : base + 8, :], qrow)
    n = lst[0]
    perm_near_pairs(n, lst, size, nb, cols, qrow, fs, ft, rt, qbuf, acc, (r2a, r2b), (fa, fb))
    if nb < nbp:
        perm_out[...] = jnp.zeros_like(perm_out)
    for i in range(nt):
        tile = slice(i * L, (i + 1) * L)
        sums = []
        for f in range(4):
            h, m, l = (acc[i, pl.ds(p * nb * 8 + f, nb, stride=8), :] for p in range(3))
            sums.append((h + m) + l)
        for a in range(3):
            perm_out[a * nbp : a * nbp + nb, tile] = xt[a][:nb, tile] * sums[3] - sums[a]
    wc = weights(nb, (KP, nbp), lax.axis_index("bead"), 1) * (1.0 / BEADS)
    parts = [hdot(wc, perm_out[a * nbp : (a + 1) * nbp, :]) for a in range(3)]
    parts += [hdot(wc, coords[a]) for a in range(3)]
    msg_out[...] = dot3(stack_comps(parts), order[...], 0)


def start_kernel(nbp, w, msg, other, order, pack, m0, cf):
    both = dot3(msg[...] + other[...], order[...], 1)
    cf[...] = both[: 2 * KP]
    row = lax.broadcasted_iota(jnp.int32, both.shape, 0)
    m0[...] = jnp.where(row < 3 * CONTR, both * pack[3 * nbp + 1 : 3 * nbp + 2, :], both)


def centered(m, center):
    return [x - c for x, c in zip(comps(m, 3), center)]


def own_center(m):
    return center_of(comps(m, 3), CONTR)


def tensor_of(e, r2, q, tensors):
    for k in range(CONTR):
        c, decay, inv, v = pair_basis(r2[k], q)
        l3 = 1.0 - decay
        l5 = l3 + (c * LN2) * decay
        w3 = (v * v) * inv
        w5 = w3 * (inv * inv)
        a_hi, a_lo = two(w5 * l5)
        b_hi, b_lo = two(w3 * l3)
        tensors[k, e, 0:L, :] = a_hi
        tensors[k, e, L : 2 * L, :] = a_lo
        tensors[k, e, 2 * L : 3 * L, :] = b_hi
        tensors[k, e, 3 * L : 4 * L, :] = b_lo


def tensor_distances(s0, t0, fs, ft, r2):
    lhs = fs[0, pl.ds(s0, L), :]
    for k in range(CONTR):
        r2[k] = dot(lhs, ft[k, :, pl.ds(t0, L)])


def own_tensors(blocks, fs, ft, cols, qrow, r2s, tensors):
    tensor_distances(blocks[0][0] * L, blocks[0][1] * L, fs, ft, r2s[0])
    for e, (s, t) in enumerate(blocks):
        if e + 1 < len(blocks):
            tensor_distances(blocks[e + 1][0] * L, blocks[e + 1][1] * L, fs, ft, r2s[(e + 1) % 2])
        tensor_of(e, r2s[e % 2], own_q(s, t, cols, qrow), tensors)


def near_tensors(n, lst, size, fs, ft, cols, qrow, r2a, r2b, r2c, tensors):
    def where_is(i):
        e = jnp.maximum(jnp.minimum(i, n - 1), 0)
        return e, pl.multiple_of(lst[1 + e], L), pl.multiple_of(lst[1 + size + e], L)

    def tensor(i, r2):
        e, s0, t0 = where_is(i)
        tensor_of(e, r2, near_q(s0, t0, cols, qrow), tensors)

    def distances(i, r2):
        _, s0, t0 = where_is(i)
        tensor_distances(s0, t0, fs, ft, r2)

    def step(p, carry):
        distances(3 * p + 1, r2b)
        tensor(3 * p, r2a)
        distances(3 * p + 2, r2c)
        tensor(3 * p + 1, r2b)
        distances(3 * p + 3, r2a)
        tensor(3 * p + 2, r2c)
        return carry

    def single(i, carry):
        e = n // 3 * 3 + i
        tensor(e, r2a)
        distances(e + 1, r2a)
        return carry

    distances(0, r2a)
    lax.fori_loop(0, n // 3, step, 0)
    lax.fori_loop(0, n % 3, single, 0)


def induce_features(mu, x, le, s, w):
    scale = 1.0 / (CUT2 * CUT2)
    m = [v * scale for v in comps(mu, 0)]
    dotted = x[0] * m[0] + x[1] * m[1] + x[2] * m[2]
    feats = m + [dotted] + [x[a] * m[b] for a in range(3) for b in range(3)]
    feats += [x[a] * dotted for a in range(3)]
    nt = w // L
    for f, v in enumerate(feats):
        for p, piece in enumerate(split3(v)):
            row = (p * 16 + f) * KP
            for i in range(nt):
                le[s * nt + i, row : row + KP, :] = piece[:, i * L : (i + 1) * L]


def features_of(le, tile, k):
    first = le[tile, pl.ds(k, 48, stride=KP), :]
    second = [le[tile, pl.ds(p * 16 * KP + k, 8, stride=KP), :] for p in range(3)]
    return first.astype(BF16), jnp.concatenate(second, 0).astype(BF16)


def twice(x):
    return jnp.concatenate([x, x], 1)


def own_sums(w, mu, m0, tensors, acc_a, acc_b, le):
    nt = w // L
    induce_features(mu, centered(m0, own_center(m0)), le, 0, w)
    acc_a[...] = jnp.zeros_like(acc_a)
    acc_b[...] = jnp.zeros_like(acc_b)
    diag, off = own_blocks(nt)
    for e, (s, t) in enumerate(diag + off):
        s0, t0 = s * L, t * L
        for k in range(CONTR):
            pa, pb = tensors[k, e, 0 : 2 * L, :], tensors[k, e, 2 * L : 4 * L, :]
            a0, b0 = k * 48, k * 24
            fa, fb = features_of(le, s, k)
            acc_a[a0 : a0 + 48, t0 : t0 + L] += dot(twice(fa), pa)
            acc_b[b0 : b0 + 24, t0 : t0 + L] += dot(twice(fb), pb)
            if s != t:
                fa, fb = features_of(le, t, k)
                back = dot(fa, pa, 1, 1)
                acc_a[a0 : a0 + 48, s0 : s0 + L] += back[:, :L] + back[:, L:]
                back = dot(fb, pb, 1, 1)
                acc_b[b0 : b0 + 24, s0 : s0 + L] += back[:, :L] + back[:, L:]


def near_sums(w, mus, cps, m0, tensors, lst, acc_a, acc_b, le, ev, bring=None):
    nt = w // L
    center = own_center(m0)
    for s, (mu, cp) in enumerate(zip(mus, cps)):
        induce_features(mu, centered(cp, center), le, s, w)
    size = 2 * nt * nt
    if bring is not None:
        bring.wait()

    def add(e):
        tile = lst[1 + e] // L
        t0 = pl.multiple_of(lst[1 + size + e], L)
        for k in range(CONTR):
            a0, b0 = k * 48, k * 24
            fa, fb = features_of(le, tile, k)
            acc_a[a0 : a0 + 48, pl.ds(t0, L)] += dot(twice(fa), tensors[k, e, 0 : 2 * L, :])
            acc_b[b0 : b0 + 24, pl.ds(t0, L)] += dot(twice(fb), tensors[k, e, 2 * L : 4 * L, :])

    def three(i, carry):
        for j in range(3):
            add(3 * i + j)
        return carry

    def single(i, carry):
        add(lst[0] // 3 * 3 + i)
        return carry

    lax.fori_loop(0, lst[0] // 3, three, 0)
    lax.fori_loop(0, lst[0] % 3, single, 0)
    ev[...] = jnp.zeros_like(ev)
    xt = centered(m0, center)
    for k in range(CONTR):
        o = k * 48
        sa = acc_a[o : o + 16, :] + acc_a[o + 16 : o + 32, :] + acc_a[o + 32 : o + 48, :]
        o = k * 24
        sb = acc_b[o : o + 8, :] + acc_b[o + 8 : o + 16, :] + acc_b[o + 16 : o + 24, :]
        x = [v[k : k + 1] for v in xt]
        along = x[0] * sa[0:1] + x[1] * sa[1:2] + x[2] * sa[2:3] - sa[3:4]
        for a in range(3):
            cross = sum(x[b] * sa[4 + 3 * a + b : 5 + 3 * a + b] for b in range(3))
            full = x[a] * along - cross + sa[13 + a : 14 + a]
            ev[a * CONTR + k : a * CONTR + k + 1, :] = 3.0 * full - sb[a : a + 1]


def own_first_kernel(nbp, w, m0, pack, tensors, acc_a, acc_b, le, fs, ft, cols, qrow, r2a, r2b):
    misc = pack[3 * nbp : 3 * nbp + 8, :]
    pieces = pair_pieces(centered(m0, own_center(m0)))
    target_features(pieces, ft, CONTR)
    source_features(pieces, fs, 0, w, CONTR)
    cols[...] = jnp.transpose(columns(misc))
    q_rows(misc, qrow)
    diag, off = own_blocks(w // L)
    own_tensors(diag + off, fs, ft, cols, qrow, (r2a, r2b), tensors)
    own_sums(w, m0, m0, tensors, acc_a, acc_b, le)


def own_kernel(w, mu, m0, tensors, acc_a, acc_b, le):
    own_sums(w, mu, m0, tensors, acc_a, acc_b, le)


def update(pack, nbp, cf, ev):
    return pack[3 * nbp + 1 : 3 * nbp + 2, :] * (cf[...] + ev[...])


def near_first_kernel(
    nbp, w, m0, m0a, m0b, pack, packa, packb, cf, acc_a_in, acc_b_in,
    mu_out, tensors, lst_out, acc_a, acc_b, fs, ft, cols, qrow, r2a, r2b, r2c, le, ev, lst, sem,
):
    nt = w // L
    base = 3 * nbp
    center = own_center(m0)
    xt = centered(m0, center)
    target_features(pair_pieces(xt), ft, CONTR)
    sranges = []
    for s, (m, pk) in enumerate(((m0a, packa), (m0b, packb))):
        misc = pk[base : base + 8, :]
        xs = centered(m, center)
        source_features(pair_pieces(xs), fs, s, w, CONTR)
        cols[s * w : (s + 1) * w, :] = jnp.transpose(columns(misc))
        sranges.append(ranges(xs[0], misc[1:2], CONTR, w))
    misc = pack[base : base + 8, :]
    size = 2 * nt * nt
    near_list(lst, size, ranges(xt[0], misc[1:2], CONTR, w), sranges)
    leave = pltpu.make_async_copy(lst, lst_out, sem)
    q_rows(misc, qrow)
    n = lst[0]
    leave.start()
    near_tensors(n, lst, size, fs, ft, cols, qrow, r2a, r2b, r2c, tensors)
    near_sums(w, [m0a, m0b], [m0a, m0b], m0, tensors, lst, acc_a, acc_b, le, ev)
    mu_out[...] = update(pack, nbp, cf, ev)
    leave.wait()


def near_kernel(
    nbp, w, mua, mub, m0, m0a, m0b, pack, cf, acc_a_in, acc_b_in, tensors, lst_hbm, mu_out, acc_a, acc_b, le, ev, lst, sem,
):
    bring = pltpu.make_async_copy(lst_hbm, lst, sem)
    bring.start()
    near_sums(w, [mua, mub], [m0a, m0b], m0, tensors, lst, acc_a, acc_b, le, ev, bring)
    mu_out[...] = update(pack, nbp, cf, ev)


def last_own_kernel(w, mu, m0, tensors, perm, order, acc_a, acc_b, perm_out, le):
    own_sums(w, mu, m0, tensors, acc_a, acc_b, le)
    perm_out[...] = dot3(perm[...], order[...], 0)


def final_kernel(
    nb, nbp, w, mua, mub, m0, m0a, m0b, mu, perm, order, acc_a_in, acc_b_in, tensors, lst_hbm,
    total_out, dip_out, acc_a, acc_b, le, ev, lst, sem,
):
    bring = pltpu.make_async_copy(lst_hbm, lst, sem)
    bring.start()
    near_sums(w, [mua, mub], [m0a, m0b], m0, tensors, lst, acc_a, acc_b, le, ev, bring)
    out = dot3(jnp.concatenate([ev[...], mu[...]], 0), order[...], 0)
    us = weights(nb, (nbp, KP), lax.axis_index("bead"), 0) * (1.0 / CONTR)
    for a, v in enumerate(comps(out, 0)):
        total_out[a] = (perm[a * nbp : (a + 1) * nbp, :] + hdot(us, v))[:nb]
        d0 = 2 * KP + a * CONTR
        dip_out[a] = out[d0 : d0 + CONTR]


def swap_pairs(count, first):
    pairs = []
    for i in range(first, count - 1, 2):
        pairs += [(i, i + 1), (i + 1, i)]
    return pairs


def call(kernel, outs, name, scratch, args, any_in=(), any_out=(), hbm_in=(), alias=None):
    vmem = pl.BlockSpec(memory_space=pltpu.VMEM)
    hbm = pl.BlockSpec(memory_space=pltpu.HBM)
    return pl.pallas_call(
        kernel,
        out_shape=[jax.ShapeDtypeStruct(s, d) for s, d in outs],
        in_specs=[pl.BlockSpec(memory_space=pl.ANY) if i in any_in else hbm if i in hbm_in else vmem for i in range(len(args))],
        out_specs=[pl.BlockSpec(memory_space=pl.ANY) if i in any_out else vmem for i in range(len(outs))],
        scratch_shapes=list(scratch),
        input_output_aliases=alias or {},
        compiler_params=pltpu.CompilerParams(vmem_limit_bytes=VMEM_LIMIT),
        name=name,
    )(*args)


def body(positions, charges, polar, molecule):
    nb, _, w = positions.shape
    nbp = -(-nb // 16) * 16
    nt = w // L
    nbead = lax.axis_size("bead")
    nspace = lax.axis_size("space")
    rows = 3 * nbp + 8
    own_size = nt * (nt + 1) // 2
    near_size = 2 * nt * nt
    part = functools.partial

    def exchange(x):
        near = lax.ppermute(x, "space", swap_pairs(nspace, 0))
        far = lax.ppermute(x, "space", swap_pairs(nspace, 1))
        return near, far

    raw = (jnp.transpose(positions, (1, 0, 2)), charges, polar, molecule)
    pack, sel = call(
        part(pack_kernel, nb, nbp, w), [((rows, w), F32), ((12 * nbp, max(nb * SLOT, L)), BF16)], "pack",
        [
            pltpu.VMEM((rows, w), F32),
            pltpu.VMEM((3, nb, w), F32),
            pltpu.VMEM((w,), F32),
            pltpu.VMEM((w,), F32),
            pltpu.VMEM((w,), jnp.int32),
            pltpu.SemaphoreType.DMA((4,)),
        ],
        tuple(pltpu.with_memory_space_constraint(v, pltpu.HBM) for v in raw), hbm_in=(0, 1, 2, 3),
    )
    packa, packb = exchange(pack)

    def pair_scratch(nsrc):
        return [
            pltpu.VMEM((nsrc * w, 8), F32),
            pltpu.VMEM((8, w), F32),
            pltpu.VMEM((4, L, L), F32),
            pltpu.VMEM((4, L, L), F32),
        ]

    def perm_scratch(nsrc, blocks):
        return [
            pltpu.VMEM((-(-nb // 4), nsrc * w, DEEP), BF16),
            pltpu.VMEM((nb * SLOT, nsrc * w), BF16),
            *pair_scratch(nsrc),
            pltpu.VMEM((max(own_size, 2), L, L), F32),
            pltpu.VMEM((4, 2 * L, L), BF16),
            pltpu.VMEM((4, 2 * L, L), BF16),
            pltpu.SMEM((2 + 2 * blocks,), jnp.int32),
        ]

    acc, ft, order, pack = call(
        part(perm_own_kernel, nb, nbp, w),
        [((nt, nb * 24, L), F32), ((nb, DEEP, w), BF16), ((w, w), BF16), ((rows, w), F32)], "perm_own",
        perm_scratch(1, own_size), (pack, sel),
    )
    perm, msg, _ = call(
        part(perm_near_kernel, nb, nbp, w), [((3 * nbp, w), F32), ((6 * CONTR, w), F32), ((nt, nb * 24, L), F32)],
        "perm_near", perm_scratch(2, near_size), (pack, packa, packb, sel, ft, acc, order), alias={5: 2},
    )

    if nbead == 2:
        other = lax.ppermute(msg, "bead", [(0, 1), (1, 0)])
    else:
        other = lax.psum(msg, "bead") - msg
    m0, cf = call(
        part(start_kernel, nbp, w), [((6 * CONTR, w), F32), ((2 * KP, w), F32)], "start", [], (msg, other, order, pack),
    )
    m0a, m0b = exchange(m0)

    def tensor_scratch(nsrc):
        return [
            pltpu.VMEM((1, nsrc * w, DEEP), BF16),
            pltpu.VMEM((CONTR, DEEP, w), BF16),
            *pair_scratch(nsrc),
        ]

    accs = [((CONTR * 48, w), F32), ((CONTR * 24, w), F32)]
    near_scratch = [pltpu.VMEM((2 * nt, 48 * KP, L), F32), pltpu.VMEM((2 * KP, w), F32)]
    list_scratch = [pltpu.SMEM((2 + 2 * near_size,), jnp.int32), pltpu.SemaphoreType.DMA]
    own_scratch = [pltpu.VMEM((nt, 48 * KP, L), F32)]
    t_own, acc_a, acc_b = call(
        part(own_first_kernel, nbp, w), [((CONTR, own_size, 4 * L, L), BF16)] + accs, "own_0",
        own_scratch + tensor_scratch(1),
        (m0, pack),
    )
    mu, t_nbr, lst, _, _ = call(
        part(near_first_kernel, nbp, w),
        [((2 * KP, w), F32), ((CONTR, near_size, 4 * L, L), BF16), ((2 + 2 * near_size,), jnp.int32)] + accs, "near_0",
        tensor_scratch(2) + [pltpu.VMEM((4, L, L), F32)] + near_scratch + list_scratch,
        (m0, m0a, m0b, pack, packa, packb, cf, acc_a, acc_b), any_out=(2,), alias={7: 3, 8: 4},
    )
    for step in range(1, ITERS):
        mua, mub = exchange(mu)
        acc_a, acc_b = call(part(own_kernel, w), accs, f"own_{step}", own_scratch, (mu, m0, t_own))
        mu, _, _ = call(
            part(near_kernel, nbp, w), [((2 * KP, w), F32)] + accs, f"near_{step}", near_scratch + list_scratch,
            (mua, mub, m0, m0a, m0b, pack, cf, acc_a, acc_b, t_nbr, lst), any_in=(10,), alias={7: 1, 8: 2},
        )
    mua, mub = exchange(mu)
    acc_a, acc_b, perm = call(
        part(last_own_kernel, w), accs + [((3 * nbp, w), F32)], "own_last", own_scratch,
        (mu, m0, t_own, perm, order),
    )
    total, dipoles, _, _ = call(
        part(final_kernel, nb, nbp, w), [((3, nb, w), F32), ((3, CONTR, w), F32)] + accs, "final",
        near_scratch + list_scratch,
        (mua, mub, m0, m0a, m0b, mu, perm, order, acc_a, acc_b, t_nbr, lst), any_in=(11,), alias={8: 2, 9: 3},
    )
    return (jnp.transpose(total, (1, 0, 2)), jnp.transpose(dipoles, (1, 0, 2)))


def solution(mesh):
    in_specs = (P("bead", None, "space"), P("space"), P("space"), P("space"))
    out_specs = (P("bead", None, "space"), P(None, None, "space"))
    return jax.shard_map(body, mesh=mesh, in_specs=in_specs, out_specs=out_specs, check_vma=False)
```
